32 devices in a mesh: dp: 8 (over y, x, core), ctx: 4 (over z).
Axes of the slice: x: 2, y: 2, z: 4, core: 2. Of those that a mesh axis runs over, the one named last changes fastest.
Arguments:
- hidden: bfloat16 [24, 832, 1024], P('dp', 'ctx'), may hold values from -6 to 6
- text_states: bfloat16 [24, 64, 1024], P('dp'), may hold values from -6 to 6
- frame_segments: int32 [24, 832], P('dp'), may hold values from 0 to 3, never falling along the last dimension, each value on 1 to 416 neighbouring positions
- text_segments: int32 [24, 64], P('dp'), may hold values from 0 to 3, as said below
- text_lengths: int32 [24], P('dp'), may hold values from 8 to 64, as said below
- cotangent: bfloat16 [24, 832, 1024], P('dp', 'ctx'), may hold values from -6 to 6
- self_query: bfloat16 [1024, 1024], P('dp', 'ctx'), may hold values from -0.1875 to 0.1875
- self_key: bfloat16 [1024, 1024], P('dp', 'ctx'), may hold values from -0.1875 to 0.1875
- self_value: bfloat16 [1024, 1024], P('dp', 'ctx'), may hold values from -0.1875 to 0.1875
- self_out: bfloat16 [1024, 1024], P('dp', 'ctx'), may hold values from -1 to 1
- cross_query: bfloat16 [1024, 1024], P('dp', 'ctx'), may hold values from -0.1875 to 0.1875
- cross_key: bfloat16 [1024, 1024], P('dp', 'ctx'), may hold values from -0.1875 to 0.1875
- cross_value: bfloat16 [1024, 1024], P('dp', 'ctx'), may hold values from -0.1875 to 0.1875
- cross_out: bfloat16 [1024, 1024], P('dp', 'ctx'), may hold values from -0.5 to 0.5
- feed_in: bfloat16 [1024, 4096], P('dp', 'ctx'), may hold values from -0.1875 to 0.1875
- feed_out: bfloat16 [4096, 1024], P('dp', 'ctx'), may hold values from -0.09375 to 0.09375
- first_gain: bfloat16 [1024], P(('dp', 'ctx')), may hold values from 0.25 to 1.75
- first_shift: bfloat16 [1024], P(('dp', 'ctx')), may hold values from -1.5 to 1.5
- second_gain: bfloat16 [1024], P(('dp', 'ctx')), may hold values from 0.25 to 1.75
- second_shift: bfloat16 [1024], P(('dp', 'ctx')), may hold values from -1.5 to 1.5
- third_gain: bfloat16 [1024], P(('dp', 'ctx')), may hold values from 0.25 to 1.75
- third_shift: bfloat16 [1024], P(('dp', 'ctx')), may hold values from -1.5 to 1.5
Outputs:
- block_output: bfloat16 [24, 832, 1024], P('dp', 'ctx')
- hidden_grad: float32 [24, 832, 1024], P('dp', 'ctx')
- text_grad: float32 [24, 64, 1024], P('dp', 'ctx')
- self_query_grad: float32 [1024, 1024], P('dp', 'ctx')
- self_key_grad: float32 [1024, 1024], P('dp', 'ctx')
- self_value_grad: float32 [1024, 1024], P('dp', 'ctx')
- self_out_grad: float32 [1024, 1024], P('dp', 'ctx')
- cross_query_grad: float32 [1024, 1024], P('dp', 'ctx')
- cross_key_grad: float32 [1024, 1024], P('dp', 'ctx')
- cross_value_grad: float32 [1024, 1024], P('dp', 'ctx')
- cross_out_grad: float32 [1024, 1024], P('dp', 'ctx')
- feed_in_grad: float32 [1024, 4096], P('dp', 'ctx')
- feed_out_grad: float32 [4096, 1024], P('dp', 'ctx')
- first_gain_grad: float32 [1024], P(('dp', 'ctx'))
- first_shift_grad: float32 [1024], P(('dp', 'ctx'))
- second_gain_grad: float32 [1024], P(('dp', 'ctx'))
- second_shift_grad: float32 [1024], P(('dp', 'ctx'))
- third_gain_grad: float32 [1024], P(('dp', 'ctx'))
- third_shift_grad: float32 [1024], P(('dp', 'ctx'))
The draws below stay inside these ranges and needn't reach their ends.
Inputs may be any that keep to these rules, and one draw needn't show every extreme that they name: `frame_segments`: each row's ids never fall and name every one of the 4 clips. `text_segments`: among the first text_lengths tokens of a row the ids never fall and every one of the 4 clips has two or more tokens; later tokens carry any clip id. `text_lengths`: some row of every draw has all 64 tokens valid.
All inputs are finite; a program needn't handle non-finite values.
Results may differ from the reference program's by a relative error of at most 0.015.
Values may be sent and summed in bfloat16 or wider, within the bound.
A program may use at most 256 MiB of HBM per device.

```python
import math
import jax
import jax.numpy as jnp
import numpy as np
from jax import lax

D = 1024
FF = 4096
HEADS = 16
HEAD = 64
TEXT = 64
CLIPS = 4
FRAMES = 832
BATCH = 24


def text_layout(key):
    base = jax.random.fold_in(key, 11)
    first_key, second_key, third_key, fourth_key = jax.random.split(base, 4)
    lengths = jax.random.randint(first_key, (BATCH,), 2 * CLIPS, TEXT + 1)
    top_row = jax.random.randint(fourth_key, (), 0, BATCH)
    lengths = jnp.where(jnp.arange(BATCH) == top_row, TEXT, lengths).astype(jnp.int32)
    stride = lengths // CLIPS
    half_range = jnp.maximum(stride // 2 - 1, 0)
    offsets = jax.random.randint(second_key, (BATCH, CLIPS - 1), -half_range[:, None], half_range[:, None] + 1)
    cuts = jnp.arange(1, CLIPS)[None, :] * stride[:, None] + offsets
    places = jnp.arange(TEXT)
    ordered = jnp.sum((places[None, :, None] >= cuts[:, None, :]).astype(jnp.int32), axis=-1)
    filler = jax.random.randint(third_key, (BATCH, TEXT), 0, CLIPS)
    text_ids = jnp.where(places[None, :] < lengths[:, None], ordered, filler).astype(jnp.int32)
    return (text_ids, lengths)


def draw_text_segments(key, part):
    return text_layout(key)[0]


def draw_text_lengths(key, part):
    return text_layout(key)[1]


def levels(own_key, shape, pieces, smallest, high):
    level = 1.0
    for axis_at, shards_of in pieces:
        draws = jax.random.uniform(jax.random.fold_in(jax.random.fold_in(own_key, 6), axis_at), (shards_of,), jnp.float32, smallest / len(pieces), high / len(pieces))
        level = level * jnp.repeat(jnp.exp(draws), shape[axis_at] // shards_of).reshape((-1,) + (1,) * (len(shape) - 1 - axis_at))
    return level


def profile(count, total, bound, slope):
    weights = [(1 << 20) // math.isqrt(standing ** slope) + 1 for standing in range(2, count + 1)]
    rest, counts = total - bound - (count - 1), [1] * (count - 1)
    while rest > 0:
        free = [i for i in range(count - 1) if counts[i] < bound]
        mass, budget = sum([weights[i] for i in free]), rest
        for i in free:
            extra = min(bound - counts[i], max(1, budget * weights[i] // mass), rest)
            counts[i] = counts[i] + extra
            rest = rest - extra
    return np.array([bound] + counts)


def ragged(own_key, number_of, total, bound, lean):
    if number_of == 2:
        one = jax.random.randint(own_key, (), max(1, total - bound), min(bound, total - 1) + 1)
        return jnp.stack([one, total - one])
    tallies = jnp.asarray(profile(number_of, total, bound, lean), jnp.int32)
    pairs = (number_of - 1) // 2
    source_of, taker = tallies[1:1 + 2 * pairs:2], tallies[2:2 + 2 * pairs:2]
    room = jnp.minimum(source_of - 1, bound - taker)
    moved = jax.random.randint(jax.random.fold_in(own_key, 1), (pairs,), 0, 1 << 20) % (room + 1)
    tallies = tallies.at[1:1 + 2 * pairs:2].set(source_of - moved).at[2:2 + 2 * pairs:2].set(taker + moved)
    return tallies[jax.random.permutation(jax.random.fold_in(own_key, 2), number_of)]


def normal_values(own_key, shape, scale, reach, cuts=(), dtype=jnp.bfloat16):
    gain = levels(own_key, shape, cuts, -0.22, 0.18) if cuts else 1.0
    values = jax.random.normal(own_key, shape, jnp.float32) * scale * gain
    return jnp.minimum(jnp.maximum(values, -reach), reach).astype(dtype)


def setup_inputs(seed: int = 0) -> dict:
    key_list = jax.random.split(jax.random.key(seed), 23)
    return {
        "hidden": normal_values(key_list[0], (BATCH, FRAMES, D), 1.0, 6.0, ((0, 8), (1, 4))),
        "text_states": normal_values(key_list[1], (BATCH, TEXT, D), 1.0, 6.0, ((0, 8),)),
        "frame_segments": jax.vmap(lambda own: jnp.searchsorted(jnp.cumsum(ragged(own, CLIPS, FRAMES, FRAMES // 2, 2)), jnp.arange(FRAMES), side="right"))(jax.random.split(key_list[2], BATCH)).reshape((BATCH, FRAMES)).astype(jnp.int32),
        "text_segments": draw_text_segments(jax.random.fold_in(key_list[22], 71), 0),
        "text_lengths": draw_text_lengths(jax.random.fold_in(key_list[22], 71), 0),
        "cotangent": normal_values(key_list[5], (BATCH, FRAMES, D), 1.0, 6.0, ((0, 8), (1, 4))),
        "self_query": normal_values(key_list[6], (D, D), D ** -0.5, 0.1875, ((0, 8), (1, 4))),
        "self_key": normal_values(key_list[7], (D, D), D ** -0.5, 0.1875, ((0, 8), (1, 4))),
        "self_value": normal_values(key_list[8], (D, D), D ** -0.5, 0.1875, ((0, 8), (1, 4))),
        "self_out": normal_values(key_list[9], (D, D), 32 ** -0.5, 1.0, ((0, 8), (1, 4))),
        "cross_query": normal_values(key_list[10], (D, D), D ** -0.5, 0.1875, ((0, 8), (1, 4))),
        "cross_key": normal_values(key_list[11], (D, D), D ** -0.5, 0.1875, ((0, 8), (1, 4))),
        "cross_value": normal_values(key_list[12], (D, D), D ** -0.5, 0.1875, ((0, 8), (1, 4))),
        "cross_out": normal_values(key_list[13], (D, D), 128 ** -0.5, 0.5, ((0, 8), (1, 4))),
        "feed_in": normal_values(key_list[14], (D, FF), D ** -0.5, 0.1875, ((0, 8), (1, 4))),
        "feed_out": normal_values(key_list[15], (FF, D), FF ** -0.5, 0.09375, ((0, 8), (1, 4))),
        "first_gain": jnp.clip(1.0 + 0.15 * jax.random.normal(key_list[16], (D,), jnp.float32), 0.25, 1.75).astype(jnp.bfloat16),
        "first_shift": normal_values(key_list[17], (D,), 0.3, 1.5, ((0, 32),)),
        "second_gain": jnp.clip(1.0 + 0.15 * jax.random.normal(key_list[18], (D,), jnp.float32), 0.25, 1.75).astype(jnp.bfloat16),
        "second_shift": normal_values(key_list[19], (D,), 0.3, 1.5, ((0, 32),)),
        "third_gain": jnp.clip(1.0 + 0.15 * jax.random.normal(key_list[20], (D,), jnp.float32), 0.25, 1.75).astype(jnp.bfloat16),
        "third_shift": normal_values(key_list[21], (D,), 0.3, 1.5, ((0, 32),)),
    }


@jax.custom_vjp
def low(v):
    return lax.optimization_barrier(v.astype(jnp.bfloat16)).astype(jnp.float32)

@jax.custom_vjp
def low_back(v):
    return v

def low_keep(v):
    return (low(v), None)

def low_pass(kept, grad):
    return (grad,)

def back_keep(v):
    return (v, None)

def back_low(kept, grad):
    return (low(grad),)
low.defvjp(low_keep, low_pass)
low_back.defvjp(back_keep, back_low)
EPSILON = 1e-05
HIGHEST = lax.Precision.HIGHEST

def rounded_both(values):
    return low_back(low(values))

def layer_norm(values, norm_gain, norm_shift):
    row_mean = lax.optimization_barrier(jnp.mean(values, axis=-1, keepdims=True))
    centred = values - row_mean
    spread = lax.optimization_barrier(jnp.mean(centred * centred, axis=-1, keepdims=True))
    return centred * lax.rsqrt(spread + EPSILON) * norm_gain + norm_shift

def gelu_exact(values):
    return 0.5 * values * (1.0 + lax.erf(values * 0.7071067811865476))

def matmul(left_side, right_side):
    return jnp.einsum('rfk,kn->rfn', left_side, right_side, precision=HIGHEST)

def attend_row(queries, key_rows, value_rows, allowed):
    query_split = queries.reshape(queries.shape[0], HEADS, HEAD)
    key_split = key_rows.reshape(key_rows.shape[0], HEADS, HEAD)
    value_split = value_rows.reshape(value_rows.shape[0], HEADS, HEAD)
    raw_scores = jnp.einsum('qhe,khe->hqk', query_split, key_split, precision=HIGHEST)
    scores = jnp.where(allowed[None], low_back(raw_scores * 0.125), -1000000000.0)
    shares = low(jnp.exp(scores - jax.nn.logsumexp(scores, axis=-1, keepdims=True)))
    blended = jnp.einsum('hqk,khe->qhe', shares, value_split, precision=HIGHEST)
    return blended.reshape(queries.shape)

def self_row(packed):
    queries, key_rows, value_rows, segments = packed
    places = jnp.arange(segments.shape[0])
    allowed = (segments[:, None] == segments[None, :]) & (places[:, None] >= places[None, :])
    return attend_row(queries, key_rows, value_rows, allowed)

def cross_row(packed):
    queries, key_rows, value_rows, segments, text_ids, length = packed
    places = jnp.arange(text_ids.shape[0])
    allowed = (segments[:, None] == text_ids[None, :]) & (places[None, :] < length)
    return attend_row(queries, key_rows, value_rows, allowed)

def reference(hidden, text_states, frame_segments, text_segments, text_lengths, cotangent, self_query, self_key, self_value, self_out, cross_query, cross_key, cross_value, cross_out, feed_in, feed_out, first_gain, first_shift, second_gain, second_shift, third_gain, third_shift):
    params = tuple((weight.astype(jnp.float32) for weight in (self_query, self_key, self_value, self_out, cross_query, cross_key, cross_value, cross_out, feed_in, feed_out, first_gain, first_shift, second_gain, second_shift, third_gain, third_shift)))

    def forward(states, texts, weights):
        first_norm = low(layer_norm(states, weights[10], weights[11]))
        queries = rounded_both(matmul(first_norm, weights[0]))
        key_rows = rounded_both(matmul(first_norm, weights[1]))
        value_rows = rounded_both(matmul(first_norm, weights[2]))
        self_mixed = rounded_both(lax.map(jax.checkpoint(self_row), (queries, key_rows, value_rows, frame_segments)))
        after_self = states + low_back(matmul(self_mixed, weights[3]))
        second_norm = low(layer_norm(after_self, weights[12], weights[13]))
        cross_queries = rounded_both(matmul(second_norm, weights[4]))
        text_keys = rounded_both(matmul(texts, weights[5]))
        text_values = rounded_both(matmul(texts, weights[6]))
        cross_mixed = rounded_both(lax.map(jax.checkpoint(cross_row), (cross_queries, text_keys, text_values, frame_segments, text_segments, text_lengths)))
        after_cross = after_self + low_back(matmul(cross_mixed, weights[7]))
        third_norm = low(layer_norm(after_cross, weights[14], weights[15]))
        pre_act = low_back(matmul(third_norm, weights[8]))
        activated = low(gelu_exact(pre_act))
        return after_cross + low_back(matmul(activated, weights[9]))
    result, pullback = jax.vjp(forward, hidden.astype(jnp.float32), text_states.astype(jnp.float32), params)
    hidden_grad, text_grad, grads = pullback(cotangent.astype(jnp.float32))
    return (result.astype(jnp.bfloat16), hidden_grad, text_grad, grads[0], grads[1], grads[2], grads[3], grads[4], grads[5], grads[6], grads[7], grads[8], grads[9], grads[10], grads[11], grads[12], grads[13], grads[14], grads[15])
```

```python
import functools

import jax
import jax.numpy as jnp
from jax import lax
from jax.experimental import pallas as pl
from jax.experimental.pallas import tpu as pltpu
from jax.sharding import PartitionSpec as P

BF = jnp.bfloat16
F32 = jnp.float32


MESH = pl.DeviceIdType.MESH
ANY = pl.BlockSpec(memory_space=pl.ANY)

def place():
    dp = lax.axis_index("dp"); z = lax.axis_index("ctx")
    core = lax.rem(dp, 2); x = lax.rem(dp // 2, 2); y = dp // 4
    return dp, z, core, x, y

def pieces_of(shapes):
    out = []
    for w, (rows, cols) in enumerate(shapes):
        n = max(1, (rows * cols) // (128 * 256))
        step = rows // n
        for i in range(n):
            out.append((w, i * step, step, rows, cols))
    return out

def gather_kernel(shapes, zn, lags, *refs):
    nw = len(shapes)
    src, hidden, dst, ext = refs[:nw], refs[nw], refs[nw + 1:2 * nw + 1], refs[2 * nw + 1]
    blank, lsem, zs, zr, xs, xr, fs, fr, cs, cr, hl, hs, hr, bs = refs[2 * nw + 2:]
    nrow = hidden.shape[0]
    dp, z, core, x, y = place()
    xn = dp + 2 - 4 * x
    yn = dp + 4 - 8 * y
    dn = yn + 2 - 4 * x
    cn = dp + 1 - 2 * core
    chunks = pieces_of(shapes)
    n = len(chunks)
    up_ok, dn_ok = z < zn - 1, z > 0

    barrier = pltpu.get_barrier_semaphore()
    for who in (xn, yn, cn):
        pl.semaphore_signal(barrier, inc=1, device_id=(who, z), device_id_type=MESH)
    @pl.when(up_ok)
    def _():
        pl.semaphore_signal(barrier, inc=1, device_id=(dp, z + 1), device_id_type=MESH)
    @pl.when(dn_ok)
    def _():
        pl.semaphore_signal(barrier, inc=1, device_id=(dp, z - 1), device_id_type=MESH)
    pl.semaphore_wait(barrier, 3 + up_ok.astype(jnp.int32) + dn_ok.astype(jnp.int32))

    def own(i):
        w, r0, r, rows, cols = chunks[i]
        return src[w].at[pl.ds(r0, r), :]
    def block(i, who, j):
        w, r0, r, rows, cols = chunks[i]
        return dst[w].at[pl.ds(pl.multiple_of(who * rows + r0, r), r), pl.ds(pl.multiple_of(j * cols, cols), cols)]
    def slab(i, who, half=None):
        w, r0, r, rows, cols = chunks[i]
        if half is None:
            return dst[w].at[pl.ds(pl.multiple_of(who * rows + r0, r), r), :]
        h = r // 2
        return dst[w].at[pl.ds(pl.multiple_of(who * rows + r0 + half * h, h), h), :]

    def remote(a, b, s, r, dev):
        return pltpu.make_async_remote_copy(a, b, s, r, device_id=dev, device_id_type=MESH)
    def zcopy(i, j, up, first=False):
        a = own(i) if first else block(i, dp, j)
        return remote(a, block(i, dp, j), zs.at[i, 0 if up else 1, j], zr.at[i, j], (dp, z + 1 if up else z - 1))
    def xcopy(i):
        return remote(slab(i, dp), slab(i, dp), xs.at[i, 0], xr.at[i, 0], (xn, z))
    def ycopy(i):
        return remote(slab(i, dp), slab(i, dp), xs.at[i, 1], xr.at[i, 1], (yn, z))
    def fcopy(i, half):
        who, to = (xn, yn) if half == 0 else (yn, xn)
        return remote(slab(i, who, half), slab(i, who, half), fs.at[i, half], fr.at[i, half], (to, z))
    def frecv(i, half):
        return remote(slab(i, dn, half), slab(i, dn, half), fs.at[i, half], fr.at[i, half], (yn, z))
    def ccopy(i, k):
        who = (dp, xn, yn, dn)[k]
        return remote(slab(i, who), slab(i, who), cs.at[i, k], cr.at[i, k], (cn, z))
    def crecv(i, k):
        who = (dp, xn, yn, dn)[k] + 1 - 2 * core
        return remote(slab(i, who), slab(i, who), cs.at[i, k], cr.at[i, k], (cn, z))
    def hlocal(r):
        return pltpu.make_async_copy(hidden.at[r], ext.at[r, 2], hl.at[r])
    def hcopy(r, hop):
        return remote(ext.at[r, 1] if hop else hidden.at[r], ext.at[r, 1 - hop], hs.at[hop, r], hr.at[hop, r], (dp, z + 1))
    def hblank(r, c):
        return pltpu.make_async_copy(blank, ext.at[r, c], bs.at[r, c])
    def lcopy(i):
        return pltpu.make_async_copy(own(i), block(i, dp, z), lsem.at[i])
    def xrecv(i):
        return remote(slab(i, xn), slab(i, xn), xs.at[i, 0], xr.at[i, 0], (xn, z))
    def yrecv(i):
        return remote(slab(i, yn), slab(i, yn), xs.at[i, 1], xr.at[i, 1], (yn, z))

    for i in range(n):
        @pl.when(up_ok)
        def _():
            zcopy(i, z, True, True).start()
        @pl.when(dn_ok)
        def _():
            zcopy(i, z, False, True).start()
        lcopy(i).start()
    for r in range(nrow):
        hlocal(r).start()
    blank[...] = jnp.zeros_like(blank)

    def halo_step(k):
        if k % 3 == 1 and k // 3 < nrow:
            @pl.when(up_ok)
            def _():
                hcopy(k // 3, 0).start()
        if k % 3 == 0 and 0 <= k // 3 - 1 < nrow:
            r = k // 3 - 1
            @pl.when(dn_ok)
            def _():
                hcopy(r, 0).wait_recv()
                @pl.when(up_ok)
                def _():
                    hcopy(r, 1).start()
        if k % 3 == 2 and 0 <= k // 3 - 1 < nrow:
            r = k // 3 - 1
            @pl.when(z == 0)
            def _():
                hblank(r, 1).start()
            @pl.when(z <= 1)
            def _():
                hblank(r, 0).start()

    def zstage(i, t):
        @pl.when(z - t >= 0)
        def _():
            zcopy(i, z - t, True).wait_recv()
            @pl.when(up_ok)
            def _():
                zcopy(i, z - t, True).start()
        @pl.when(z + t < zn)
        def _():
            zcopy(i, z + t, False).wait_recv()
            @pl.when(dn_ok)
            def _():
                zcopy(i, z + t, False).start()
    def stage(s, i):
        if s == 0 or s == 1:
            zstage(i, s + 1)
        elif s == 2:
            zstage(i, 3)
            lcopy(i).wait()
            xcopy(i).start(); ycopy(i).start(); ccopy(i, 0).start()
        elif s == 3:
            xrecv(i).wait_recv()
            fcopy(i, 0).start(); ccopy(i, 1).start()
            yrecv(i).wait_recv()
            fcopy(i, 1).start(); ccopy(i, 2).start()
        elif s == 4:
            frecv(i, 0).wait_recv(); frecv(i, 1).wait_recv()
            ccopy(i, 3).start()
        else:
            for k in range(4):
                crecv(i, k).wait_recv()
    for k in range(n + lags[-1]):
        halo_step(k)
        for s, lag in enumerate(lags):
            if 0 <= k - lag < n:
                stage(s, k - lag)
    for r in range(nrow):
        hlocal(r).wait()
        @pl.when(up_ok)
        def _():
            hcopy(r, 0).wait_send()
        @pl.when(up_ok & dn_ok)
        def _():
            hcopy(r, 1).wait_send()
        @pl.when(z >= 2)
        def _():
            hcopy(r, 1).wait_recv()
        @pl.when(z == 0)
        def _():
            hblank(r, 1).wait()
        @pl.when(z <= 1)
        def _():
            hblank(r, 0).wait()
    for i in range(n):
        for j in range(zn):
            @pl.when(up_ok & (j <= z))
            def _():
                zcopy(i, j, True).wait_send()
            @pl.when(dn_ok & (j >= z))
            def _():
                zcopy(i, j, False).wait_send()
        xcopy(i).wait_send(); ycopy(i).wait_send()
        fcopy(i, 0).wait_send(); fcopy(i, 1).wait_send()
        for k in range(4):
            ccopy(i, k).wait_send()

def gather(weights, hidden, dpn, zn, cid=0, lags=(0, 1, 2, 4, 6, 8)):
    shapes = tuple(tuple(w.shape) for w in weights)
    n = len(pieces_of(shapes))
    D = pltpu.SemaphoreType.DMA
    rows, frames, width = hidden.shape
    return pl.pallas_call(
        functools.partial(gather_kernel, shapes, zn, lags),
        out_shape=[jax.ShapeDtypeStruct((dpn * r, zn * c), jnp.bfloat16) for r, c in shapes] + [jax.ShapeDtypeStruct((rows, 3, frames, width), jnp.bfloat16)],
        in_specs=[pl.BlockSpec(memory_space=pltpu.VMEM)] * (len(shapes) + 1),
        out_specs=[ANY] * (len(shapes) + 1),
        scratch_shapes=[pltpu.VMEM((frames, width), jnp.bfloat16), D((n,)), D((n, 2, zn)), D((n, zn)), D((n, 2)), D((n, 2)), D((n, 2)), D((n, 2)), D((n, 4)), D((n, 4)),
                        D((rows,)), D((2, rows)), D((2, rows)), D((rows, 2))],
        compiler_params=pltpu.CompilerParams(collective_id=cid, has_side_effects=True),
        name="gather",
    )(*weights, hidden)

def add_rows(dst, terms, rows, step=16):
    @pl.loop(0, rows // step)
    def _(q):
        s = pl.ds(pl.multiple_of(q * step, step), step)
        total = terms[0][s, :].astype(F32)
        for t in terms[1:]:
            total = total + t[s, :].astype(F32)
        dst[s, :] = total.astype(dst.dtype)

def scatter_kernel(shapes, nhalo, zn, lags, *refs):
    nw = len(shapes)
    it = iter(refs)
    take = lambda k: [next(it) for _ in range(k)]
    grads = take(nw)
    text, halo = take(2)
    outs = take(nw)
    text_out, halo_out = take(2)
    acc, rh, rxy, rz = take(nw), take(nw), take(nw), take(nw)
    kinds = sorted({(s[0] // (1 if s[0]*s[1] <= 128*256 else (s[0]*s[1]) // (128*256)), s[1]) for s in shapes})
    stage = dict(zip(kinds, take(len(kinds))))
    tz, h2, h1, hs = take(4)
    ls, cs, cr, hsd, hrc, xs, xr, zs, zr, tzs, tzr, hls, hss, hrs = take(14)
    dp, z, core, x, y = place()
    xn = dp + 2 - 4 * x
    yn = dp + 4 - 8 * y
    dn = yn + 2 - 4 * x
    flip = 1 - 2 * core
    cn = dp + flip
    chunks = pieces_of(shapes)
    first = {}
    for i, c in enumerate(chunks):
        first.setdefault(c[0], i)
    n = len(chunks)
    up_ok, dn_ok = z < zn - 1, z > 0
    barrier = pltpu.get_barrier_semaphore()
    for who in (xn, yn, cn):
        pl.semaphore_signal(barrier, inc=1, device_id=(who, z), device_id_type=MESH)
    @pl.when(up_ok)
    def _():
        pl.semaphore_signal(barrier, inc=1, device_id=(dp, z + 1), device_id_type=MESH)
    @pl.when(dn_ok)
    def _():
        pl.semaphore_signal(barrier, inc=1, device_id=(dp, z - 1), device_id_type=MESH)
    pl.semaphore_wait(barrier, 3 + up_ok.astype(jnp.int32) + dn_ok.astype(jnp.int32))

    def remote(a, b, s, r, dev):
        return pltpu.make_async_remote_copy(a, b, s, r, device_id=dev, device_id_type=MESH)
    def slab(i, who):
        w, r0, r, rows, cols = chunks[i]
        return grads[w].at[pl.ds(pl.multiple_of(who * rows + r0, r), r), :]
    fam = (dp, xn, yn, dn)
    def at(buf, i, *rest):
        w = chunks[i][0]
        return buf[w].at[(i - first[w],) + rest]
    def ccopy(i, k):
        return remote(slab(i, fam[k] + flip), at(acc, i, k), cs.at[i, k], cr.at[i, k], (cn, z))
    def staged(i):
        w, r0, r, rows, cols = chunks[i]
        return stage[(r, cols)]
    slots = {}
    cnt = {}
    for i, c in enumerate(chunks):
        key = (c[2], c[4]); slots[i] = cnt.get(key, 0) % 2; cnt[key] = cnt.get(key, 0) + 1
    kidx = {k: q for q, k in enumerate(kinds)}
    def lcopy(i, k):
        key = (chunks[i][2], chunks[i][4])
        return pltpu.make_async_copy(slab(i, fam[k]), staged(i).at[slots[i], k], ls.at[kidx[key], slots[i], k])
    prev = {}
    nxt = {}
    last = {}
    for i, c in enumerate(chunks):
        key = (c[2], c[4])
        last.setdefault(key, []).append(i)
    for key, l in last.items():
        for a, b in zip(l, l[2:]):
            nxt[a] = b
    def half(ref, i, h):
        r = chunks[i][2]
        return ref.at[pl.ds(h * (r // 2), r // 2), :]
    def dcopy(i, h):
        return remote(half(at(acc, i, 3), i, h), at(rh, i, h), hsd.at[i, h], hrc.at[i, h], ((xn, yn)[h], z))
    def xcopy(i, d, h):
        return remote(half(at(acc, i, 1 + d), i, h), half(at(rxy, i, d), i, h), xs.at[i, d, h], xr.at[i, d, h], ((xn, yn)[d], z))
    def col(ref, i, j):
        cols = chunks[i][4]
        return ref.at[:, pl.ds(j * cols, cols)]
    def zcopy(i, up, j):
        return remote(col(at(acc, i, 0), i, j), at(rz, i, 0 if up else 1, j), zs.at[i, 0 if up else 1, j], zr.at[i, 0 if up else 1, j], (dp, z + 1 if up else z - 1))
    tc = text.shape[1] // zn
    tr = text.shape[0]
    def tcopy(up, j):
        return remote(text.at[:, pl.ds(j * tc, tc)], tz.at[0 if up else 1, j], tzs.at[0 if up else 1, j], tzr.at[0 if up else 1, j], (dp, z + 1 if up else z - 1))
    def h2copy(r):
        return remote(halo.at[r, 0], h2.at[r], hss.at[0, r], hrs.at[0, r], (dp, z - 1))
    def h1local(r):
        return pltpu.make_async_copy(halo.at[r, 1], h1.at[r], hls.at[r])
    def h1copy(r):
        return remote(h1.at[r], halo_out.at[r], hss.at[1, r], hrs.at[1, r], (dp, z - 1))

    @pl.when(z >= 2)
    def _():
        for r in range(nhalo):
            h2copy(r).start()
    @pl.when(dn_ok)
    def _():
        for r in range(nhalo):
            h1local(r).start()
    for i in range(n):
        for k in (3, 1, 2, 0):
            ccopy(i, k).start()
    for key, l in last.items():
        for i in l[:2]:
            for k in (3, 1, 2, 0):
                lcopy(i, k).start()

    def zadd(i, j, z_static, up):
        w, r0, r, rows, cols = chunks[i]
        a = col(at(acc, i, 0), i, j)
        add_rows(a, [a, at(rz, i, 0 if up else 1, j)], r)
    def zstage(i, t):
        w, r0, r, rows, cols = chunks[i]
        for up in (True, False):
            @pl.when(z == (t if up else zn - 1 - t))
            def _(up=up):
                zz = t if up else zn - 1 - t
                js = range(zz + 1, zn) if up else range(zz - 1, -1, -1)
                for j in js:
                    if t > 0:
                        zcopy(i, up, j).wait_recv()
                        zadd(i, j, zz, up)
                    zcopy(i, up, j).start()
                if t > 0:
                    zcopy(i, up, zz).wait_recv()
    def final(i):
        w, r0, r, rows, cols = chunks[i]
        o = outs[w].at[pl.ds(r0, r), :]
        for zz in range(zn):
            @pl.when(z == zz)
            def _(zz=zz):
                terms = [col(at(acc, i, 0), i, zz)]
                if zz > 0: terms.append(at(rz, i, 0, zz))
                if zz < zn - 1: terms.append(at(rz, i, 1, zz))
                add_rows(o, terms, r)
    def text_stage(t):
        for up in (True, False):
            @pl.when(z == (t if up else zn - 1 - t))
            def _(up=up):
                zz = t if up else zn - 1 - t
                js = range(zz + 1, zn) if up else range(zz - 1, -1, -1)
                for j in js:
                    if t > 0:
                        tcopy(up, j).wait_recv()
                        a = text.at[:, pl.ds(j * tc, tc)]
                        add_rows(a, [a, tz.at[0 if up else 1, j]], tr)
                    tcopy(up, j).start()
                if t > 0:
                    tcopy(up, zz).wait_recv()
    def text_final():
        for zz in range(zn):
            @pl.when(z == zz)
            def _(zz=zz):
                terms = [text.at[:, pl.ds(zz * tc, tc)]]
                if zz > 0: terms.append(tz.at[0, zz])
                if zz < zn - 1: terms.append(tz.at[1, zz])
                add_rows(text_out, terms, tr)
    def halo_stage(r):
        @pl.when(dn_ok)
        def _():
            h1local(r).wait()
            @pl.when(up_ok)
            def _():
                h2copy(r).wait_recv()
                add_rows(h1.at[r], [h1.at[r], h2.at[r]], h1.shape[1])
            h1copy(r).start()
        @pl.when(z == zn - 1)
        def _():
            pltpu.make_async_copy(hs, halo_out.at[r], hls.at[r]).start()

    def stage_of(s, i):
        w, r0, r, rows, cols = chunks[i]
        if s == 0:
            A = lambda k: at(acc, i, k)
            S = lambda k: staged(i).at[slots[i], k]
            for k in (3, 1, 2, 0):
                ccopy(i, k).wait_recv()
                lcopy(i, k).wait()
                add_rows(A(k), [A(k), S(k)], r)
                if k == 1:
                    dcopy(i, 0).start(); dcopy(i, 1).start()
                if k == 2:
                    xcopy(i, 0, 0).start()
                if k == 0:
                    xcopy(i, 1, 1).start()
            if i in nxt:
                for k in (3, 1, 2, 0):
                    lcopy(nxt[i], k).start()
        elif s == 1:
            dcopy(i, 0).wait_recv()
            a = half(at(acc, i, 2), i, 0)
            add_rows(a, [a, at(rh, i, 0)], r // 2, min(16, r // 2))
            dcopy(i, 1).wait_recv()
            b = half(at(acc, i, 1), i, 1)
            add_rows(b, [b, at(rh, i, 1)], r // 2, min(16, r // 2))
            xcopy(i, 1, 0).start()
            xcopy(i, 0, 1).start()
        elif s == 2:
            for d in range(2):
                for h in range(2):
                    xcopy(i, d, h).wait_recv()
            a = at(acc, i, 0)
            add_rows(a, [a, at(rxy, i, 0), at(rxy, i, 1)], r)
            zstage(i, 0)
        elif s < 2 + zn:
            zstage(i, s - 2)
            if s == 1 + zn:
                final(i)
    for k in range(n + lags[-1]):
        for s, lag in enumerate(lags):
            if 0 <= k - lag < n:
                stage_of(s, k - lag)
        if k == 0:
            hs[...] = jnp.zeros_like(hs)
        if 1 <= k <= zn:
            text_stage(k - 1)
        if k == zn + 1:
            text_final()
        if 2 <= k < 2 + nhalo:
            halo_stage(k - 2)
    for i in range(n):
        for k in range(4):
            ccopy(i, k).wait_send()
        for h in range(2):
            dcopy(i, h).wait_send()
            for d in range(2):
                xcopy(i, d, h).wait_send()
        for j in range(zn):
            @pl.when(up_ok & (j > z))
            def _():
                zcopy(i, True, j).wait_send()
            @pl.when(dn_ok & (j < z))
            def _():
                zcopy(i, False, j).wait_send()
    for j in range(zn):
        @pl.when(up_ok & (j > z))
        def _():
            tcopy(True, j).wait_send()
        @pl.when(dn_ok & (j < z))
        def _():
            tcopy(False, j).wait_send()
    for r in range(nhalo):
        @pl.when(z >= 2)
        def _():
            h2copy(r).wait_send()
        @pl.when(dn_ok)
        def _():
            h1copy(r).wait_send()
        @pl.when(up_ok)
        def _():
            h1copy(r).wait_recv()
        @pl.when(z == zn - 1)
        def _():
            pltpu.make_async_copy(hs, halo_out.at[r], hls.at[r]).wait()

def scatter(grads, text, halo, dpn, zn, cid=1, lags=(0, 1, 2, 3, 4, 5)):
    shapes = tuple((g.shape[0] // dpn, g.shape[1] // zn) for g in grads)
    chunks = pieces_of(shapes)
    n = len(chunks)
    cnt = [sum(c[0] == w for c in chunks) for w in range(len(shapes))]
    rr = [next(c[2] for c in chunks if c[0] == w) for w in range(len(shapes))]
    kinds = sorted({(r, s[1]) for r, s in zip(rr, shapes)})
    D = pltpu.SemaphoreType.DMA
    V = pltpu.VMEM
    T = halo.shape
    tr, tc = text.shape[0], text.shape[1] // zn
    scratch = [V((cnt[w], 4, rr[w], zn * shapes[w][1]), BF) for w in range(len(shapes))]
    scratch += [V((cnt[w], 2, rr[w] // 2, zn * shapes[w][1]), BF) for w in range(len(shapes))]
    scratch += [V((cnt[w], 2, rr[w], zn * shapes[w][1]), BF) for w in range(len(shapes))]
    scratch += [V((cnt[w], 2, zn, rr[w], shapes[w][1]), BF) for w in range(len(shapes))]
    scratch += [V((2, 4, r, zn * c), BF) for r, c in kinds]
    scratch += [V((2, zn, tr, tc), BF), V((T[0],) + T[2:], BF), V((T[0],) + T[2:], BF), V(T[2:], BF)]
    scratch += [D((len(kinds), 2, 4)), D((n, 4)), D((n, 4)), D((n, 2)), D((n, 2)), D((n, 2, 2)), D((n, 2, 2)), D((n, 2, zn)), D((n, 2, zn)),
                D((2, zn)), D((2, zn)), D((T[0],)), D((2, T[0])), D((2, T[0]))]
    VM = pl.BlockSpec(memory_space=pltpu.VMEM)
    return pl.pallas_call(
        functools.partial(scatter_kernel, shapes, T[0], zn, lags),
        out_shape=[jax.ShapeDtypeStruct(s, F32) for s in shapes] + [jax.ShapeDtypeStruct((tr, tc), F32), jax.ShapeDtypeStruct((T[0],) + T[2:], BF)],
        in_specs=[ANY] * len(shapes) + [VM, ANY],
        out_specs=[VM] * (len(shapes) + 1) + [ANY],
        scratch_shapes=scratch,
        compiler_params=pltpu.CompilerParams(collective_id=cid, has_side_effects=True, vmem_limit_bytes=60 << 20),
        name="scatter",
    )(*grads, text, halo)

HEAD = 64
SCALE = 0.125
MASKED = -1e9

def dot(a, b, ca, cb):
    return lax.dot_general(a, b, (((ca,), (cb,)), ((), ())), preferred_element_type=F32)

def lane_is(shape, h):
    lanes = lax.broadcasted_iota(jnp.int32, shape, 1)
    return (lanes < HEAD) if h == 0 else (lanes >= HEAD)

def self_allowed(q_ids, k_ids, back):
    nq, nk = q_ids.shape[0], k_ids.shape[1]
    qi = lax.broadcasted_iota(jnp.int32, (nq, nk), 0)
    ki = lax.broadcasted_iota(jnp.int32, (nq, nk), 1)
    return (q_ids == k_ids) & (ki <= qi + back)

def self_forward_kernel(qs, ks, q, k, v, o, lse, bias):
    nq, nk = q.shape[1], k.shape[1]
    @pl.when(pl.program_id(1) == 0)
    def _():
        bias[...] = jnp.where(self_allowed(qs[0], ks[0], nk - nq), 0.0, MASKED)
    q2, k2, v2 = q[0], k[0], v[0]
    outs, totals = [], []
    for h in range(2):
        mine = lane_is(q2.shape, h)
        qh = jnp.where(mine, q2 * jnp.asarray(SCALE, BF), jnp.zeros_like(q2))
        s = dot(qh, k2, 1, 1) + bias[...]
        top = jnp.max(s, axis=1, keepdims=True)
        p = jnp.exp(s - top)
        total = jnp.sum(p, axis=1, keepdims=True)
        outs.append(dot(p.astype(BF), v2, 1, 0) / total)
        totals.append(jnp.broadcast_to(top + jnp.log(total), q2.shape))
    first = lane_is(q2.shape, 0)
    o[0] = jnp.where(first, outs[0], outs[1]).astype(BF)
    lse[0] = jnp.where(first, totals[0], totals[1])

def self_backward_kernel(qs, ks, q, k, v, lse, do, dq, dk, dv, bias):
    nq, nk = q.shape[1], k.shape[1]
    @pl.when(pl.program_id(1) == 0)
    def _():
        bias[...] = jnp.where(self_allowed(qs[0], ks[0], nk - nq), 0.0, MASKED)
    q2, k2, v2, d2 = q[0], k[0], v[0], do[0]
    gq, gk, gv = [], [], []
    for h in range(2):
        mine = lane_is(q2.shape, h)
        zero = jnp.zeros_like(q2)
        qh = jnp.where(mine, q2 * jnp.asarray(SCALE, BF), zero)
        dh = jnp.where(mine, d2, zero)
        s = dot(qh, k2, 1, 1) + bias[...]
        p = jnp.exp(s - lse[0][:, h * HEAD:h * HEAD + 1])
        dp = dot(dh, v2, 1, 1)
        inner = jnp.sum(p * dp, axis=1, keepdims=True)
        ds = (p * (dp - inner)).astype(BF)
        gq.append(dot(ds, k2, 1, 0) * SCALE)
        gk.append(dot(ds, qh, 0, 0))
        gv.append(dot(p.astype(BF), dh, 0, 0))
    dq[0] = jnp.where(lane_is(q2.shape, 0), gq[0], gq[1]).astype(BF)
    dk[0] = (gk[0] + gk[1]).astype(BF)
    dv[0] = (gv[0] + gv[1]).astype(BF)

def specs(nq, nk):
    qb = pl.BlockSpec((1, nq, 128), lambda r, p: (r, 0, p))
    kb = pl.BlockSpec((1, nk, 128), lambda r, p: (r, 0, p))
    qid = pl.BlockSpec((1, nq, 1), lambda r, p: (r, 0, 0))
    kid = pl.BlockSpec((1, 1, nk), lambda r, p: (r, 0, 0))
    return qb, kb, qid, kid

def self_forward(q, k, v, q_ids, k_ids):
    rows, nq, width = q.shape
    nk = k.shape[1]
    qb, kb, qid, kid = specs(nq, nk)
    return pl.pallas_call(
        self_forward_kernel, grid=(rows, width // 128),
        in_specs=[qid, kid, qb, kb, kb], out_specs=[qb, qb],
        out_shape=[jax.ShapeDtypeStruct(q.shape, BF), jax.ShapeDtypeStruct(q.shape, F32)],
        scratch_shapes=[pltpu.VMEM((nq, nk), F32)], name="self_attention",
    )(q_ids[:, :, None], k_ids[:, None, :], q, k, v)

def self_backward(q, k, v, lse, do, q_ids, k_ids):
    rows, nq, width = q.shape
    nk = k.shape[1]
    qb, kb, qid, kid = specs(nq, nk)
    return pl.pallas_call(
        self_backward_kernel, grid=(rows, width // 128),
        in_specs=[qid, kid, qb, kb, kb, qb, qb], out_specs=[qb, kb, kb],
        out_shape=[jax.ShapeDtypeStruct(q.shape, BF), jax.ShapeDtypeStruct(k.shape, BF), jax.ShapeDtypeStruct(k.shape, BF)],
        scratch_shapes=[pltpu.VMEM((nq, nk), F32)], name="self_attention_back",
    )(q_ids[:, :, None], k_ids[:, None, :], q, k, v, lse, do)

def pair_keys(k2):
    first = lane_is(k2.shape, 0)
    zero = jnp.zeros_like(k2)
    return jnp.concatenate([jnp.where(first, k2, zero), jnp.where(first, zero, k2)], axis=0)

def halves(values, tokens, reduce, fill):
    left = lax.broadcasted_iota(jnp.int32, values.shape, 1) < tokens
    a = reduce(jnp.where(left, values, fill), axis=1, keepdims=True)
    b = reduce(jnp.where(left, fill, values), axis=1, keepdims=True)
    return jnp.where(left, a, b)

def cross_shares(q2, kk, ids_q, ids_k, tokens):
    s = dot(q2 * jnp.asarray(SCALE, BF), kk, 1, 1)
    s = jnp.where(ids_q == ids_k, s, MASKED)
    p = jnp.exp(s - halves(s, tokens, jnp.max, MASKED))
    return p / halves(p, tokens, jnp.sum, 0.0)

def cross_forward_kernel(qs, ks, q, k, v, o):
    tokens = k.shape[1]
    p = cross_shares(q[0], pair_keys(k[0]), qs[0], ks[0], tokens)
    o[0] = dot(p.astype(BF), pair_keys(v[0]), 1, 0).astype(BF)

def cross_backward_kernel(qs, ks, q, k, v, do, dq, dk, dv):
    tokens = k.shape[1]
    q2, d2 = q[0], do[0]
    kk, vv = pair_keys(k[0]), pair_keys(v[0])
    p = cross_shares(q2, kk, qs[0], ks[0], tokens)
    dp = dot(d2, vv, 1, 1)
    ds = (p * (dp - halves(p * dp, tokens, jnp.sum, 0.0))).astype(BF)
    dq[0] = (dot(ds, kk, 1, 0) * SCALE).astype(BF)
    gk = dot(ds, q2, 0, 0) * SCALE
    gv = dot(p.astype(BF), d2, 0, 0)
    first = lane_is((tokens, 128), 0)
    dk[0] = jnp.where(first, gk[:tokens], gk[tokens:]).astype(BF)
    dv[0] = jnp.where(first, gv[:tokens], gv[tokens:]).astype(BF)

def cross_specs(nq, nk):
    qb, kb, qid, _ = specs(nq, nk)
    return qb, kb, qid, pl.BlockSpec((1, 1, 2 * nk), lambda r, p: (r, 0, 0))

def cross_forward(q, k, v, q_ids, k_ids):
    rows, nq, width = q.shape
    qb, kb, qid, kid = cross_specs(nq, k.shape[1])
    return pl.pallas_call(
        cross_forward_kernel, grid=(rows, width // 128),
        in_specs=[qid, kid, qb, kb, kb], out_specs=qb,
        out_shape=jax.ShapeDtypeStruct(q.shape, BF), name="cross_attention",
    )(q_ids[:, :, None], jnp.concatenate([k_ids, k_ids], axis=1)[:, None, :], q, k, v)

def cross_backward(q, k, v, do, q_ids, k_ids):
    rows, nq, width = q.shape
    qb, kb, qid, kid = cross_specs(nq, k.shape[1])
    return pl.pallas_call(
        cross_backward_kernel, grid=(rows, width // 128),
        in_specs=[qid, kid, qb, kb, kb, qb], out_specs=[qb, kb, kb],
        out_shape=[jax.ShapeDtypeStruct(q.shape, BF), jax.ShapeDtypeStruct(k.shape, BF), jax.ShapeDtypeStruct(k.shape, BF)],
        name="cross_attention_back",
    )(q_ids[:, :, None], jnp.concatenate([k_ids, k_ids], axis=1)[:, None, :], q, k, v, do)

EPS = 1e-05
W = 1024
SLAB = 128
VEC = 16

class Names:
    def __init__(self, names, refs):
        for n, r in zip(names, refs, strict=True):
            setattr(self, n, r)

def barrier_with(peers):
    sem = pltpu.get_barrier_semaphore()
    total = 0
    for who, zz, ok in peers:
        def send(who=who, zz=zz):
            pl.semaphore_signal(sem, inc=1, device_id=(who, zz), device_id_type=MESH)
        if ok is None:
            send()
            total = total + 1
        else:
            pl.when(ok)(send)
            total = total + ok.astype(jnp.int32)
    pl.semaphore_wait(sem, total)

def blocks(rows, step, body):
    @pl.loop(0, rows // step)
    def _(q):
        body(pl.ds(pl.multiple_of(q * step, step), step))

def tiles(width, tile, body):
    @pl.loop(0, width // tile)
    def _(n):
        body(n, pl.ds(pl.multiple_of(n * tile, tile), tile))

def lanes_at(n, size, offset=0):
    return pl.ds(pl.multiple_of(n, 128) + offset if offset else pl.multiple_of(n, 128), size)

def standard(v):
    centred = v - jnp.mean(v, axis=-1, keepdims=True)
    scale = lax.rsqrt(jnp.mean(centred * centred, axis=-1, keepdims=True) + EPS)
    return centred * scale, scale

def gelu_pair(u):
    half_erf = 0.5 * (1.0 + lax.erf(u * 0.7071067811865476))
    return u * half_erf, half_erf + u * (0.3989422804014327 * jnp.exp(-0.5 * u * u))

class Pump:
    def __init__(self, step, count, ready):
        self.step, self.count, self.ready, self.next, self.clock = step, count, ready, 0, 0.0
    def upto(self, k):
        while self.next <= min(k, self.count - 1):
            self.step(self.next)
            self.next += 1
    def work(self, cost):
        self.clock += cost
        while self.next < self.count and self.ready(self.next) <= self.clock:
            self.upto(self.next)

F_IN = ["q_w", "k_w", "v_w", "o_w", "cq_w", "ck_w", "cv_w", "co_w", "fi_w", "fo_w", "vecs", "hidden", "text", "cot", "q_ids", "k_ids", "t_ids"]
F_OUT = ["weights", "gains", "halo", "first", "q", "k", "v", "lse", "mixed", "after_self", "second", "cq", "tk", "tv", "cmix", "after_cross", "third", "pre_grad", "fo_grad", "block"]
F_SCR = ["s_halo", "s_pool", "s_q", "s_mixed", "s_lse", "s_as", "s_second", "s_cq", "s_tk", "s_tv", "s_cmix", "s_ac", "s_third", "s_act", "s_w", "s_fog", "s_bias", "s_vec", "s_gain", "s_out",
         "lsem", "zs", "zr", "xs", "xr", "fs", "fr", "cs", "cr", "hs", "hr", "ws", "save", "fogs"]

def forward_kernel(zn, rows, frames, *refs):
    r_ = Names(F_IN + F_OUT + F_SCR, refs)
    T, E = rows * frames, 3 * frames
    heads2 = W // 128
    dp, z, core, x, y = place()
    xn = dp + 2 - 4 * x
    yn = dp + 4 - 8 * y
    dn = yn + 2 - 4 * x
    cn = dp + 1 - 2 * core
    up_ok, dn_ok = z < zn - 1, z > 0
    order = [VEC] + list(range(16))
    n = len(order)
    barrier_with([(xn, z, None), (yn, z, None), (cn, z, None), (dp, z + 1, up_ok), (dp, z - 1, dn_ok)])

    def own(i):
        if i == VEC:
            return r_.vecs
        if i < 8:
            return refs[i]
        if i < 12:
            return r_.fi_w.at[:, pl.ds((i - 8) * 256, 256)]
        return r_.fo_w.at[pl.ds((i - 12) * SLAB, SLAB), :]
    def slab(i, who, half=None):
        base = r_.s_vec if i == VEC else r_.weights.at[i]
        size = 16 if i == VEC else SLAB
        if half is None:
            return base.at[pl.ds(pl.multiple_of(who * size, size), size), :]
        h = size // 2
        return base.at[pl.ds(pl.multiple_of(who * size + half * h, h), h), :]
    def block(i, who, j):
        base = r_.s_vec if i == VEC else r_.weights.at[i]
        size, cols = (16, 128) if i == VEC else (SLAB, 256)
        return base.at[pl.ds(pl.multiple_of(who * size, size), size), pl.ds(pl.multiple_of(j * cols, cols), cols)]
    def remote(a, b, s, r, dev):
        return pltpu.make_async_remote_copy(a, b, s, r, device_id=dev, device_id_type=MESH)
    def zcopy(i, j, up, first=False):
        a = own(i) if first else block(i, dp, j)
        return remote(a, block(i, dp, j), r_.zs.at[i, 0 if up else 1, j], r_.zr.at[i, j], (dp, z + 1 if up else z - 1))
    def xcopy(i, d):
        return remote(slab(i, dp), slab(i, dp), r_.xs.at[i, d], r_.xr.at[i, d], ((xn, yn)[d], z))
    def xrecv(i, d):
        who = (xn, yn)[d]
        return remote(slab(i, who), slab(i, who), r_.xs.at[i, d], r_.xr.at[i, d], (who, z))
    def fcopy(i, half):
        who, to = (xn, yn) if half == 0 else (yn, xn)
        return remote(slab(i, who, half), slab(i, who, half), r_.fs.at[i, half], r_.fr.at[i, half], (to, z))
    def frecv(i, half):
        return remote(slab(i, dn, half), slab(i, dn, half), r_.fs.at[i, half], r_.fr.at[i, half], (yn, z))
    def ccopy(i, k):
        who = (dp, xn, yn, dn)[k]
        return remote(slab(i, who), slab(i, who), r_.cs.at[i, k], r_.cr.at[i, k], (cn, z))
    def crecv(i, k):
        who = (dp, xn, yn, dn)[k] + 1 - 2 * core
        return remote(slab(i, who), slab(i, who), r_.cs.at[i, k], r_.cr.at[i, k], (cn, z))
    def lcopy(i):
        return pltpu.make_async_copy(own(i), block(i, dp, z), r_.lsem.at[i])
    def hcopy(r, hop):
        a = r_.s_halo.at[r, 1] if hop else r_.hidden.at[pl.ds(r * frames, frames), :]
        return remote(a, r_.s_halo.at[r, 1 - hop], r_.hs.at[hop, r], r_.hr.at[hop, r], (dp, z + 1))
    def begin(i):
        @pl.when(up_ok)
        def _():
            zcopy(i, z, True, True).start()
        @pl.when(dn_ok)
        def _():
            zcopy(i, z, False, True).start()
        lcopy(i).start()
    def zstage(i, t):
        @pl.when(z - t >= 0)
        def _():
            zcopy(i, z - t, True).wait_recv()
            @pl.when(up_ok)
            def _():
                zcopy(i, z - t, True).start()
        @pl.when(z + t < zn)
        def _():
            zcopy(i, z + t, False).wait_recv()
            @pl.when(dn_ok)
            def _():
                zcopy(i, z + t, False).start()
    done = {i: 0 for i in order}
    def advance(i, s):
        while done[i] < s:
            done[i] += 1
            t = done[i]
            if t < zn - 1:
                zstage(i, t)
            elif t == zn - 1:
                zstage(i, t)
                lcopy(i).wait()
                xcopy(i, 0).start(); xcopy(i, 1).start(); ccopy(i, 0).start()
            elif t == zn:
                for d in range(2):
                    xrecv(i, d).wait_recv()
                    fcopy(i, d).start(); ccopy(i, 1 + d).start()
            elif t == zn + 1:
                frecv(i, 0).wait_recv(); frecv(i, 1).wait_recv()
                ccopy(i, 3).start()
            else:
                for k in range(4):
                    crecv(i, k).wait_recv()
    LAST = zn + 2
    lags = (0, 1, 2, 4, 6, 7)
    AHEAD = 6
    def halo_step(k):
        for r in range(rows):
            if k == 2 * r:
                @pl.when(up_ok)
                def _():
                    hcopy(r, 0).start()
            if k == 2 * r + 4:
                @pl.when(dn_ok)
                def _():
                    hcopy(r, 0).wait_recv()
                    @pl.when(up_ok)
                    def _():
                        hcopy(r, 1).start()
    def step(k):
        if k + AHEAD < n:
            begin(order[k + AHEAD])
        for s, lag in enumerate(lags):
            if 0 <= k - lag < n:
                advance(order[k - lag], s + 1)
        halo_step(k)
    x_time = lambda a: 10.0 + 8.9 * (a + 0.3)
    pump = Pump(step, n + lags[-1], lambda k: x_time(k - 4))
    def need(i):
        a = order.index(i)
        pump.upto(a + 5)
        advance(i, LAST)
        pump.clock = max(pump.clock, x_time(a) + 10.0)
    SLOTS = 3
    slot_of, held = {}, [None] * SLOTS
    def load(i, slot):
        need(i)
        slot_of[i] = slot
        return pltpu.make_async_copy(r_.weights.at[i], r_.s_w.at[slot], r_.ws.at[slot])
    for a in range(AHEAD):
        begin(order[a])

    saves = []
    def save(src, dst):
        c = pltpu.make_async_copy(src, dst, r_.save.at[len(saves)])
        c.start()
        saves.append(c)
        return c
    waited = set()
    def settle(c):
        if id(c) not in waited:
            c.wait()
            waited.add(id(c))

    def dense(lhs, slot, emit, tile=256):
        tiles(W, tile, lambda m, c: emit(m, c, dot(lhs(), r_.s_w[slot, :, c], 1, 0)))
    def gain(k):
        return r_.s_gain[k:k + 1, :]
    def norm(src, dst, at_src, at_dst, count, step, g):
        @pl.loop(0, count // step)
        def _(q):
            o = pl.multiple_of(q * step, step)
            v = src[pl.ds(at_src + o, step), :].astype(F32)
            dst[pl.ds(at_dst + o, step), :] = (standard(v)[0] * gain(g) + gain(g + 1)).astype(BF)

    FIRST, KEY, VAL = 0, rows * E, 2 * rows * E
    pool = r_.s_pool
    @pl.when(z == 0)
    def _():
        r_.s_halo[:, 1] = jnp.zeros((rows, frames, W), BF)
    @pl.when(z <= 1)
    def _():
        r_.s_halo[:, 0] = jnp.zeros((rows, frames, W), BF)

    need(VEC)
    share = W // (8 * zn)
    for d in range(8):
        g = r_.s_vec[pl.ds(d * 16, 16), :].astype(F32)
        total = g[:, :128]
        for j in range(1, zn):
            total = total + pltpu.roll(g[:, j * 128:(j + 1) * 128], j * share, 1)
        r_.s_gain[:, d * 128:(d + 1) * 128] = total
    r_.gains[...] = r_.s_gain[...]
    for r in range(rows):
        norm(r_.hidden, pool, r * frames, FIRST + r * E + 2 * frames, frames, 16, 0)
    pump.work(6)
    c = load(0, 0); c.start(); c.wait()
    for r in range(rows):
        def emit(m, c, v, r=r):
            r_.s_q[pl.ds(r * frames, frames), c] = v.astype(BF)
        dense(lambda r=r: pool[pl.ds(FIRST + r * E + 2 * frames, frames), :], 0, emit)
    save(r_.s_q, r_.q)
    pump.work(3)
    kc = load(1, 1); kc.start()
    vc = load(2, 2); vc.start()
    kc.wait(); vc.wait()

    def attend(r):
        qi = r_.q_ids[pl.ds(r * frames, frames), :]
        r_.s_bias[...] = jnp.where(self_allowed(qi, r_.k_ids[r], E - frames), 0.0, MASKED)
        def pair(p):
            c = pl.ds(pl.multiple_of(p * 128, 128), 128)
            rq = pl.ds(r * frames, frames)
            q2 = r_.s_q[rq, c]
            k2 = pool[pl.ds(KEY + r * E, E), c]
            v2 = pool[pl.ds(VAL + r * E, E), c]
            outs, totals = [], []
            for h in range(2):
                mine = lane_is(q2.shape, h)
                qh = jnp.where(mine, q2 * jnp.asarray(SCALE, BF), jnp.zeros_like(q2))
                s = dot(qh, k2, 1, 1) + r_.s_bias[...]
                top = jnp.max(s, axis=1, keepdims=True)
                p_ = jnp.exp(s - top)
                total = jnp.sum(p_, axis=1, keepdims=True)
                outs.append(dot(p_.astype(BF), v2, 1, 0) / total)
                totals.append(jnp.broadcast_to(top + jnp.log(total), q2.shape))
            first = lane_is(q2.shape, 0)
            r_.s_mixed[rq, c] = jnp.where(first, outs[0], outs[1]).astype(BF)
            r_.s_lse[rq, c] = jnp.where(first, totals[0], totals[1])
        for part in range(2):
            pl.loop(part * heads2 // 2, (part + 1) * heads2 // 2)(pair)
            pump.work(4.5)

    for r in range(rows):
        pump.upto(2 * r + 4)
        @pl.when(z >= 2)
        def _():
            hcopy(r, 1).wait_recv()
        for c in range(2):
            norm(r_.s_halo.at[r, c], pool, 0, FIRST + r * E + c * frames, frames, 16, 0)
        save(r_.s_halo.at[r], r_.halo.at[r])
        save(pool.at[pl.ds(FIRST + r * E, E), :], r_.first.at[pl.ds(r * E, E), :])
        for base, slot in ((KEY, 1), (VAL, 2)):
            def emit(m, c, v, base=base, r=r):
                pool[pl.ds(base + r * E, E), c] = v.astype(BF)
            dense(lambda r=r: pool[pl.ds(FIRST + r * E, E), :], slot, emit)
            save(pool.at[pl.ds(base + r * E, E), :], (r_.k if base == KEY else r_.v).at[pl.ds(r * E, E), :])
        pump.work(6)
        attend(r)
    save(r_.s_mixed, r_.mixed); save(r_.s_lse, r_.lse)

    c = load(3, 0); c.start(); c.wait()
    def emit(m, c, v):
        r_.s_as[:, c] = r_.hidden[:, c].astype(F32) + v
    dense(lambda: r_.s_mixed[...], 0, emit)
    pump.work(3)
    norm(r_.s_as, r_.s_second, 0, 0, T, 48, 2)
    save(r_.s_as, r_.after_self); save(r_.s_second, r_.second)
    pump.work(3)
    c = load(4, 1); c.start(); c.wait()
    def emit(m, c, v):
        r_.s_cq[:, c] = v.astype(BF)
    dense(lambda: r_.s_second[...], 1, emit)
    save(r_.s_cq, r_.cq)
    pump.work(3)
    for i, slot, dst, out in ((5, 2, r_.s_tk, r_.tk), (6, 0, r_.s_tv, r_.tv)):
        c = load(i, slot); c.start(); c.wait()
        def emit(m, c, v, dst=dst):
            dst[:, c] = v.astype(BF)
        dense(lambda: r_.text[...], slot, emit)
        save(dst, out)
        pump.work(2)
    tokens = r_.text.shape[0] // rows
    for r in range(rows):
        def pair(p, r=r):
            c = pl.ds(pl.multiple_of(p * 128, 128), 128)
            rq, rk = pl.ds(r * frames, frames), pl.ds(r * tokens, tokens)
            sh = cross_shares(r_.s_cq[rq, c], pair_keys(r_.s_tk[rk, c]), r_.q_ids[rq, :], r_.t_ids[r], tokens)
            r_.s_cmix[rq, c] = dot(sh.astype(BF), pair_keys(r_.s_tv[rk, c]), 1, 0).astype(BF)
        pl.loop(0, heads2)(pair)
        pump.work(4)
    save(r_.s_cmix, r_.cmix)
    c = load(7, 1); c.start(); c.wait()
    def emit(m, c, v):
        r_.s_ac[:, c] = r_.s_as[:, c] + v
    dense(lambda: r_.s_cmix[...], 1, emit)
    pump.work(3)
    norm(r_.s_ac, r_.s_third, 0, 0, T, 48, 4)
    ac_saved = save(r_.s_ac, r_.after_cross); save(r_.s_third, r_.third)
    pump.work(3)

    for c in saves:
        settle(c)
    SLOPE, PRE = 0, 4 * T
    for i in range(4):
        slot = (2 + i) % SLOTS
        c = load(8 + i, slot); c.start(); c.wait()
        def emit(m, c, v, i=i):
            act, slope = gelu_pair(v)
            for h in range(2):
                to = (i % 2) * 2 + h
                lanes = pl.ds(pl.multiple_of((2 * m + i // 2) * 128, 128), 128)
                part = slice(h * 128, (h + 1) * 128)
                r_.s_act[to, :, lanes] = act[:, part].astype(BF)
                pool[pl.ds(SLOPE + to * T, T), lanes] = slope[:, part].astype(BF)
        dense(lambda: r_.s_third[...], slot, emit)
        pump.work(5)
    fog = []
    def out_grad(i):
        def body(m, c):
            r_.s_fog[i % 2, c, :] = dot(r_.s_act[i, :, c], r_.cot[...], 0, 0).astype(BF)
        if i >= 2:
            fog[i - 2].wait()
        tiles(W, 256, body)
        g = pltpu.make_async_copy(r_.s_fog.at[i % 2], r_.fo_grad.at[i], r_.fogs.at[i])
        g.start()
        fog.append(g)
        pump.work(4)
    for i in range(4):
        out_grad(i)
    for i in range(4):
        slot = i % SLOTS
        c = load(12 + i, slot); c.start(); c.wait()
        def emit(m, c, v):
            r_.s_ac[:, c] = r_.s_ac[:, c] + v
        dense(lambda i=i: r_.s_act[i], slot, emit)
        def body(m, c, i=i, slot=slot):
            v = dot(r_.cot[...], r_.s_w[slot, c, :], 1, 1)
            v = v * pool[pl.ds(SLOPE + i * T, T), c].astype(F32)
            for h in range(2):
                to = h * 2 + i // 2
                lanes = pl.ds(pl.multiple_of(m * 256, 256) + (i % 2) * 128, 128)
                pool[pl.ds(PRE + to * T, T), lanes] = v[:, h * 128:(h + 1) * 128].astype(BF)
        tiles(W, 256, body)
        pump.work(5)
    def body(s):
        r_.s_out[s, :] = r_.s_ac[s, :].astype(BF)
    blocks(T, 48, body)
    save(r_.s_out, r_.block)
    for i in range(4):
        save(pool.at[pl.ds(PRE + i * T, T), :], r_.pre_grad.at[i])

    pump.upto(pump.count)
    for i in order:
        advance(i, LAST)
    for c in fog[2:]:
        c.wait()
    for c in saves:
        settle(c)
    for r in range(rows):
        @pl.when(up_ok)
        def _():
            hcopy(r, 0).wait_send()
        @pl.when(up_ok & dn_ok)
        def _():
            hcopy(r, 1).wait_send()
    for i in order:
        for j in range(zn):
            @pl.when(up_ok & (j <= z))
            def _():
                zcopy(i, j, True).wait_send()
            @pl.when(dn_ok & (j >= z))
            def _():
                zcopy(i, j, False).wait_send()
        for k in range(2):
            xcopy(i, k).wait_send(); fcopy(i, k).wait_send()
        for k in range(4):
            ccopy(i, k).wait_send()

def forward(weights, vecs, hidden, text, cot, q_ids, k_ids, t_ids, zn, rows, frames, cid=2):
    T, E = rows * frames, 3 * frames
    S = jax.ShapeDtypeStruct
    D, V = pltpu.SemaphoreType.DMA, pltpu.VMEM
    VM = pl.BlockSpec(memory_space=pltpu.VMEM)
    tok = text.shape[0]
    outs = dict(weights=S((16, W, W), BF), gains=S((16, W), F32), halo=S((rows, 2, frames, W), BF), first=S((rows * E, W), BF), q=S((T, W), BF), k=S((rows * E, W), BF),
                v=S((rows * E, W), BF), lse=S((T, W), F32), mixed=S((T, W), BF), after_self=S((T, W), F32), second=S((T, W), BF), cq=S((T, W), BF), tk=S((tok, W), BF), tv=S((tok, W), BF),
                cmix=S((T, W), BF), after_cross=S((T, W), F32), third=S((T, W), BF), pre_grad=S((4, T, W), BF), fo_grad=S((4, W, W), BF), block=S((T, W), BF))
    scratch = [V((rows, 2, frames, W), BF), V((3 * rows * E, W), BF), V((T, W), BF), V((T, W), BF), V((T, W), F32), V((T, W), F32), V((T, W), BF), V((T, W), BF), V((tok, W), BF), V((tok, W), BF),
               V((T, W), BF), V((T, W), F32), V((T, W), BF), V((4, T, W), BF), V((3, W, W), BF), V((2, W, W), BF), V((frames, E), F32), V((128, 512), BF), V((16, W), F32), V((T, W), BF)]
    n = 17
    scratch += [D((n,)), D((n, 2, zn)), D((n, zn)), D((n, 2)), D((n, 2)), D((n, 2)), D((n, 2)), D((n, 4)), D((n, 4)), D((2, rows)), D((2, rows)), D((3,)), D((48,)), D((4,))]
    result = pl.pallas_call(
        functools.partial(forward_kernel, zn, rows, frames),
        out_shape=[outs[k] for k in F_OUT],
        in_specs=[VM] * len(F_IN), out_specs=[VM if k == "gains" else ANY for k in F_OUT],
        scratch_shapes=scratch,
        compiler_params=pltpu.CompilerParams(collective_id=cid, has_side_effects=True, vmem_limit_bytes=62 << 20),
        name="forward",
    )(*weights, vecs, hidden, text, cot, q_ids, k_ids, t_ids)
    return dict(zip(F_OUT, result))

SLOTS_G, SLOTS_A = 3, 8

def add_rows(dst, terms, rows, step=32):
    step = min(step, rows)
    @pl.loop(0, rows // step)
    def _(q):
        s = pl.ds(pl.multiple_of(q * step, step), step)
        total = terms[0][s, :].astype(F32)
        for t in terms[1:]:
            total = total + t[s, :].astype(F32)
        dst[s, :] = total.astype(dst.dtype)

def fold(v):
    return jnp.sum(v.reshape(v.shape[0] // 8, 8, v.shape[1]), axis=0)

B_IN = ["gains", "q_ids", "k_ids", "t_ids", "text",
        "hidden", "cot", "weights", "halo", "first", "q", "k", "v", "lse", "mixed", "after_self", "second", "cq", "tk", "tv", "cmix", "after_cross", "third", "pre_grad", "fo_grad"]
B_IN_VMEM = 5
B_OUT = ["g_q", "g_k", "g_v", "g_o", "g_cq", "g_ck", "g_cv", "g_co", "g_fi", "g_fo", "g_vec", "g_text", "g_hidden"]
B_SCR = ["p", "fa", "fb", "fc", "w", "g", "acc", "rh", "rxy", "rz", "vg", "vacc", "vrh", "vrxy", "vrz", "t", "tsrc", "trz", "h2s", "h2l", "h1", "hb", "hal", "bias", "sums",
         "cs", "cr", "ds", "dr", "xs", "xr", "zs", "zr", "ts", "tr", "hs", "hr", "credit", "ld", "ws", "outsem"]

def backward_kernel(zn, rows, frames, *refs):
    r_ = Names(B_IN + B_OUT + B_SCR, refs)
    T, E = rows * frames, 3 * frames
    heads2 = W // 128
    dp, z, core, x, y = place()
    xn = dp + 2 - 4 * x
    yn = dp + 4 - 8 * y
    dn = yn + 2 - 4 * x
    flip = 1 - 2 * core
    cn = dp + flip
    up_ok, dn_ok = z < zn - 1, z > 0
    peers = [(xn, z, None), (yn, z, None), (cn, z, None), (dp, z + 1, up_ok), (dp, z - 1, dn_ok)]
    barrier_with(peers)
    order = [12, 13, 14, 15, 8, 9, 10, 11, 7, 4, 5, 6, 3, 1, 2, 0, VEC]
    place_of = {i: a for a, i in enumerate(order)}
    fam = (dp, xn, yn, dn)

    def size(i):
        return (16, 128) if i == VEC else (SLAB, 256)
    def g(i):
        return r_.vg if i == VEC else r_.g.at[place_of[i] % SLOTS_G]
    def buf(i, big, small, *rest):
        base = small if i == VEC else big.at[place_of[i] % SLOTS_A]
        return base.at[rest] if rest else base
    def acc(i, k):
        return buf(i, r_.acc, r_.vacc, k)
    def gslab(i, who):
        s = size(i)[0]
        return g(i).at[pl.ds(pl.multiple_of(who * s, s), s), :]
    def remote(a, b, s, r, dev):
        return pltpu.make_async_remote_copy(a, b, s, r, device_id=dev, device_id_type=MESH)
    def ccopy(i, k):
        return remote(gslab(i, fam[k] + flip), acc(i, k), r_.cs.at[i, k], r_.cr.at[i, k], (cn, z))
    def half(ref, i, h):
        n = size(i)[0] // 2
        return ref.at[pl.ds(h * n, n), :]
    def dcopy(i, h):
        return remote(half(acc(i, 3), i, h), buf(i, r_.rh, r_.vrh, h), r_.ds.at[i, h], r_.dr.at[i, h], ((xn, yn)[h], z))
    def xcopy(i, d, h):
        return remote(half(acc(i, 1 + d), i, h), half(buf(i, r_.rxy, r_.vrxy, d), i, h), r_.xs.at[i, d, h], r_.xr.at[i, d, h], ((xn, yn)[d], z))
    def col(ref, i, j):
        c = size(i)[1]
        return ref.at[:, pl.ds(j * c, c)]
    def landing(up, zz, j):
        return j - zz if up else zn - zz + j
    def zcopy(i, up, zz, j):
        to = zz + 1 if up else zz - 1
        return remote(col(acc(i, 0), i, j), buf(i, r_.rz, r_.vrz, landing(up, to, j)), r_.zs.at[i, 0 if up else 1, j], r_.zr.at[i, 0 if up else 1, j], (dp, to))
    def zrecv(i, up, zz, j):
        b = buf(i, r_.rz, r_.vrz, landing(up, zz, j))
        return remote(b, b, r_.zs.at[i, 0 if up else 1, j], r_.zr.at[i, 0 if up else 1, j], (dp, zz - 1 if up else zz + 1))
    def zroles(t, body):
        for up in (True, False):
            zz = t if up else zn - 1 - t
            pl.when(z == zz)(functools.partial(body, up, zz))
    def zstage(i, t):
        def body(up, zz):
            for j in (range(zz + 1, zn) if up else range(zz - 1, -1, -1)):
                if t > 0:
                    zrecv(i, up, zz, j).wait_recv()
                    a = col(acc(i, 0), i, j)
                    add_rows(a, [a, buf(i, r_.rz, r_.vrz, landing(up, zz, j))], size(i)[0])
                zcopy(i, up, zz, j).start()
            if t > 0:
                zrecv(i, up, zz, zz).wait_recv()
        zroles(t, body)
    def result(i):
        if i == VEC:
            return r_.g_vec
        if i < 8:
            return refs[len(B_IN) + i]
        if i < 12:
            return r_.g_fi.at[:, pl.ds((i - 8) * 256, 256)]
        return r_.g_fo.at[pl.ds((i - 12) * SLAB, SLAB), :]
    def final(i):
        for zz in range(zn):
            @pl.when(z == zz)
            def _(zz=zz):
                terms = [col(acc(i, 0), i, zz)]
                if zz > 0:
                    terms.append(buf(i, r_.rz, r_.vrz, landing(True, zz, zz)))
                if zz < zn - 1:
                    terms.append(buf(i, r_.rz, r_.vrz, landing(False, zz, zz)))
                add_rows(result(i), terms, size(i)[0])
                for j in range(zn):
                    if j > zz:
                        zcopy(i, True, zz, j).wait_send()
                    if j < zz:
                        zcopy(i, False, zz, j).wait_send()
        for h in range(2):
            dcopy(i, h).wait_send()
            for d in range(2):
                xcopy(i, d, h).wait_send()
        if place_of[i] + SLOTS_A < 16:
            for s, (who, zz, ok) in enumerate(peers):
                def send(s=s, who=who, zz=zz):
                    pl.semaphore_signal(r_.credit.at[(0, 1, 2, 4, 3)[s]], inc=1, device_id=(who, zz), device_id_type=MESH)
                send() if ok is None else pl.when(ok)(send)
    FINAL = 3 + zn
    done = {}
    def advance(i, upto):
        while done[i] < upto:
            done[i] += 1
            s = done[i]
            rows_ = size(i)[0]
            if s == 1:
                for k in (3, 1, 2, 0):
                    ccopy(i, k).wait_recv()
                    add_rows(acc(i, k), [acc(i, k), gslab(i, fam[k])], rows_)
                    if k == 1:
                        dcopy(i, 0).start(); dcopy(i, 1).start()
                    if k == 2:
                        xcopy(i, 0, 0).start()
                    if k == 0:
                        xcopy(i, 1, 1).start()
                for k in range(4):
                    ccopy(i, k).wait_send()
            elif s == 2:
                for d, h in ((1, 0), (0, 1)):
                    dcopy(i, h).wait_recv()
                    a = half(acc(i, 1 + d), i, h)
                    add_rows(a, [a, buf(i, r_.rh, r_.vrh, h)], rows_ // 2)
                xcopy(i, 1, 0).start(); xcopy(i, 0, 1).start()
            elif s == 3:
                for d in range(2):
                    for h in range(2):
                        xcopy(i, d, h).wait_recv()
                add_rows(acc(i, 0), [acc(i, 0), buf(i, r_.rxy, r_.vrxy, 0), buf(i, r_.rxy, r_.vrxy, 1)], rows_)
                zstage(i, 0)
            elif s < FINAL:
                zstage(i, s - 3)
            else:
                final(i)
    clock = [0.0, 0.0]
    pending = []
    def run_pending(now):
        pending.sort()
        while pending and pending[0][0] <= now:
            _, i, s = pending.pop(0)
            advance(i, s)
    def work(cost):
        clock[0] += cost
        run_pending(clock[0])
    def grab(i):
        a = place_of[i]
        if i != VEC and a >= SLOTS_G:
            advance(order[a - SLOTS_G], 1)
        return g(i)
    def submit(i):
        a = place_of[i]
        done[i] = 0
        if i != VEC and a >= SLOTS_A:
            advance(order[a - SLOTS_A], FINAL)
            for s, (_, _, ok) in enumerate(peers):
                def take(s=s):
                    pl.semaphore_wait(r_.credit.at[s], 1)
                take() if ok is None else pl.when(ok)(take)
        for k in (3, 1, 2, 0):
            ccopy(i, k).start()
        t1 = clock[0] + 4.0
        b = max(t1, clock[1])
        clock[1] = b + 8.9
        for s, t in enumerate([t1, b + 5.0, b + 10.0] + [b + 10.0 + 2.5 * q for q in range(1, zn)] + [b + 10.0 + 2.5 * zn]):
            pending.append((t, i, s + 1))

    loads = [0]
    def fetch(src, dst):
        c = pltpu.make_async_copy(src, dst, r_.ld.at[loads[0]])
        loads[0] += 1
        c.start()
        return c
    wslot = [0]
    def weight(i):
        s = wslot[0] % 2
        wslot[0] += 1
        c = pltpu.make_async_copy(r_.weights.at[i], r_.w.at[s], r_.ws.at[i])
        c.start()
        return s, c
    p = r_.p
    def rows_of(at, count):
        return p.at[pl.ds(at, count), :]
    def outer(lhs, rhs, dst):
        def body(m, c):
            dst[c, :] = dot(lhs(c), rhs(), 0, 0).astype(BF)
        tiles(W, 256, body)
    def back(grad, slot, emit):
        def body(m, c):
            emit(c, dot(grad(), r_.w[slot, c, :], 1, 1))
        tiles(W, 256, body)
    def gain(k):
        return r_.gains[k:k + 1, :]
    def add_sum(k, v):
        r_.sums[pl.ds(k * 8, 8), :] += fold(v)
    def norm_back(k, value, grad, resid, out, low, count=T, step=48, sums=True):
        def body(s):
            xhat, scale = standard(value(s))
            gr = grad(s)
            if sums:
                add_sum(k, gr * xhat)
                add_sum(k + 1, gr)
            e = gr * gain(k)
            inner = jnp.mean(e * xhat, axis=-1, keepdims=True)
            v = resid(s) + scale * (e - jnp.mean(e, axis=-1, keepdims=True) - xhat * inner)
            out[s, :] = v
            if low is not None:
                low[s, :] = v.astype(BF)
        blocks(count, step, body)

    K, V, FI, Q, DO = 0, rows * E, 2 * rows * E, 3 * rows * E, 3 * rows * E + T
    r_.sums[...] = jnp.zeros_like(r_.sums)
    fo_loads = [fetch(r_.fo_grad.at[i], grab(12 + i)) for i in range(SLOTS_G)]
    third_c = fetch(r_.third, rows_of(FI, T))
    pg = [fetch(r_.pre_grad.at[i], rows_of(K + i * T, T)) for i in range(3)]
    cot_c = fetch(r_.cot, rows_of(V, T))
    ac_c = fetch(r_.after_cross, r_.fc)
    for i in range(SLOTS_G):
        fo_loads[i].wait()
        submit(12 + i)
        work(0.5)
    third_c.wait()
    nxt = weight(8)
    pg.append(fetch(r_.pre_grad.at[3], rows_of(V + T, T)))
    at_pg = [K, K + T, K + 2 * T, V + T]
    for i in range(4):
        slot, wc = nxt
        pg[i].wait(); wc.wait()
        if i < 3:
            nxt = weight(9 + i)
        def emit(c, v, i=i):
            r_.fa[:, c] = v if i == 0 else r_.fa[:, c] + v
        back(lambda i=i: p[pl.ds(at_pg[i], T), :], slot, emit)
        work(2.5)
        if i == 0:
            for q in range(SLOTS_G, 4):
                c = fetch(r_.fo_grad.at[q], grab(12 + q)); c.wait()
                submit(12 + q)
                work(0.5)
        outer(lambda c: p[pl.ds(FI, T), c], lambda i=i: p[pl.ds(at_pg[i], T), :], grab(8 + i))
        submit(8 + i)
        work(2.5)
    cmix_c = fetch(r_.cmix, rows_of(V + T, T))
    co_slot, co_c = weight(7)
    cq_c = fetch(r_.cq, rows_of(FI, T))
    second_c = fetch(r_.second, rows_of(FI + T, T))
    mixed_c = fetch(r_.mixed, rows_of(FI + 2 * T, T))
    k_c = fetch(r_.k, rows_of(K, rows * E))
    t_c = [fetch(r_.tk, r_.t.at[0]), fetch(r_.tv, r_.t.at[1])]
    cot_c.wait(); ac_c.wait()
    norm_back(4, lambda s: r_.fc[s, :], lambda s: r_.fa[s, :], lambda s: p[pl.ds(pl.multiple_of(V + s.start, 16), s.size), :].astype(F32), r_.fa, rows_of(DO, T))
    as_c = fetch(r_.after_self, r_.fc)
    work(4)
    cmix_c.wait(); co_c.wait()
    outer(lambda c: p[pl.ds(V + T, T), c], lambda: p[pl.ds(DO, T), :], grab(7))
    submit(7)
    work(2)
    def emit(c, v):
        p[pl.ds(V + 2 * T, T), c] = v.astype(BF)
    back(lambda: p[pl.ds(DO, T), :], co_slot, emit)
    work(2)
    cqw_slot, cqw_c = weight(4)
    ckw_slot, ckw_c = weight(5)
    cq_c.wait(); t_c[0].wait(); t_c[1].wait()
    tokens = r_.text.shape[0] // rows
    for r in range(rows):
        def pair(h, r=r):
            c = pl.ds(pl.multiple_of(h * 128, 128), 128)
            rk = pl.ds(r * tokens, tokens)
            qrows = pl.ds(FI + r * frames, frames)
            q2, d2 = p[qrows, c], p[pl.ds(V + 2 * T + r * frames, frames), c]
            kk, vv = pair_keys(r_.t[0, rk, c]), pair_keys(r_.t[1, rk, c])
            sh = cross_shares(q2, kk, r_.q_ids[pl.ds(r * frames, frames), :], r_.t_ids[r], tokens)
            dsh = dot(d2, vv, 1, 1)
            ds = (sh * (dsh - halves(sh * dsh, tokens, jnp.sum, 0.0))).astype(BF)
            p[qrows, c] = (dot(ds, kk, 1, 0) * SCALE).astype(BF)
            gk = dot(ds, q2, 0, 0) * SCALE
            gv = dot(sh.astype(BF), d2, 0, 0)
            first = lane_is((tokens, 128), 0)
            r_.t[0, rk, c] = jnp.where(first, gk[:tokens], gk[tokens:]).astype(BF)
            r_.t[1, rk, c] = jnp.where(first, gv[:tokens], gv[tokens:]).astype(BF)
        pl.loop(0, heads2)(pair)
        work(5)
    v_c = fetch(r_.v, rows_of(V, rows * E))
    second_c.wait()
    outer(lambda c: p[pl.ds(FI + T, T), c], lambda: p[pl.ds(FI, T), :], grab(4))
    submit(4)
    work(2)
    cqw_c.wait()
    def emit(c, v):
        r_.fb[:, c] = v
    back(lambda: p[pl.ds(FI, T), :], cqw_slot, emit)
    work(2)
    cvw_slot, cvw_c = weight(6)
    as_c.wait()
    norm_back(2, lambda s: r_.fc[s, :], lambda s: r_.fb[s, :], lambda s: r_.fa[s, :], r_.fa, rows_of(Q, T))
    lse_c = fetch(r_.lse, r_.fc)
    work(4)
    outer(lambda c: r_.text[:, c], lambda: r_.t[0], grab(5))
    submit(5)
    work(1)
    ckw_c.wait()
    def body(m, c):
        v = dot(r_.t[0], r_.w[ckw_slot, c, :], 1, 1)
        r_.fb[pl.ds(0, rows * tokens), c] = v
    tiles(W, 256, body)
    ow_slot, ow_c = weight(3)
    outer(lambda c: r_.text[:, c], lambda: r_.t[1], grab(6))
    submit(6)
    work(1)
    cvw_c.wait()
    part = tokens // zn
    def body(m, c):
        v = r_.fb[pl.ds(0, rows * tokens), c] + dot(r_.t[1], r_.w[cvw_slot, c, :], 1, 1)
        for r in range(rows):
            for j in range(zn):
                r_.tsrc[j, r * part:(r + 1) * part, c] = v[r * tokens + j * part:r * tokens + (j + 1) * part].astype(BF)
    tiles(W, 256, body)
    kw_slot, kw_c = weight(1)
    def tcopy(up, zz, j):
        to = zz + 1 if up else zz - 1
        return remote(r_.tsrc.at[j], r_.trz.at[landing(up, to, j)], r_.ts.at[0 if up else 1, j], r_.tr.at[0 if up else 1, j], (dp, to))
    def trecv(up, zz, j):
        b = r_.trz.at[landing(up, zz, j)]
        return remote(b, b, r_.ts.at[0 if up else 1, j], r_.tr.at[0 if up else 1, j], (dp, zz - 1 if up else zz + 1))
    def tstage(t):
        def body(up, zz):
            for j in (range(zz + 1, zn) if up else range(zz - 1, -1, -1)):
                if t > 0:
                    trecv(up, zz, j).wait_recv()
                    add_rows(r_.tsrc.at[j], [r_.tsrc.at[j], r_.trz.at[landing(up, zz, j)]], rows * part, 16)
                tcopy(up, zz, j).start()
            if t > 0:
                trecv(up, zz, zz).wait_recv()
        zroles(t, body)
    def tfinal():
        for zz in range(zn):
            @pl.when(z == zz)
            def _(zz=zz):
                terms = [r_.tsrc.at[zz]]
                if zz > 0:
                    terms.append(r_.trz.at[landing(True, zz, zz)])
                if zz < zn - 1:
                    terms.append(r_.trz.at[landing(False, zz, zz)])
                add_rows(r_.g_text, terms, rows * part, 16)
                for j in range(zn):
                    if j > zz:
                        tcopy(True, zz, j).wait_send()
                    if j < zz:
                        tcopy(False, zz, j).wait_send()
    tstage(0)
    mixed_c.wait()
    outer(lambda c: p[pl.ds(FI + 2 * T, T), c], lambda: p[pl.ds(Q, T), :], grab(3))
    submit(3)
    work(2)
    ow_c.wait()
    def emit(c, v):
        p[pl.ds(DO, T), c] = v.astype(BF)
    back(lambda: p[pl.ds(Q, T), :], ow_slot, emit)
    work(2)
    vw_slot, vw_c = weight(2)
    q_c = fetch(r_.q, rows_of(Q, T))
    first_c = fetch(r_.first, rows_of(FI, rows * E))
    tstage(1)
    lse_c.wait(); k_c.wait(); v_c.wait(); q_c.wait()
    kw_c.wait(); vw_c.wait()

    def h2copy(r):
        return remote(r_.h2s.at[r], r_.h2l.at[r], r_.hs.at[0, r], r_.hr.at[0, r], (dp, z - 1))
    def h1copy(r):
        return remote(r_.h1.at[r], r_.hb.at[r], r_.hs.at[1, r], r_.hr.at[1, r], (dp, z - 1))
    def pass_on(r):
        @pl.when(dn_ok)
        def _():
            @pl.when(up_ok)
            def _():
                h2copy(r).wait_recv()
                add_rows(r_.h1.at[r], [r_.h1.at[r], r_.h2l.at[r]], frames, 16)
            h1copy(r).start()
    for r in range(rows):
        hal_c = fetch(r_.halo.at[r], r_.hal)
        r_.bias[...] = jnp.where(self_allowed(r_.q_ids[pl.ds(r * frames, frames), :], r_.k_ids[r], E - frames), 0.0, MASKED)
        def pair(h, r=r):
            c = pl.ds(pl.multiple_of(h * 128, 128), 128)
            rq, rk, rv = pl.ds(Q + r * frames, frames), pl.ds(K + r * E, E), pl.ds(V + r * E, E)
            q2, k2, v2, d2 = p[rq, c], p[rk, c], p[rv, c], p[pl.ds(DO + r * frames, frames), c]
            total = r_.fc[pl.ds(r * frames, frames), c]
            gq, gk, gv = [], [], []
            for h_ in range(2):
                mine = lane_is(q2.shape, h_)
                zero = jnp.zeros_like(q2)
                qh = jnp.where(mine, q2 * jnp.asarray(SCALE, BF), zero)
                dh = jnp.where(mine, d2, zero)
                s = dot(qh, k2, 1, 1) + r_.bias[...]
                sh = jnp.exp(s - total[:, h_ * HEAD:h_ * HEAD + 1])
                dsh = dot(dh, v2, 1, 1)
                ds = (sh * (dsh - jnp.sum(sh * dsh, axis=1, keepdims=True))).astype(BF)
                gq.append(dot(ds, k2, 1, 0) * SCALE)
                gk.append(dot(ds, qh, 0, 0))
                gv.append(dot(sh.astype(BF), dh, 0, 0))
            p[rq, c] = jnp.where(lane_is(q2.shape, 0), gq[0], gq[1]).astype(BF)
            p[rk, c] = (gk[0] + gk[1]).astype(BF)
            p[rv, c] = (gv[0] + gv[1]).astype(BF)
        for part_ in range(2):
            pl.loop(part_ * heads2 // 2, (part_ + 1) * heads2 // 2)(pair)
            work(6.5)
        def body(m, c, r=r):
            v = dot(p[pl.ds(K + r * E, E), :], r_.w[kw_slot, c, :], 1, 1) + dot(p[pl.ds(V + r * E, E), :], r_.w[vw_slot, c, :], 1, 1)
            r_.h2s[r, :, c] = v[:frames].astype(BF)
            r_.h1[r, :, c] = v[frames:2 * frames].astype(BF)
            r_.fb[pl.ds(r * frames, frames), c] = v[2 * frames:]
        tiles(W, 256, body)
        hal_c.wait()
        for q in range(2):
            src = (r_.h2s, r_.h1)[q]
            def body(s, q=q, src=src, r=r):
                gr = src[r, s, :].astype(F32)
                add_sum(0, gr * standard(r_.hal[q, s, :].astype(F32))[0])
                add_sum(1, gr)
            blocks(frames, 16, body)
        @pl.when(z >= 2)
        def _():
            h2copy(r).start()
        if r == 0:
            tstage(2)
        if r == 1:
            tstage(3)
            tfinal()
        work(5)
        if r > 0:
            pass_on(r - 1)
    hid_c = fetch(r_.hidden, rows_of(DO, T))
    qw_slot, qw_c = weight(0)
    first_c.wait()
    outer(lambda c: p[pl.ds(FI, rows * E), c], lambda: p[pl.ds(K, rows * E), :], grab(1))
    submit(1)
    work(4)
    pass_on(rows - 1)
    outer(lambda c: p[pl.ds(FI, rows * E), c], lambda: p[pl.ds(V, rows * E), :], grab(2))
    submit(2)
    work(4)
    gq_ = grab(0)
    def body(m, c):
        total = None
        for r in range(rows):
            v = dot(p[pl.ds(FI + r * E + 2 * frames, frames), c], p[pl.ds(Q + r * frames, frames), :], 0, 0)
            total = v if total is None else total + v
        gq_[c, :] = total.astype(BF)
    tiles(W, 256, body)
    submit(0)
    work(2)
    qw_c.wait(); hid_c.wait()
    def emit(c, v):
        r_.fb[:, c] = r_.fb[:, c] + v
    back(lambda: p[pl.ds(Q, T), :], qw_slot, emit)
    work(2)
    def body(s):
        gr = r_.fb[s, :]
        add_sum(0, gr * standard(p[pl.ds(pl.multiple_of(DO + s.start, 16), s.size), :].astype(F32))[0])
        add_sum(1, gr)
    blocks(T, 48, body)
    sums = jnp.sum(r_.sums[...].reshape(6, 8, W), axis=1)
    sums = jnp.concatenate([sums, jnp.zeros((10, W), F32)], axis=0)
    share = W // (8 * zn)
    keep = lax.broadcasted_iota(jnp.int32, (16, 128), 1) < share
    for d in range(8):
        v = sums[:, d * 128:(d + 1) * 128]
        for j in range(zn):
            moved = pltpu.roll(v, (128 - j * share) % 128, 1)
            r_.vg[d * 16:(d + 1) * 16, j * 128:(j + 1) * 128] = jnp.where(keep, moved, 0.0).astype(BF)
    submit(VEC)
    work(3)
    for r in range(rows):
        @pl.when(up_ok)
        def _():
            h1copy(r).wait_recv()
            add_rows(r_.fb.at[pl.ds(r * frames, frames), :], [r_.fb.at[pl.ds(r * frames, frames), :], r_.hb.at[r]], frames, 16)
    norm_back(0, lambda s: p[pl.ds(pl.multiple_of(DO + s.start, 16), s.size), :].astype(F32), lambda s: r_.fb[s, :], lambda s: r_.fa[s, :], r_.fa, None, sums=False)
    oc = pltpu.make_async_copy(r_.fa, r_.g_hidden, r_.outsem.at[0])
    oc.start()
    run_pending(1e9)
    oc.wait()
    for r in range(rows):
        @pl.when(z >= 2)
        def _():
            h2copy(r).wait_send()
        @pl.when(dn_ok)
        def _():
            h1copy(r).wait_send()

def backward(f, hidden, text, cot, q_ids, k_ids, t_ids, zn, rows, frames, cid=3):
    T, E = rows * frames, 3 * frames
    S = jax.ShapeDtypeStruct
    D, V = pltpu.SemaphoreType.DMA, pltpu.VMEM
    VM = pl.BlockSpec(memory_space=pltpu.VMEM)
    tok = text.shape[0]
    part = tok // zn
    vals = dict(f, hidden=hidden, text=text, cot=cot, q_ids=q_ids, k_ids=k_ids, t_ids=t_ids)
    outs = [S((128, 256), F32)] * 8 + [S((128, 1024), F32), S((512, 256), F32), S((16, 128), F32), S((part, W), F32), S((T, W), F32)]
    A = SLOTS_A
    scratch = [V((3 * rows * E + 2 * T, W), BF), V((T, W), F32), V((T, W), F32), V((T, W), F32), V((2, W, W), BF), V((SLOTS_G, W, W), BF),
               V((A, 4, 128, W), BF), V((A, 2, 64, W), BF), V((A, 2, 128, W), BF), V((A, zn + 1, 128, 256), BF),
               V((128, 512), BF), V((4, 16, 512), BF), V((2, 8, 512), BF), V((2, 16, 512), BF), V((zn + 1, 16, 128), BF),
               V((2, tok, W), BF), V((zn, part, W), BF), V((zn + 1, part, W), BF),
               V((rows, frames, W), BF), V((rows, frames, W), BF), V((rows, frames, W), BF), V((rows, frames, W), BF), V((2, frames, W), BF), V((frames, E), F32), V((48, W), F32)]
    n = 17
    scratch += [D((n, 4)), D((n, 4)), D((n, 2)), D((n, 2)), D((n, 2, 2)), D((n, 2, 2)), D((n, 2, zn)), D((n, 2, zn)), D((2, zn)), D((2, zn)), D((2, rows)), D((2, rows)),
                pltpu.SemaphoreType.REGULAR((5,)), D((40,)), D((16,)), D((1,))]
    return pl.pallas_call(
        functools.partial(backward_kernel, zn, rows, frames),
        out_shape=outs,
        in_specs=[VM] * B_IN_VMEM + [ANY] * (len(B_IN) - B_IN_VMEM), out_specs=[VM] * (len(B_OUT) - 1) + [ANY],
        scratch_shapes=scratch,
        compiler_params=pltpu.CompilerParams(collective_id=cid, has_side_effects=True, vmem_limit_bytes=63 << 20),
        name="backward",
    )(*[vals[k] for k in B_IN])

EPSILON = 1e-05

def project(left_side, right_side, kind=F32):
    return jnp.einsum("rfk,kn->rfn", left_side, right_side, preferred_element_type=F32).astype(kind)

def project_back(gradient, right_side, kind=F32):
    return jnp.einsum("rfn,kn->rfk", gradient, right_side, preferred_element_type=F32).astype(kind)

def weight_grad(left_side, gradient):
    return jnp.einsum("rfk,rfn->kn", left_side, gradient, preferred_element_type=F32).astype(BF)

def normalized(values):
    values = values.astype(F32)
    centred = values - jnp.mean(values, axis=-1, keepdims=True)
    scale = lax.rsqrt(jnp.mean(centred * centred, axis=-1, keepdims=True) + EPSILON)
    return centred * scale, scale

def norm_back(values, gain, grad):
    xhat, scale = normalized(values)
    e = gain * grad
    inner = jnp.mean(e * xhat, axis=-1, keepdims=True)
    inputs = scale * (e - jnp.mean(e, axis=-1, keepdims=True) - xhat * inner)
    return jnp.sum(grad * xhat, axis=(0, 1)), jnp.sum(grad, axis=(0, 1)), inputs

def gelu_parts(u):
    half_erf = 0.5 * (1.0 + lax.erf(u * 0.7071067811865476))
    return u * half_erf, half_erf + u * (0.3989422804014327 * jnp.exp(-0.5 * u * u))

def gather_all(weights, vectors, hidden, dpn, zn):
    rows, frames, width = hidden.shape
    share = vectors.shape[1]
    if (dpn, zn) == (8, 4):
        packed = jnp.pad(vectors, ((0, 16 - vectors.shape[0]), (0, 128 - share)))
        *whole, packed, ext = gather(list(weights) + [packed], hidden, dpn, zn)
        packed = packed.reshape(dpn, 16, zn, 128)[:, :vectors.shape[0], :, :share]
        return whole, packed.transpose(1, 0, 2, 3).reshape(vectors.shape[0], width), ext
    whole = [lax.all_gather(lax.all_gather(w, "ctx", axis=1, tiled=True), "dp", axis=0, tiled=True) for w in weights]
    near = lax.ppermute(hidden, "ctx", [(i, i + 1) for i in range(zn - 1)])
    far = lax.ppermute(hidden, "ctx", [(i, i + 2) for i in range(zn - 2)])
    return whole, lax.all_gather(vectors, ("dp", "ctx"), axis=1, tiled=True), jnp.stack([far, near, hidden], axis=1)

def scatter_all(grads, vectors, text, halo, dpn, zn):
    count, width = vectors.shape
    rows, tokens = text.shape[:2]
    if (dpn, zn) == (8, 4):
        share = width // (dpn * zn)
        packed = jnp.pad(vectors.reshape(count, dpn, zn, share).transpose(1, 0, 2, 3), ((0, 0), (0, 16 - count), (0, 0), (0, 128 - share)))
        packed = packed.reshape(dpn * 16, zn * 128).astype(BF)
        folded = text.reshape(rows, zn, tokens // zn, width).transpose(0, 2, 1, 3).reshape(rows * tokens // zn, zn * width)
        *own, packed, folded, back = scatter(list(grads) + [packed], folded, halo, dpn, zn)
        return own, packed[:count, :share], folded.reshape(rows, tokens // zn, width), back
    own = [lax.psum_scatter(lax.psum_scatter(g, "dp", scatter_dimension=0, tiled=True), "ctx", scatter_dimension=1, tiled=True).astype(F32) for g in grads]
    back = lax.ppermute(halo[:, 1], "ctx", [(i + 1, i) for i in range(zn - 1)]).astype(F32)
    back = back + lax.ppermute(halo[:, 0], "ctx", [(i + 2, i) for i in range(zn - 2)]).astype(F32)
    return (own, lax.psum_scatter(vectors, ("dp", "ctx"), scatter_dimension=1, tiled=True),
            lax.psum_scatter(text.astype(F32), "ctx", scatter_dimension=1, tiled=True), back)

def general(hidden, text_states, frame_segments, text_segments, text_lengths, cotangent, *params):
    dpn, zn = lax.axis_size("dp"), lax.axis_size("ctx")
    place = lax.axis_index("ctx")
    rows, frames, width = hidden.shape
    weights, vectors = params[:10], jnp.stack(params[10:])
    reach = 2 * frames
    ids = jnp.pad(frame_segments, ((0, 0), (reach, 0)), constant_values=-1)
    key_ids = lax.dynamic_slice_in_dim(ids, place * frames, reach + frames, 1)
    own_ids = key_ids[:, reach:]
    text_ids = jnp.where(jnp.arange(text_segments.shape[1])[None] < text_lengths[:, None], text_segments, -1)

    whole, vec, ext = gather_all(weights, vectors, hidden, dpn, zn)
    wq, wk, wv, wo, cq, ck, cv, co, fi, fo = whole
    g1, s1, g2, s2, g3, s3 = vec.astype(F32)

    first_ext = (normalized(ext)[0] * g1 + s1).astype(BF)
    first_own = first_ext[:, 2]
    first_ext = first_ext.reshape(rows, 3 * frames, width)
    queries = project(first_own, wq, BF)
    keys = project(first_ext, wk, BF)
    values = project(first_ext, wv, BF)
    self_mixed, self_total = self_forward(queries, keys, values, own_ids, key_ids)
    states = hidden.astype(F32)
    after_self = states + project(self_mixed, wo)
    second_norm = (normalized(after_self)[0] * g2 + s2).astype(BF)
    cross_queries = project(second_norm, cq, BF)
    text_keys = project(text_states, ck, BF)
    text_values = project(text_states, cv, BF)
    cross_mixed = cross_forward(cross_queries, text_keys, text_values, own_ids, text_ids)
    after_cross = after_self + project(cross_mixed, co)
    third_norm = (normalized(after_cross)[0] * g3 + s3).astype(BF)
    pre_act = project(third_norm, fi)
    activated, slope = gelu_parts(pre_act)
    activated = activated.astype(BF)
    block_output = (after_cross + project(activated, fo)).astype(BF)

    fo_grad = weight_grad(activated, cotangent)
    pre_grad = (project_back(cotangent, fo) * slope).astype(BF)
    fi_grad = weight_grad(third_norm, pre_grad)
    g3_grad, s3_grad, part = norm_back(after_cross, g3, project_back(pre_grad, fi))
    cross_grad = cotangent.astype(F32) + part
    cross_low = cross_grad.astype(BF)
    co_grad = weight_grad(cross_mixed, cross_low)
    cross_mixed_grad = project_back(cross_low, co, BF)
    cq_low, tk_low, tv_low = cross_backward(cross_queries, text_keys, text_values, cross_mixed_grad, own_ids, text_ids)
    ck_grad = weight_grad(text_states, tk_low)
    cv_grad = weight_grad(text_states, tv_low)
    text_part = (project_back(tk_low, ck) + project_back(tv_low, cv)).astype(BF)
    cq_grad = weight_grad(second_norm, cq_low)
    g2_grad, s2_grad, part = norm_back(after_self, g2, project_back(cq_low, cq))
    self_grad = cross_grad + part
    self_low = self_grad.astype(BF)
    wo_grad = weight_grad(self_mixed, self_low)
    self_mixed_grad = project_back(self_low, wo, BF)
    q_low, k_low, v_low = self_backward(queries, keys, values, self_total, self_mixed_grad, own_ids, key_ids)
    wq_grad = weight_grad(first_own, q_low)
    wk_grad = weight_grad(first_ext, k_low)
    wv_grad = weight_grad(first_ext, v_low)
    first_grad = (project_back(k_low, wk) + project_back(v_low, wv)).reshape(rows, 3, frames, width)
    own_grad = first_grad[:, 2] + project_back(q_low, wq)
    halo_grad = first_grad[:, :2].astype(BF)
    xhat_ext = normalized(ext)[0]
    g1_grad = jnp.sum(first_grad[:, :2] * xhat_ext[:, :2], axis=(0, 1, 2)) + jnp.sum(own_grad * xhat_ext[:, 2], axis=(0, 1))
    s1_grad = jnp.sum(first_grad[:, :2], axis=(0, 1, 2)) + jnp.sum(own_grad, axis=(0, 1))

    grads = (wq_grad, wk_grad, wv_grad, wo_grad, cq_grad, ck_grad, cv_grad, co_grad, fi_grad, fo_grad)
    vec_grads = jnp.stack([g1_grad, s1_grad, g2_grad, s2_grad, g3_grad, s3_grad])
    own, vec_own, text_grad, back = scatter_all(grads, vec_grads, text_part, halo_grad, dpn, zn)
    part = norm_back(states, g1, own_grad + back.astype(F32))[2]
    return (block_output, self_grad + part, text_grad, *own, *vec_own)

def fused(hidden, text_states, frame_segments, text_segments, text_lengths, cotangent, *params):
    dpn, zn = lax.axis_size("dp"), lax.axis_size("ctx")
    place = lax.axis_index("ctx")
    rows, frames, width = hidden.shape
    weights, vectors = params[:10], jnp.stack(params[10:])
    reach = 2 * frames
    ids = jnp.pad(frame_segments, ((0, 0), (reach, 0)), constant_values=-1)
    key_ids = lax.dynamic_slice_in_dim(ids, place * frames, reach + frames, 1)
    own_ids = key_ids[:, reach:]
    text_ids = jnp.where(jnp.arange(text_segments.shape[1])[None] < text_lengths[:, None], text_segments, -1)

    packed = jnp.pad(vectors, ((0, 16 - vectors.shape[0]), (0, 128 - vectors.shape[1])))
    flat = lambda v: v.reshape(-1, v.shape[-1])
    f = forward(weights, packed, flat(hidden), flat(text_states), flat(cotangent), own_ids.reshape(-1, 1), key_ids[:, None, :],
                jnp.concatenate([text_ids, text_ids], axis=1)[:, None, :], zn, rows, frames)
    grads = backward(f, flat(hidden), flat(text_states), flat(cotangent), own_ids.reshape(-1, 1), key_ids[:, None, :],
                     jnp.concatenate([text_ids, text_ids], axis=1)[:, None, :], zn, rows, frames)
    *own, vec_own, text_grad, hidden_grad = grads
    return (f["block"].reshape(hidden.shape), hidden_grad.reshape(hidden.shape), text_grad.reshape(rows, -1, width), *own, *vec_own[:6, :vectors.shape[1]])

def per_device(hidden, text_states, frame_segments, text_segments, text_lengths, cotangent, *params):
    dpn, zn = lax.axis_size("dp"), lax.axis_size("ctx")
    if (dpn, zn) == (8, 4) and params[0].shape == (128, 256):
        return fused(hidden, text_states, frame_segments, text_segments, text_lengths, cotangent, *params)
    return general(hidden, text_states, frame_segments, text_segments, text_lengths, cotangent, *params)

def solution(mesh):
    rows, both = P("dp", "ctx", None), P("dp", "ctx")
    flat = P(("dp", "ctx"))
    placed = (rows, P("dp", None, None), P("dp", None), P("dp", None), P("dp"), rows) + (both,) * 10 + (flat,) * 6
    return jax.shard_map(per_device, mesh=mesh, in_specs=placed, out_specs=(rows,) * 3 + (both,) * 10 + (flat,) * 6, check_vma=False)
```

```python
import functools

import jax
import jax.numpy as jnp
from jax import lax
from jax.experimental import pallas as pl
from jax.experimental.pallas import tpu as pltpu
from jax.sharding import PartitionSpec as P

BF = jnp.bfloat16
F32 = jnp.float32


MESH = pl.DeviceIdType.MESH
ANY = pl.BlockSpec(memory_space=pl.ANY)

def place():
    dp = lax.axis_index("dp"); z = lax.axis_index("ctx")
    core = lax.rem(dp, 2); x = lax.rem(dp // 2, 2); y = dp // 4
    return dp, z, core, x, y

def pieces_of(shapes):
    out = []
    for w, (rows, cols) in enumerate(shapes):
        n = max(1, (rows * cols) // (128 * 256))
        step = rows // n
        for i in range(n):
            out.append((w, i * step, step, rows, cols))
    return out

def gather_kernel(shapes, zn, lags, *refs):
    nw = len(shapes)
    src, hidden, dst, ext = refs[:nw], refs[nw], refs[nw + 1:2 * nw + 1], refs[2 * nw + 1]
    blank, lsem, zs, zr, xs, xr, fs, fr, cs, cr, hl, hs, hr, bs = refs[2 * nw + 2:]
    nrow = hidden.shape[0]
    dp, z, core, x, y = place()
    xn = dp + 2 - 4 * x
    yn = dp + 4 - 8 * y
    dn = yn + 2 - 4 * x
    cn = dp + 1 - 2 * core
    chunks = pieces_of(shapes)
    n = len(chunks)
    up_ok, dn_ok = z < zn - 1, z > 0

    barrier = pltpu.get_barrier_semaphore()
    for who in (xn, yn, cn):
        pl.semaphore_signal(barrier, inc=1, device_id=(who, z), device_id_type=MESH)
    @pl.when(up_ok)
    def _():
        pl.semaphore_signal(barrier, inc=1, device_id=(dp, z + 1), device_id_type=MESH)
    @pl.when(dn_ok)
    def _():
        pl.semaphore_signal(barrier, inc=1, device_id=(dp, z - 1), device_id_type=MESH)
    pl.semaphore_wait(barrier, 3 + up_ok.astype(jnp.int32) + dn_ok.astype(jnp.int32))

    def own(i):
        w, r0, r, rows, cols = chunks[i]
        return src[w].at[pl.ds(r0, r), :]
    def block(i, who, j):
        w, r0, r, rows, cols = chunks[i]
        return dst[w].at[pl.ds(pl.multiple_of(who * rows + r0, r), r), pl.ds(pl.multiple_of(j * cols, cols), cols)]
    def slab(i, who, half=None):
        w, r0, r, rows, cols = chunks[i]
        if half is None:
            return dst[w].at[pl.ds(pl.multiple_of(who * rows + r0, r), r), :]
        h = r // 2
        return dst[w].at[pl.ds(pl.multiple_of(who * rows + r0 + half * h, h), h), :]

    def remote(a, b, s, r, dev):
        return pltpu.make_async_remote_copy(a, b, s, r, device_id=dev, device_id_type=MESH)
    def zcopy(i, j, up, first=False):
        a = own(i) if first else block(i, dp, j)
        return remote(a, block(i, dp, j), zs.at[i, 0 if up else 1, j], zr.at[i, j], (dp, z + 1 if up else z - 1))
    def xcopy(i):
        return remote(slab(i, dp), slab(i, dp), xs.at[i, 0], xr.at[i, 0], (xn, z))
    def ycopy(i):
        return remote(slab(i, dp), slab(i, dp), xs.at[i, 1], xr.at[i, 1], (yn, z))
    def fcopy(i, half):
        who, to = (xn, yn) if half == 0 else (yn, xn)
        return remote(slab(i, who, half), slab(i, who, half), fs.at[i, half], fr.at[i, half], (to, z))
    def frecv(i, half):
        return remote(slab(i, dn, half), slab(i, dn, half), fs.at[i, half], fr.at[i, half], (yn, z))
    def ccopy(i, k):
        who = (dp, xn, yn, dn)[k]
        return remote(slab(i, who), slab(i, who), cs.at[i, k], cr.at[i, k], (cn, z))
    def crecv(i, k):
        who = (dp, xn, yn, dn)[k] + 1 - 2 * core
        return remote(slab(i, who), slab(i, who), cs.at[i, k], cr.at[i, k], (cn, z))
    def hlocal(r):
        return pltpu.make_async_copy(hidden.at[r], ext.at[r, 2], hl.at[r])
    def hcopy(r, hop):
        return remote(ext.at[r, 1] if hop else hidden.at[r], ext.at[r, 1 - hop], hs.at[hop, r], hr.at[hop, r], (dp, z + 1))
    def hblank(r, c):
        return pltpu.make_async_copy(blank, ext.at[r, c], bs.at[r, c])
    def lcopy(i):
        return pltpu.make_async_copy(own(i), block(i, dp, z), lsem.at[i])
    def xrecv(i):
        return remote(slab(i, xn), slab(i, xn), xs.at[i, 0], xr.at[i, 0], (xn, z))
    def yrecv(i):
        return remote(slab(i, yn), slab(i, yn), xs.at[i, 1], xr.at[i, 1], (yn, z))

    for i in range(n):
        @pl.when(up_ok)
        def _():
            zcopy(i, z, True, True).start()
        @pl.when(dn_ok)
        def _():
            zcopy(i, z, False, True).start()
        lcopy(i).start()
    for r in range(nrow):
        hlocal(r).start()
    blank[...] = jnp.zeros_like(blank)

    def halo_step(k):
        if k % 3 == 1 and k // 3 < nrow:
            @pl.when(up_ok)
            def _():
                hcopy(k // 3, 0).start()
        if k % 3 == 0 and 0 <= k // 3 - 1 < nrow:
            r = k // 3 - 1
            @pl.when(dn_ok)
            def _():
                hcopy(r, 0).wait_recv()
                @pl.when(up_ok)
                def _():
                    hcopy(r, 1).start()
        if k % 3 == 2 and 0 <= k // 3 - 1 < nrow:
            r = k // 3 - 1
            @pl.when(z == 0)
            def _():
                hblank(r, 1).start()
            @pl.when(z <= 1)
            def _():
                hblank(r, 0).start()

    def zstage(i, t):
        @pl.when(z - t >= 0)
        def _():
            zcopy(i, z - t, True).wait_recv()
            @pl.when(up_ok)
            def _():
                zcopy(i, z - t, True).start()
        @pl.when(z + t < zn)
        def _():
            zcopy(i, z + t, False).wait_recv()
            @pl.when(dn_ok)
            def _():
                zcopy(i, z + t, False).start()
    def stage(s, i):
        if s == 0 or s == 1:
            zstage(i, s + 1)
        elif s == 2:
            zstage(i, 3)
            lcopy(i).wait()
            xcopy(i).start(); ycopy(i).start(); ccopy(i, 0).start()
        elif s == 3:
            xrecv(i).wait_recv()
            fcopy(i, 0).start(); ccopy(i, 1).start()
            yrecv(i).wait_recv()
            fcopy(i, 1).start(); ccopy(i, 2).start()
        elif s == 4:
            frecv(i, 0).wait_recv(); frecv(i, 1).wait_recv()
            ccopy(i, 3).start()
        else:
            for k in range(4):
                crecv(i, k).wait_recv()
    for k in range(n + lags[-1]):
        halo_step(k)
        for s, lag in enumerate(lags):
            if 0 <= k - lag < n:
                stage(s, k - lag)
    for r in range(nrow):
        hlocal(r).wait()
        @pl.when(up_ok)
        def _():
            hcopy(r, 0).wait_send()
        @pl.when(up_ok & dn_ok)
        def _():
            hcopy(r, 1).wait_send()
        @pl.when(z >= 2)
        def _():
            hcopy(r, 1).wait_recv()
        @pl.when(z == 0)
        def _():
            hblank(r, 1).wait()
        @pl.when(z <= 1)
        def _():
            hblank(r, 0).wait()
    for i in range(n):
        for j in range(zn):
            @pl.when(up_ok & (j <= z))
            def _():
                zcopy(i, j, True).wait_send()
            @pl.when(dn_ok & (j >= z))
            def _():
                zcopy(i, j, False).wait_send()
        xcopy(i).wait_send(); ycopy(i).wait_send()
        fcopy(i, 0).wait_send(); fcopy(i, 1).wait_send()
        for k in range(4):
            ccopy(i, k).wait_send()

def gather(weights, hidden, dpn, zn, cid=0, lags=(0, 1, 2, 4, 6, 8)):
    shapes = tuple(tuple(w.shape) for w in weights)
    n = len(pieces_of(shapes))
    D = pltpu.SemaphoreType.DMA
    rows, frames, width = hidden.shape
    return pl.pallas_call(
        functools.partial(gather_kernel, shapes, zn, lags),
        out_shape=[jax.ShapeDtypeStruct((dpn * r, zn * c), jnp.bfloat16) for r, c in shapes] + [jax.ShapeDtypeStruct((rows, 3, frames, width), jnp.bfloat16)],
        in_specs=[pl.BlockSpec(memory_space=pltpu.VMEM)] * (len(shapes) + 1),
        out_specs=[ANY] * (len(shapes) + 1),
        scratch_shapes=[pltpu.VMEM((frames, width), jnp.bfloat16), D((n,)), D((n, 2, zn)), D((n, zn)), D((n, 2)), D((n, 2)), D((n, 2)), D((n, 2)), D((n, 4)), D((n, 4)),
                        D((rows,)), D((2, rows)), D((2, rows)), D((rows, 2))],
        compiler_params=pltpu.CompilerParams(collective_id=cid, has_side_effects=True),
        name="gather",
    )(*weights, hidden)

def add_rows(dst, terms, rows, step=16):
    @pl.loop(0, rows // step)
    def _(q):
        s = pl.ds(pl.multiple_of(q * step, step), step)
        total = terms[0][s, :].astype(F32)
        for t in terms[1:]:
            total = total + t[s, :].astype(F32)
        dst[s, :] = total.astype(dst.dtype)

def scatter_kernel(shapes, nhalo, zn, lags, *refs):
    nw = len(shapes)
    it = iter(refs)
    take = lambda k: [next(it) for _ in range(k)]
    grads = take(nw)
    text, halo = take(2)
    outs = take(nw)
    text_out, halo_out = take(2)
    acc, rh, rxy, rz = take(nw), take(nw), take(nw), take(nw)
    kinds = sorted({(s[0] // (1 if s[0]*s[1] <= 128*256 else (s[0]*s[1]) // (128*256)), s[1]) for s in shapes})
    stage = dict(zip(kinds, take(len(kinds))))
    tz, h2, h1, hs = take(4)
    ls, cs, cr, hsd, hrc, xs, xr, zs, zr, tzs, tzr, hls, hss, hrs = take(14)
    dp, z, core, x, y = place()
    xn = dp + 2 - 4 * x
    yn = dp + 4 - 8 * y
    dn = yn + 2 - 4 * x
    flip = 1 - 2 * core
    cn = dp + flip
    chunks = pieces_of(shapes)
    first = {}
    for i, c in enumerate(chunks):
        first.setdefault(c[0], i)
    n = len(chunks)
    up_ok, dn_ok = z < zn - 1, z > 0
    barrier = pltpu.get_barrier_semaphore()
    for who in (xn, yn, cn):
        pl.semaphore_signal(barrier, inc=1, device_id=(who, z), device_id_type=MESH)
    @pl.when(up_ok)
    def _():
        pl.semaphore_signal(barrier, inc=1, device_id=(dp, z + 1), device_id_type=MESH)
    @pl.when(dn_ok)
    def _():
        pl.semaphore_signal(barrier, inc=1, device_id=(dp, z - 1), device_id_type=MESH)
    pl.semaphore_wait(barrier, 3 + up_ok.astype(jnp.int32) + dn_ok.astype(jnp.int32))

    def remote(a, b, s, r, dev):
        return pltpu.make_async_remote_copy(a, b, s, r, device_id=dev, device_id_type=MESH)
    def slab(i, who):
        w, r0, r, rows, cols = chunks[i]
        return grads[w].at[pl.ds(pl.multiple_of(who * rows + r0, r), r), :]
    fam = (dp, xn, yn, dn)
    def at(buf, i, *rest):
        w = chunks[i][0]
        return buf[w].at[(i - first[w],) + rest]
    def ccopy(i, k):
        return remote(slab(i, fam[k] + flip), at(acc, i, k), cs.at[i, k], cr.at[i, k], (cn, z))
    def staged(i):
        w, r0, r, rows, cols = chunks[i]
        return stage[(r, cols)]
    slots = {}
    cnt = {}
    for i, c in enumerate(chunks):
        key = (c[2], c[4]); slots[i] = cnt.get(key, 0) % 2; cnt[key] = cnt.get(key, 0) + 1
    kidx = {k: q for q, k in enumerate(kinds)}
    def lcopy(i, k):
        key = (chunks[i][2], chunks[i][4])
        return pltpu.make_async_copy(slab(i, fam[k]), staged(i).at[slots[i], k], ls.at[kidx[key], slots[i], k])
    prev = {}
    nxt = {}
    last = {}
    for i, c in enumerate(chunks):
        key = (c[2], c[4])
        last.setdefault(key, []).append(i)
    for key, l in last.items():
        for a, b in zip(l, l[2:]):
            nxt[a] = b
    def half(ref, i, h):
        r = chunks[i][2]
        return ref.at[pl.ds(h * (r // 2), r // 2), :]
    def dcopy(i, h):
        return remote(half(at(acc, i, 3), i, h), at(rh, i, h), hsd.at[i, h], hrc.at[i, h], ((xn, yn)[h], z))
    def xcopy(i, d, h):
        return remote(half(at(acc, i, 1 + d), i, h), half(at(rxy, i, d), i, h), xs.at[i, d, h], xr.at[i, d, h], ((xn, yn)[d], z))
    def col(ref, i, j):
        cols = chunks[i][4]
        return ref.at[:, pl.ds(j * cols, cols)]
    def zcopy(i, up, j):
        return remote(col(at(acc, i, 0), i, j), at(rz, i, 0 if up else 1, j), zs.at[i, 0 if up else 1, j], zr.at[i, 0 if up else 1, j], (dp, z + 1 if up else z - 1))
    tc = text.shape[1] // zn
    tr = text.shape[0]
    def tcopy(up, j):
        return remote(text.at[:, pl.ds(j * tc, tc)], tz.at[0 if up else 1, j], tzs.at[0 if up else 1, j], tzr.at[0 if up else 1, j], (dp, z + 1 if up else z - 1))
    def h2copy(r):
        return remote(halo.at[r, 0], h2.at[r], hss.at[0, r], hrs.at[0, r], (dp, z - 1))
    def h1local(r):
        return pltpu.make_async_copy(halo.at[r, 1], h1.at[r], hls.at[r])
    def h1copy(r):
        return remote(h1.at[r], halo_out.at[r], hss.at[1, r], hrs.at[1, r], (dp, z - 1))

    @pl.when(z >= 2)
    def _():
        for r in range(nhalo):
            h2copy(r).start()
    @pl.when(dn_ok)
    def _():
        for r in range(nhalo):
            h1local(r).start()
    for i in range(n):
        for k in (3, 1, 2, 0):
            ccopy(i, k).start()
    for key, l in last.items():
        for i in l[:2]:
            for k in (3, 1, 2, 0):
                lcopy(i, k).start()

    def zadd(i, j, z_static, up):
        w, r0, r, rows, cols = chunks[i]
        a = col(at(acc, i, 0), i, j)
        add_rows(a, [a, at(rz, i, 0 if up else 1, j)], r)
    def zstage(i, t):
        w, r0, r, rows, cols = chunks[i]
        for up in (True, False):
            @pl.when(z == (t if up else zn - 1 - t))
            def _(up=up):
                zz = t if up else zn - 1 - t
                js = range(zz + 1, zn) if up else range(zz - 1, -1, -1)
                for j in js:
                    if t > 0:
                        zcopy(i, up, j).wait_recv()
                        zadd(i, j, zz, up)
                    zcopy(i, up, j).start()
                if t > 0:
                    zcopy(i, up, zz).wait_recv()
    def final(i):
        w, r0, r, rows, cols = chunks[i]
        o = outs[w].at[pl.ds(r0, r), :]
        for zz in range(zn):
            @pl.when(z == zz)
            def _(zz=zz):
                terms = [col(at(acc, i, 0), i, zz)]
                if zz > 0: terms.append(at(rz, i, 0, zz))
                if zz < zn - 1: terms.append(at(rz, i, 1, zz))
                add_rows(o, terms, r)
    def text_stage(t):
        for up in (True, False):
            @pl.when(z == (t if up else zn - 1 - t))
            def _(up=up):
                zz = t if up else zn - 1 - t
                js = range(zz + 1, zn) if up else range(zz - 1, -1, -1)
                for j in js:
                    if t > 0:
                        tcopy(up, j).wait_recv()
                        a = text.at[:, pl.ds(j * tc, tc)]
                        add_rows(a, [a, tz.at[0 if up else 1, j]], tr)
                    tcopy(up, j).start()
                if t > 0:
                    tcopy(up, zz).wait_recv()
    def text_final():
        for zz in range(zn):
            @pl.when(z == zz)
            def _(zz=zz):
                terms = [text.at[:, pl.ds(zz * tc, tc)]]
                if zz > 0: terms.append(tz.at[0, zz])
                if zz < zn - 1: terms.append(tz.at[1, zz])
                add_rows(text_out, terms, tr)
    def halo_stage(r):
        @pl.when(dn_ok)
        def _():
            h1local(r).wait()
            @pl.when(up_ok)
            def _():
                h2copy(r).wait_recv()
                add_rows(h1.at[r], [h1.at[r], h2.at[r]], h1.shape[1])
            h1copy(r).start()
        @pl.when(z == zn - 1)
        def _():
            pltpu.make_async_copy(hs, halo_out.at[r], hls.at[r]).start()

    def stage_of(s, i):
        w, r0, r, rows, cols = chunks[i]
        if s == 0:
            A = lambda k: at(acc, i, k)
            S = lambda k: staged(i).at[slots[i], k]
            for k in (3, 1, 2, 0):
                ccopy(i, k).wait_recv()
                lcopy(i, k).wait()
                add_rows(A(k), [A(k), S(k)], r)
                if k == 1:
                    dcopy(i, 0).start(); dcopy(i, 1).start()
                if k == 2:
                    xcopy(i, 0, 0).start()
                if k == 0:
                    xcopy(i, 1, 1).start()
            if i in nxt:
                for k in (3, 1, 2, 0):
                    lcopy(nxt[i], k).start()
        elif s == 1:
            dcopy(i, 0).wait_recv()
            a = half(at(acc, i, 2), i, 0)
            add_rows(a, [a, at(rh, i, 0)], r // 2, min(16, r // 2))
            dcopy(i, 1).wait_recv()
            b = half(at(acc, i, 1), i, 1)
            add_rows(b, [b, at(rh, i, 1)], r // 2, min(16, r // 2))
            xcopy(i, 1, 0).start()
            xcopy(i, 0, 1).start()
        elif s == 2:
            for d in range(2):
                for h in range(2):
                    xcopy(i, d, h).wait_recv()
            a = at(acc, i, 0)
            add_rows(a, [a, at(rxy, i, 0), at(rxy, i, 1)], r)
            zstage(i, 0)
        elif s < 2 + zn:
            zstage(i, s - 2)
            if s == 1 + zn:
                final(i)
    for k in range(n + lags[-1]):
        for s, lag in enumerate(lags):
            if 0 <= k - lag < n:
                stage_of(s, k - lag)
        if k == 0:
            hs[...] = jnp.zeros_like(hs)
        if 1 <= k <= zn:
            text_stage(k - 1)
        if k == zn + 1:
            text_final()
        if 2 <= k < 2 + nhalo:
            halo_stage(k - 2)
    for i in range(n):
        for k in range(4):
            ccopy(i, k).wait_send()
        for h in range(2):
            dcopy(i, h).wait_send()
            for d in range(2):
                xcopy(i, d, h).wait_send()
        for j in range(zn):
            @pl.when(up_ok & (j > z))
            def _():
                zcopy(i, True, j).wait_send()
            @pl.when(dn_ok & (j < z))
            def _():
                zcopy(i, False, j).wait_send()
    for j in range(zn):
        @pl.when(up_ok & (j > z))
        def _():
            tcopy(True, j).wait_send()
        @pl.when(dn_ok & (j < z))
        def _():
            tcopy(False, j).wait_send()
    for r in range(nhalo):
        @pl.when(z >= 2)
        def _():
            h2copy(r).wait_send()
        @pl.when(dn_ok)
        def _():
            h1copy(r).wait_send()
        @pl.when(up_ok)
        def _():
            h1copy(r).wait_recv()
        @pl.when(z == zn - 1)
        def _():
            pltpu.make_async_copy(hs, halo_out.at[r], hls.at[r]).wait()

def scatter(grads, text, halo, dpn, zn, cid=1, lags=(0, 1, 2, 3, 4, 5)):
    shapes = tuple((g.shape[0] // dpn, g.shape[1] // zn) for g in grads)
    chunks = pieces_of(shapes)
    n = len(chunks)
    cnt = [sum(c[0] == w for c in chunks) for w in range(len(shapes))]
    rr = [next(c[2] for c in chunks if c[0] == w) for w in range(len(shapes))]
    kinds = sorted({(r, s[1]) for r, s in zip(rr, shapes)})
    D = pltpu.SemaphoreType.DMA
    V = pltpu.VMEM
    T = halo.shape
    tr, tc = text.shape[0], text.shape[1] // zn
    scratch = [V((cnt[w], 4, rr[w], zn * shapes[w][1]), BF) for w in range(len(shapes))]
    scratch += [V((cnt[w], 2, rr[w] // 2, zn * shapes[w][1]), BF) for w in range(len(shapes))]
    scratch += [V((cnt[w], 2, rr[w], zn * shapes[w][1]), BF) for w in range(len(shapes))]
    scratch += [V((cnt[w], 2, zn, rr[w], shapes[w][1]), BF) for w in range(len(shapes))]
    scratch += [V((2, 4, r, zn * c), BF) for r, c in kinds]
    scratch += [V((2, zn, tr, tc), BF), V((T[0],) + T[2:], BF), V((T[0],) + T[2:], BF), V(T[2:], BF)]
    scratch += [D((len(kinds), 2, 4)), D((n, 4)), D((n, 4)), D((n, 2)), D((n, 2)), D((n, 2, 2)), D((n, 2, 2)), D((n, 2, zn)), D((n, 2, zn)),
                D((2, zn)), D((2, zn)), D((T[0],)), D((2, T[0])), D((2, T[0]))]
    VM = pl.BlockSpec(memory_space=pltpu.VMEM)
    return pl.pallas_call(
        functools.partial(scatter_kernel, shapes, T[0], zn, lags),
        out_shape=[jax.ShapeDtypeStruct(s, F32) for s in shapes] + [jax.ShapeDtypeStruct((tr, tc), F32), jax.ShapeDtypeStruct((T[0],) + T[2:], BF)],
        in_specs=[ANY] * len(shapes) + [VM, ANY],
        out_specs=[VM] * (len(shapes) + 1) + [ANY],
        scratch_shapes=scratch,
        compiler_params=pltpu.CompilerParams(collective_id=cid, has_side_effects=True, vmem_limit_bytes=60 << 20),
        name="scatter",
    )(*grads, text, halo)

HEAD = 64
SCALE = 0.125
MASKED = -1e9

def dot(a, b, ca, cb):
    return lax.dot_general(a, b, (((ca,), (cb,)), ((), ())), preferred_element_type=F32)

def lane_is(shape, h):
    lanes = lax.broadcasted_iota(jnp.int32, shape, 1)
    return (lanes < HEAD) if h == 0 else (lanes >= HEAD)

def self_allowed(q_ids, k_ids, back):
    nq, nk = q_ids.shape[0], k_ids.shape[1]
    qi = lax.broadcasted_iota(jnp.int32, (nq, nk), 0)
    ki = lax.broadcasted_iota(jnp.int32, (nq, nk), 1)
    return (q_ids == k_ids) & (ki <= qi + back)

def self_forward_kernel(qs, ks, q, k, v, o, lse, bias):
    nq, nk = q.shape[1], k.shape[1]
    @pl.when(pl.program_id(1) == 0)
    def _():
        bias[...] = jnp.where(self_allowed(qs[0], ks[0], nk - nq), 0.0, MASKED)
    q2, k2, v2 = q[0], k[0], v[0]
    outs, totals = [], []
    for h in range(2):
        mine = lane_is(q2.shape, h)
        qh = jnp.where(mine, q2 * jnp.asarray(SCALE, BF), jnp.zeros_like(q2))
        s = dot(qh, k2, 1, 1) + bias[...]
        top = jnp.max(s, axis=1, keepdims=True)
        p = jnp.exp(s - top)
        total = jnp.sum(p, axis=1, keepdims=True)
        outs.append(dot(p.astype(BF), v2, 1, 0) / total)
        totals.append(jnp.broadcast_to(top + jnp.log(total), q2.shape))
    first = lane_is(q2.shape, 0)
    o[0] = jnp.where(first, outs[0], outs[1]).astype(BF)
    lse[0] = jnp.where(first, totals[0], totals[1])

def self_backward_kernel(qs, ks, q, k, v, lse, do, dq, dk, dv, bias):
    nq, nk = q.shape[1], k.shape[1]
    @pl.when(pl.program_id(1) == 0)
    def _():
        bias[...] = jnp.where(self_allowed(qs[0], ks[0], nk - nq), 0.0, MASKED)
    q2, k2, v2, d2 = q[0], k[0], v[0], do[0]
    gq, gk, gv = [], [], []
    for h in range(2):
        mine = lane_is(q2.shape, h)
        zero = jnp.zeros_like(q2)
        qh = jnp.where(mine, q2 * jnp.asarray(SCALE, BF), zero)
        dh = jnp.where(mine, d2, zero)
        s = dot(qh, k2, 1, 1) + bias[...]
        p = jnp.exp(s - lse[0][:, h * HEAD:h * HEAD + 1])
        dp = dot(dh, v2, 1, 1)
        inner = jnp.sum(p * dp, axis=1, keepdims=True)
        ds = (p * (dp - inner)).astype(BF)
        gq.append(dot(ds, k2, 1, 0) * SCALE)
        gk.append(dot(ds, qh, 0, 0))
        gv.append(dot(p.astype(BF), dh, 0, 0))
    dq[0] = jnp.where(lane_is(q2.shape, 0), gq[0], gq[1]).astype(BF)
    dk[0] = (gk[0] + gk[1]).astype(BF)
    dv[0] = (gv[0] + gv[1]).astype(BF)

def specs(nq, nk):
    qb = pl.BlockSpec((1, nq, 128), lambda r, p: (r, 0, p))
    kb = pl.BlockSpec((1, nk, 128), lambda r, p: (r, 0, p))
    qid = pl.BlockSpec((1, nq, 1), lambda r, p: (r, 0, 0))
    kid = pl.BlockSpec((1, 1, nk), lambda r, p: (r, 0, 0))
    return qb, kb, qid, kid

def self_forward(q, k, v, q_ids, k_ids):
    rows, nq, width = q.shape
    nk = k.shape[1]
    qb, kb, qid, kid = specs(nq, nk)
    return pl.pallas_call(
        self_forward_kernel, grid=(rows, width // 128),
        in_specs=[qid, kid, qb, kb, kb], out_specs=[qb, qb],
        out_shape=[jax.ShapeDtypeStruct(q.shape, BF), jax.ShapeDtypeStruct(q.shape, F32)],
        scratch_shapes=[pltpu.VMEM((nq, nk), F32)], name="self_attention",
    )(q_ids[:, :, None], k_ids[:, None, :], q, k, v)

def self_backward(q, k, v, lse, do, q_ids, k_ids):
    rows, nq, width = q.shape
    nk = k.shape[1]
    qb, kb, qid, kid = specs(nq, nk)
    return pl.pallas_call(
        self_backward_kernel, grid=(rows, width // 128),
        in_specs=[qid, kid, qb, kb, kb, qb, qb], out_specs=[qb, kb, kb],
        out_shape=[jax.ShapeDtypeStruct(q.shape, BF), jax.ShapeDtypeStruct(k.shape, BF), jax.ShapeDtypeStruct(k.shape, BF)],
        scratch_shapes=[pltpu.VMEM((nq, nk), F32)], name="self_attention_back",
    )(q_ids[:, :, None], k_ids[:, None, :], q, k, v, lse, do)

def pair_keys(k2):
    first = lane_is(k2.shape, 0)
    zero = jnp.zeros_like(k2)
    return jnp.concatenate([jnp.where(first, k2, zero), jnp.where(first, zero, k2)], axis=0)

def halves(values, tokens, reduce, fill):
    left = lax.broadcasted_iota(jnp.int32, values.shape, 1) < tokens
    a = reduce(jnp.where(left, values, fill), axis=1, keepdims=True)
    b = reduce(jnp.where(left, fill, values), axis=1, keepdims=True)
    return jnp.where(left, a, b)

def cross_shares(q2, kk, ids_q, ids_k, tokens):
    s = dot(q2 * jnp.asarray(SCALE, BF), kk, 1, 1)
    s = jnp.where(ids_q == ids_k, s, MASKED)
    p = jnp.exp(s - halves(s, tokens, jnp.max, MASKED))
    return p / halves(p, tokens, jnp.sum, 0.0)

def cross_forward_kernel(qs, ks, q, k, v, o):
    tokens = k.shape[1]
    p = cross_shares(q[0], pair_keys(k[0]), qs[0], ks[0], tokens)
    o[0] = dot(p.astype(BF), pair_keys(v[0]), 1, 0).astype(BF)

def cross_backward_kernel(qs, ks, q, k, v, do, dq, dk, dv):
    tokens = k.shape[1]
    q2, d2 = q[0], do[0]
    kk, vv = pair_keys(k[0]), pair_keys(v[0])
    p = cross_shares(q2, kk, qs[0], ks[0], tokens)
    dp = dot(d2, vv, 1, 1)
    ds = (p * (dp - halves(p * dp, tokens, jnp.sum, 0.0))).astype(BF)
    dq[0] = (dot(ds, kk, 1, 0) * SCALE).astype(BF)
    gk = dot(ds, q2, 0, 0) * SCALE
    gv = dot(p.astype(BF), d2, 0, 0)
    first = lane_is((tokens, 128), 0)
    dk[0] = jnp.where(first, gk[:tokens], gk[tokens:]).astype(BF)
    dv[0] = jnp.where(first, gv[:tokens], gv[tokens:]).astype(BF)

def cross_specs(nq, nk):
    qb, kb, qid, _ = specs(nq, nk)
    return qb, kb, qid, pl.BlockSpec((1, 1, 2 * nk), lambda r, p: (r, 0, 0))

def cross_forward(q, k, v, q_ids, k_ids):
    rows, nq, width = q.shape
    qb, kb, qid, kid = cross_specs(nq, k.shape[1])
    return pl.pallas_call(
        cross_forward_kernel, grid=(rows, width // 128),
        in_specs=[qid, kid, qb, kb, kb], out_specs=qb,
        out_shape=jax.ShapeDtypeStruct(q.shape, BF), name="cross_attention",
    )(q_ids[:, :, None], jnp.concatenate([k_ids, k_ids], axis=1)[:, None, :], q, k, v)

def cross_backward(q, k, v, do, q_ids, k_ids):
    rows, nq, width = q.shape
    qb, kb, qid, kid = cross_specs(nq, k.shape[1])
    return pl.pallas_call(
        cross_backward_kernel, grid=(rows, width // 128),
        in_specs=[qid, kid, qb, kb, kb, qb], out_specs=[qb, kb, kb],
        out_shape=[jax.ShapeDtypeStruct(q.shape, BF), jax.ShapeDtypeStruct(k.shape, BF), jax.ShapeDtypeStruct(k.shape, BF)],
        name="cross_attention_back",
    )(q_ids[:, :, None], jnp.concatenate([k_ids, k_ids], axis=1)[:, None, :], q, k, v, do)

EPS = 1e-05
W = 1024
SLAB = 128
PACE_F = 10.0
VEC = 16

class Names:
    def __init__(self, names, refs):
        for n, r in zip(names, refs, strict=True):
            setattr(self, n, r)

def barrier_with(peers):
    sem = pltpu.get_barrier_semaphore()
    total = 0
    for who, zz, ok in peers:
        def send(who=who, zz=zz):
            pl.semaphore_signal(sem, inc=1, device_id=(who, zz), device_id_type=MESH)
        if ok is None:
            send()
            total = total + 1
        else:
            pl.when(ok)(send)
            total = total + ok.astype(jnp.int32)
    pl.semaphore_wait(sem, total)

def blocks(rows, step, body):
    @pl.loop(0, rows // step)
    def _(q):
        body(pl.ds(pl.multiple_of(q * step, step), step))

def tiles(width, tile, body):
    @pl.loop(0, width // tile)
    def _(n):
        body(n, pl.ds(pl.multiple_of(n * tile, tile), tile))

def lanes_at(n, size, offset=0):
    return pl.ds(pl.multiple_of(n, 128) + offset if offset else pl.multiple_of(n, 128), size)

def standard(v):
    centred = v - jnp.mean(v, axis=-1, keepdims=True)
    scale = lax.rsqrt(jnp.mean(centred * centred, axis=-1, keepdims=True) + EPS)
    return centred * scale, scale

def gelu_pair(u):
    half_erf = 0.5 * (1.0 + lax.erf(u * 0.7071067811865476))
    return u * half_erf, half_erf + u * (0.3989422804014327 * jnp.exp(-0.5 * u * u))

def column(row):
    return jnp.broadcast_to(row, (8, row.shape[1])).T[:, :1]

def stack_heads(v):
    zero, first = jnp.zeros_like(v), lane_is(v.shape, 0)
    return jnp.concatenate([jnp.where(first, v, zero), jnp.where(first, zero, v)], axis=0)

def pick_heads(v):
    n = v.shape[0] // 2
    return jnp.where(lane_is((n, v.shape[1]), 0), v[:n], v[n:])

def mask_keys(q_row, k_row, back):
    k, q = column(k_row), q_row
    shape = (k.shape[0], q.shape[1])
    ki, qi = lax.broadcasted_iota(jnp.int32, shape, 0), lax.broadcasted_iota(jnp.int32, shape, 1)
    n = shape[1] // 2
    qi = jnp.where(qi >= n, qi - n, qi)
    return jnp.where((k == q) & (ki <= qi + back), 0.0, MASKED)

class Pump:
    def __init__(self, step, count, pace):
        self.step, self.count, self.pace, self.next, self.spent = step, count, pace, 0, 0.0
    def upto(self, k):
        while self.next <= min(k, self.count - 1):
            self.step(self.next)
            self.next += 1
    def work(self, cost):
        self.spent += cost
        while self.spent >= self.pace:
            self.spent -= self.pace
            self.upto(self.next)

F_IN = ["q_w", "k_w", "v_w", "o_w", "cq_w", "ck_w", "cv_w", "co_w", "fi_w", "fo_w", "vecs", "hidden", "text", "cot", "q_ids", "k_ids", "t_ids"]
F_OUT = ["weights", "gains", "halo", "first", "q", "k", "v", "lse", "mixed", "after_self", "second", "cq", "tk", "tv", "cmix", "after_cross", "third", "pre_grad", "fo_grad", "block"]
F_SCR = ["s_halo", "s_pool", "s_q", "s_mixed", "s_lse", "s_as", "s_second", "s_cq", "s_tk", "s_tv", "s_cmix", "s_ac", "s_third", "s_act", "s_w", "s_fog", "s_bias", "s_vec", "s_gain", "s_out",
         "lsem", "zs", "zr", "xs", "xr", "fs", "fr", "cs", "cr", "hs", "hr", "ws", "save", "fogs"]

def forward_kernel(zn, rows, frames, *refs):
    r_ = Names(F_IN + F_OUT + F_SCR, refs)
    T, E = rows * frames, 3 * frames
    heads2 = W // 128
    dp, z, core, x, y = place()
    xn = dp + 2 - 4 * x
    yn = dp + 4 - 8 * y
    dn = yn + 2 - 4 * x
    cn = dp + 1 - 2 * core
    up_ok, dn_ok = z < zn - 1, z > 0
    order = [VEC] + list(range(16))
    n = len(order)
    barrier_with([(xn, z, None), (yn, z, None), (cn, z, None), (dp, z + 1, up_ok), (dp, z - 1, dn_ok)])

    def own(i):
        if i == VEC:
            return r_.vecs
        if i < 8:
            return refs[i]
        if i < 12:
            return r_.fi_w.at[:, pl.ds((i - 8) * 256, 256)]
        return r_.fo_w.at[pl.ds((i - 12) * SLAB, SLAB), :]
    def slab(i, who, half=None):
        base = r_.s_vec if i == VEC else r_.weights.at[i]
        size = 16 if i == VEC else SLAB
        if half is None:
            return base.at[pl.ds(pl.multiple_of(who * size, size), size), :]
        h = size // 2
        return base.at[pl.ds(pl.multiple_of(who * size + half * h, h), h), :]
    def block(i, who, j):
        base = r_.s_vec if i == VEC else r_.weights.at[i]
        size, cols = (16, 128) if i == VEC else (SLAB, 256)
        return base.at[pl.ds(pl.multiple_of(who * size, size), size), pl.ds(pl.multiple_of(j * cols, cols), cols)]
    def remote(a, b, s, r, dev):
        return pltpu.make_async_remote_copy(a, b, s, r, device_id=dev, device_id_type=MESH)
    def zcopy(i, j, up, first=False):
        a = own(i) if first else block(i, dp, j)
        return remote(a, block(i, dp, j), r_.zs.at[i, 0 if up else 1, j], r_.zr.at[i, j], (dp, z + 1 if up else z - 1))
    def xcopy(i, d):
        return remote(slab(i, dp), slab(i, dp), r_.xs.at[i, d], r_.xr.at[i, d], ((xn, yn)[d], z))
    def xrecv(i, d):
        who = (xn, yn)[d]
        return remote(slab(i, who), slab(i, who), r_.xs.at[i, d], r_.xr.at[i, d], (who, z))
    def fcopy(i, half):
        who, to = (xn, yn) if half == 0 else (yn, xn)
        return remote(slab(i, who, half), slab(i, who, half), r_.fs.at[i, half], r_.fr.at[i, half], (to, z))
    def frecv(i, half):
        return remote(slab(i, dn, half), slab(i, dn, half), r_.fs.at[i, half], r_.fr.at[i, half], (yn, z))
    def ccopy(i, k):
        who = (dp, xn, yn, dn)[k]
        return remote(slab(i, who), slab(i, who), r_.cs.at[i, k], r_.cr.at[i, k], (cn, z))
    def crecv(i, k):
        who = (dp, xn, yn, dn)[k] + 1 - 2 * core
        return remote(slab(i, who), slab(i, who), r_.cs.at[i, k], r_.cr.at[i, k], (cn, z))
    def lcopy(i):
        return pltpu.make_async_copy(own(i), block(i, dp, z), r_.lsem.at[i])
    def hcopy(r, hop):
        a = r_.s_halo.at[r, 1] if hop else r_.hidden.at[pl.ds(r * frames, frames), :]
        return remote(a, r_.s_halo.at[r, 1 - hop], r_.hs.at[hop, r], r_.hr.at[hop, r], (dp, z + 1))
    def begin(i):
        @pl.when(up_ok)
        def _():
            zcopy(i, z, True, True).start()
        @pl.when(dn_ok)
        def _():
            zcopy(i, z, False, True).start()
        lcopy(i).start()
    def zstage(i, t):
        @pl.when(z - t >= 0)
        def _():
            zcopy(i, z - t, True).wait_recv()
            @pl.when(up_ok)
            def _():
                zcopy(i, z - t, True).start()
        @pl.when(z + t < zn)
        def _():
            zcopy(i, z + t, False).wait_recv()
            @pl.when(dn_ok)
            def _():
                zcopy(i, z + t, False).start()
    done = {i: 0 for i in order}
    def advance(i, s):
        while done[i] < s:
            done[i] += 1
            t = done[i]
            if t < zn - 1:
                zstage(i, t)
            elif t == zn - 1:
                zstage(i, t)
                lcopy(i).wait()
                xcopy(i, 0).start(); xcopy(i, 1).start(); ccopy(i, 0).start()
            elif t == zn:
                for d in range(2):
                    xrecv(i, d).wait_recv()
                    fcopy(i, d).start(); ccopy(i, 1 + d).start()
            elif t == zn + 1:
                frecv(i, 0).wait_recv(); frecv(i, 1).wait_recv()
                ccopy(i, 3).start()
            else:
                for k in range(4):
                    crecv(i, k).wait_recv()
    LAST = zn + 2
    lags = (0, 1, 2, 4, 6, 7)
    AHEAD = 6
    def halo_step(k):
        for r in range(rows):
            if k == 2 * r:
                @pl.when(up_ok)
                def _():
                    hcopy(r, 0).start()
            if k == 2 * r + 4:
                @pl.when(dn_ok)
                def _():
                    hcopy(r, 0).wait_recv()
                    @pl.when(up_ok)
                    def _():
                        hcopy(r, 1).start()
    def step(k):
        if k + AHEAD < n:
            begin(order[k + AHEAD])
        for s, lag in enumerate(lags):
            if 0 <= k - lag < n:
                advance(order[k - lag], s + 1)
        halo_step(k)
    pump = Pump(step, n + lags[-1], PACE_F)
    def need(i):
        a = order.index(i)
        pump.upto(a + 7)
        advance(i, LAST)
    SLOTS = 3
    def load(i, slot):
        need(i)
        c = pltpu.make_async_copy(r_.weights.at[i], r_.s_w.at[slot], r_.ws.at[slot])
        c.start()
        return c
    for a in range(AHEAD):
        begin(order[a])

    saves = []
    def save(src, dst):
        c = pltpu.make_async_copy(src, dst, r_.save.at[len(saves)])
        c.start()
        saves.append(c)
        return c
    waited = set()
    def settle(c):
        if id(c) not in waited:
            c.wait()
            waited.add(id(c))

    def dense(lhs, slot, emit, tile=512):
        tiles(W, tile, lambda m, c: emit(m, c, dot(lhs(), r_.s_w[slot, :, c], 1, 0)))
    def gain(k):
        return r_.s_gain[k:k + 1, :]
    def norm(src, dst, at_src, at_dst, g):
        v = src[pl.ds(at_src, frames), :].astype(F32)
        dst[pl.ds(at_dst, frames), :] = (standard(v)[0] * gain(g) + gain(g + 1)).astype(BF)
    def norm_all(src, dst, g):
        pl.loop(0, rows)(lambda r: norm(src, dst, pl.multiple_of(r * frames, frames), pl.multiple_of(r * frames, frames), g))

    FIRST, KEY, VAL = 0, rows * E, 2 * rows * E
    pool = r_.s_pool
    @pl.when(z == 0)
    def _():
        r_.s_halo[:, 1] = jnp.zeros((rows, frames, W), BF)
    @pl.when(z <= 1)
    def _():
        r_.s_halo[:, 0] = jnp.zeros((rows, frames, W), BF)

    need(VEC)
    share = W // (8 * zn)
    for d in range(8):
        g = r_.s_vec[pl.ds(d * 16, 16), :].astype(F32)
        total = g[:, :128]
        for j in range(1, zn):
            total = total + pltpu.roll(g[:, j * 128:(j + 1) * 128], j * share, 1)
        r_.s_gain[:, d * 128:(d + 1) * 128] = total
    r_.gains[...] = r_.s_gain[...]
    for r in range(rows):
        norm(r_.hidden, pool, r * frames, FIRST + r * E + 2 * frames, 0)
    pump.work(6)
    load(0, 0).wait()
    for r in range(rows):
        def emit(m, c, v, r=r):
            r_.s_q[pl.ds(r * frames, frames), c] = v.astype(BF)
        dense(lambda r=r: pool[pl.ds(FIRST + r * E + 2 * frames, frames), :], 0, emit)
    save(r_.s_q, r_.q)
    pump.work(2.5)
    kc = load(1, 1)
    vc = load(2, 2)
    kc.wait(); vc.wait()

    def attend(r):
        r_.s_bias[...] = mask_keys(r_.q_ids[r], r_.k_ids[r], E - frames)
        def pair(p):
            c = pl.ds(pl.multiple_of(p * 128, 128), 128)
            rq = pl.ds(r * frames, frames)
            qs = stack_heads(r_.s_q[rq, c] * jnp.asarray(SCALE, BF))
            s = dot(pool[pl.ds(KEY + r * E, E), c], qs, 1, 1) + r_.s_bias[...]
            top = jnp.max(s, axis=0, keepdims=True)
            sh = jnp.exp(s - top)
            total = jnp.sum(sh, axis=0, keepdims=True)
            out = dot((sh / total).astype(BF), pool[pl.ds(VAL + r * E, E), c], 0, 0)
            r_.s_mixed[rq, c] = pick_heads(out).astype(BF)
            r_.s_lse[r, pl.ds(p, 1), :] = top + jnp.log(total)
        for part in range(4):
            pl.loop(part * heads2 // 4, (part + 1) * heads2 // 4)(pair)
            pump.work(2.6)

    for r in range(rows):
        pump.upto(2 * r + 4)
        @pl.when(z >= 2)
        def _():
            hcopy(r, 1).wait_recv()
        for c in range(2):
            norm(r_.s_halo.at[r, c], pool, 0, FIRST + r * E + c * frames, 0)
        save(r_.s_halo.at[r], r_.halo.at[r])
        save(pool.at[pl.ds(FIRST + r * E, E), :], r_.first.at[pl.ds(r * E, E), :])
        for base, slot in ((KEY, 1), (VAL, 2)):
            def emit(m, c, v, base=base, r=r):
                pool[pl.ds(base + r * E, E), c] = v.astype(BF)
            dense(lambda r=r: pool[pl.ds(FIRST + r * E, E), :], slot, emit)
            save(pool.at[pl.ds(base + r * E, E), :], (r_.k if base == KEY else r_.v).at[pl.ds(r * E, E), :])
        pump.work(5.5)
        if r == rows - 1:
            c3, c4, c5 = load(3, 0), load(4, 1), load(5, 2)
        attend(r)
    save(r_.s_mixed, r_.mixed); save(r_.s_lse, r_.lse)

    c3.wait()
    def emit(m, c, v):
        r_.s_as[:, c] = r_.hidden[:, c].astype(F32) + v
    dense(lambda: r_.s_mixed[...], 0, emit)
    pump.work(2.2)
    c6 = load(6, 0)
    norm_all(r_.s_as, r_.s_second, 2)
    save(r_.s_as, r_.after_self); save(r_.s_second, r_.second)
    pump.work(1.5)
    c4.wait()
    def emit(m, c, v):
        r_.s_cq[:, c] = v.astype(BF)
    dense(lambda: r_.s_second[...], 1, emit)
    save(r_.s_cq, r_.cq)
    pump.work(2.2)
    c7 = load(7, 1)
    for ready, slot, dst, out in ((c5, 2, r_.s_tk, r_.tk), (c6, 0, r_.s_tv, r_.tv)):
        ready.wait()
        def emit(m, c, v, dst=dst):
            dst[:, c] = v.astype(BF)
        dense(lambda: r_.text[...], slot, emit)
        save(dst, out)
        pump.work(1)
    c8 = load(8, 2)
    tokens = r_.text.shape[0] // rows
    for r in range(rows):
        def pair(p, r=r):
            c = pl.ds(pl.multiple_of(p * 128, 128), 128)
            rq, rk = pl.ds(r * frames, frames), pl.ds(r * tokens, tokens)
            sh = cross_shares(r_.s_cq[rq, c], pair_keys(r_.s_tk[rk, c]), ids, r_.t_ids[r], tokens)
            r_.s_cmix[rq, c] = dot(sh.astype(BF), pair_keys(r_.s_tv[rk, c]), 1, 0).astype(BF)
        ids = column(r_.q_ids[r][:, :frames])
        pl.loop(0, heads2)(pair)
        pump.work(3.7)
    save(r_.s_cmix, r_.cmix)
    c9 = load(9, 0)
    c7.wait()
    def emit(m, c, v):
        r_.s_ac[:, c] = r_.s_as[:, c] + v
    dense(lambda: r_.s_cmix[...], 1, emit)
    pump.work(2.2)
    norm_all(r_.s_ac, r_.s_third, 4)
    save(r_.s_ac, r_.after_cross); save(r_.s_third, r_.third)
    pump.work(1.5)

    for c in saves:
        settle(c)
    SLOPE, PRE = 0, 4 * T
    ready = {8: (2, c8), 9: (0, c9)}
    for i in range(4):
        if i == 0:
            ready[10] = (1, load(10, 1))
        slot, c = ready[8 + i]
        c.wait()
        def emit(m, c, v, i=i):
            act, slope = gelu_pair(v)
            for u in range(4):
                to = (i % 2) * 2 + u % 2
                lanes = pl.ds(pl.multiple_of((2 * (2 * m + u // 2) + i // 2) * 128, 128), 128)
                part = slice(u * 128, (u + 1) * 128)
                r_.s_act[to, :, lanes] = act[:, part].astype(BF)
                pool[pl.ds(SLOPE + to * T, T), lanes] = slope[:, part].astype(BF)
        dense(lambda: r_.s_third[...], slot, emit)
        pump.work(3.6)
        if i < 2:
            ready[11 + i] = (slot, load(11 + i, slot))
    fog = []
    def out_grad(i):
        def body(m, c):
            r_.s_fog[i % 2, c, :] = dot(r_.s_act[i, :, c], r_.cot[...], 0, 0).astype(BF)
        if i >= 2:
            fog[i - 2].wait()
        tiles(W, 512, body)
        g = pltpu.make_async_copy(r_.s_fog.at[i % 2], r_.fo_grad.at[i], r_.fogs.at[i])
        g.start()
        fog.append(g)
        pump.work(2.8)
    out_grad(0); out_grad(1)
    ready[13] = (1, load(13, 1))
    out_grad(2); out_grad(3)
    ready[14] = (2, load(14, 2))
    for i in range(4):
        slot, c = ready[12 + i]
        c.wait()
        def emit(m, c, v):
            r_.s_ac[:, c] = r_.s_ac[:, c] + v
        dense(lambda i=i: r_.s_act[i], slot, emit)
        def body(m, c, i=i, slot=slot):
            v = dot(r_.cot[...], r_.s_w[slot, c, :], 1, 1)
            v = v * pool[pl.ds(SLOPE + i * T, T), c].astype(F32)
            for u in range(4):
                to = (u % 2) * 2 + i // 2
                lanes = pl.ds(pl.multiple_of((2 * m + u // 2) * 256, 256) + (i % 2) * 128, 128)
                pool[pl.ds(PRE + to * T, T), lanes] = v[:, u * 128:(u + 1) * 128].astype(BF)
        tiles(W, 512, body)
        pump.work(4.4)
        if i == 0:
            ready[15] = (slot, load(15, slot))
    def body(s):
        r_.s_out[s, :] = r_.s_ac[s, :].astype(BF)
    blocks(T, frames, body)
    save(r_.s_out, r_.block)
    for i in range(4):
        save(pool.at[pl.ds(PRE + i * T, T), :], r_.pre_grad.at[i])

    pump.upto(pump.count)
    for i in order:
        advance(i, LAST)
    for c in fog[2:]:
        c.wait()
    for c in saves:
        settle(c)
    for r in range(rows):
        @pl.when(up_ok)
        def _():
            hcopy(r, 0).wait_send()
        @pl.when(up_ok & dn_ok)
        def _():
            hcopy(r, 1).wait_send()
    for i in order:
        for j in range(zn):
            @pl.when(up_ok & (j <= z))
            def _():
                zcopy(i, j, True).wait_send()
            @pl.when(dn_ok & (j >= z))
            def _():
                zcopy(i, j, False).wait_send()
        for k in range(2):
            xcopy(i, k).wait_send(); fcopy(i, k).wait_send()
        for k in range(4):
            ccopy(i, k).wait_send()

def forward(weights, vecs, hidden, text, cot, q_ids, k_ids, t_ids, zn, rows, frames, cid=2):
    T, E = rows * frames, 3 * frames
    S = jax.ShapeDtypeStruct
    D, V = pltpu.SemaphoreType.DMA, pltpu.VMEM
    VM = pl.BlockSpec(memory_space=pltpu.VMEM)
    tok = text.shape[0]
    outs = dict(weights=S((16, W, W), BF), gains=S((16, W), F32), halo=S((rows, 2, frames, W), BF), first=S((rows * E, W), BF), q=S((T, W), BF), k=S((rows * E, W), BF),
                v=S((rows * E, W), BF), lse=S((rows, W // 128, 2 * frames), F32), mixed=S((T, W), BF), after_self=S((T, W), F32), second=S((T, W), BF), cq=S((T, W), BF), tk=S((tok, W), BF), tv=S((tok, W), BF),
                cmix=S((T, W), BF), after_cross=S((T, W), F32), third=S((T, W), BF), pre_grad=S((4, T, W), BF), fo_grad=S((4, W, W), BF), block=S((T, W), BF))
    scratch = [V((rows, 2, frames, W), BF), V((3 * rows * E, W), BF), V((T, W), BF), V((T, W), BF), V((rows, W // 128, 2 * frames), F32), V((T, W), F32), V((T, W), BF), V((T, W), BF), V((tok, W), BF), V((tok, W), BF),
               V((T, W), BF), V((T, W), F32), V((T, W), BF), V((4, T, W), BF), V((3, W, W), BF), V((2, W, W), BF), V((E, 2 * frames), F32), V((128, 512), BF), V((16, W), F32), V((T, W), BF)]
    n = 17
    scratch += [D((n,)), D((n, 2, zn)), D((n, zn)), D((n, 2)), D((n, 2)), D((n, 2)), D((n, 2)), D((n, 4)), D((n, 4)), D((2, rows)), D((2, rows)), D((3,)), D((48,)), D((4,))]
    result = pl.pallas_call(
        functools.partial(forward_kernel, zn, rows, frames),
        out_shape=[outs[k] for k in F_OUT],
        in_specs=[VM] * len(F_IN), out_specs=[VM if k == "gains" else ANY for k in F_OUT],
        scratch_shapes=scratch,
        compiler_params=pltpu.CompilerParams(collective_id=cid, has_side_effects=True, vmem_limit_bytes=62 << 20),
        name="forward",
    )(*weights, vecs, hidden, text, cot, q_ids, k_ids, t_ids)
    return dict(zip(F_OUT, result))

SLOTS_G, SLOTS_A = 3, 8
PACE_B = 10.0
LAGS_B = (0, 1, 3, 4, 5, 6, 7)

def add_rows(dst, terms, rows, step=64):
    step = min(step, rows)
    @pl.loop(0, rows // step)
    def _(q):
        s = pl.ds(pl.multiple_of(q * step, step), step)
        total = terms[0][s, :].astype(F32)
        for t in terms[1:]:
            total = total + t[s, :].astype(F32)
        dst[s, :] = total.astype(dst.dtype)

def fold(v):
    return jnp.sum(v.reshape(v.shape[0] // 8, 8, v.shape[1]), axis=0)

B_IN = ["gains", "q_ids", "k_ids", "t_ids", "text",
        "hidden", "cot", "weights", "halo", "first", "q", "k", "v", "lse", "mixed", "after_self", "second", "cq", "tk", "tv", "cmix", "after_cross", "third", "pre_grad", "fo_grad"]
B_IN_VMEM = 5
B_OUT = ["g_q", "g_k", "g_v", "g_o", "g_cq", "g_ck", "g_cv", "g_co", "g_fi", "g_fo", "g_vec", "g_text", "g_hidden"]
B_SCR = ["p", "fa", "fb", "fc", "w", "g", "acc", "rh", "rxy", "rz", "vg", "vacc", "vrh", "vrxy", "vrz", "t", "tsrc", "trz", "h2s", "h2l", "h1", "hb", "hal", "bias", "lse_s", "sums",
         "cs", "cr", "ds", "dr", "xs", "xr", "zs", "zr", "ts", "tr", "hs", "hr", "credit", "ld", "ws", "outsem"]

def backward_kernel(zn, rows, frames, *refs):
    r_ = Names(B_IN + B_OUT + B_SCR, refs)
    T, E = rows * frames, 3 * frames
    heads2 = W // 128
    dp, z, core, x, y = place()
    xn = dp + 2 - 4 * x
    yn = dp + 4 - 8 * y
    dn = yn + 2 - 4 * x
    flip = 1 - 2 * core
    cn = dp + flip
    up_ok, dn_ok = z < zn - 1, z > 0
    peers = [(xn, z, None), (yn, z, None), (cn, z, None), (dp, z + 1, up_ok), (dp, z - 1, dn_ok)]
    barrier_with(peers)
    order = [12, 13, 14, 15, 8, 9, 10, 11, 7, 4, 5, 6, 3, 1, 2, 0, VEC]
    place_of = {i: a for a, i in enumerate(order)}
    fam = (dp, xn, yn, dn)

    def size(i):
        return (16, 128) if i == VEC else (SLAB, 256)
    def g(i):
        return r_.vg if i == VEC else r_.g.at[place_of[i] % SLOTS_G]
    def buf(i, big, small, *rest):
        base = small if i == VEC else big.at[place_of[i] % SLOTS_A]
        return base.at[rest] if rest else base
    def acc(i, k):
        return buf(i, r_.acc, r_.vacc, k)
    def gslab(i, who):
        s = size(i)[0]
        return g(i).at[pl.ds(pl.multiple_of(who * s, s), s), :]
    def remote(a, b, s, r, dev):
        return pltpu.make_async_remote_copy(a, b, s, r, device_id=dev, device_id_type=MESH)
    def ccopy(i, k):
        return remote(gslab(i, fam[k] + flip), acc(i, k), r_.cs.at[i, k], r_.cr.at[i, k], (cn, z))
    def half(ref, i, h):
        n = size(i)[0] // 2
        return ref.at[pl.ds(h * n, n), :]
    def dcopy(i, h):
        return remote(half(acc(i, 3), i, h), buf(i, r_.rh, r_.vrh, h), r_.ds.at[i, h], r_.dr.at[i, h], ((xn, yn)[h], z))
    def xcopy(i, d, h):
        return remote(half(acc(i, 1 + d), i, h), half(buf(i, r_.rxy, r_.vrxy, d), i, h), r_.xs.at[i, d, h], r_.xr.at[i, d, h], ((xn, yn)[d], z))
    def col(ref, i, j):
        c = size(i)[1]
        return ref.at[:, pl.ds(j * c, c)]
    def landing(up, zz, j):
        return j - zz if up else zn - zz + j
    def zcopy(i, up, zz, j):
        to = zz + 1 if up else zz - 1
        return remote(col(acc(i, 0), i, j), buf(i, r_.rz, r_.vrz, landing(up, to, j)), r_.zs.at[i, 0 if up else 1, j], r_.zr.at[i, 0 if up else 1, j], (dp, to))
    def zrecv(i, up, zz, j):
        b = buf(i, r_.rz, r_.vrz, landing(up, zz, j))
        return remote(b, b, r_.zs.at[i, 0 if up else 1, j], r_.zr.at[i, 0 if up else 1, j], (dp, zz - 1 if up else zz + 1))
    def zroles(t, body):
        for up in (True, False):
            zz = t if up else zn - 1 - t
            pl.when(z == zz)(functools.partial(body, up, zz))
    def zstage(i, t):
        def body(up, zz):
            for j in (range(zz + 1, zn) if up else range(zz - 1, -1, -1)):
                if t > 0:
                    zrecv(i, up, zz, j).wait_recv()
                    a = col(acc(i, 0), i, j)
                    add_rows(a, [a, buf(i, r_.rz, r_.vrz, landing(up, zz, j))], size(i)[0])
                zcopy(i, up, zz, j).start()
            if t > 0:
                zrecv(i, up, zz, zz).wait_recv()
        zroles(t, body)
    def result(i):
        if i == VEC:
            return r_.g_vec
        if i < 8:
            return refs[len(B_IN) + i]
        if i < 12:
            return r_.g_fi.at[:, pl.ds((i - 8) * 256, 256)]
        return r_.g_fo.at[pl.ds((i - 12) * SLAB, SLAB), :]
    def final(i):
        for zz in range(zn):
            @pl.when(z == zz)
            def _(zz=zz):
                terms = [col(acc(i, 0), i, zz)]
                if zz > 0:
                    terms.append(buf(i, r_.rz, r_.vrz, landing(True, zz, zz)))
                if zz < zn - 1:
                    terms.append(buf(i, r_.rz, r_.vrz, landing(False, zz, zz)))
                add_rows(result(i), terms, size(i)[0])
                for j in range(zn):
                    if j > zz:
                        zcopy(i, True, zz, j).wait_send()
                    if j < zz:
                        zcopy(i, False, zz, j).wait_send()
        for h in range(2):
            dcopy(i, h).wait_send()
            for d in range(2):
                xcopy(i, d, h).wait_send()
        if place_of[i] + SLOTS_A < 16:
            for s, (who, zz, ok) in enumerate(peers):
                def send(s=s, who=who, zz=zz):
                    pl.semaphore_signal(r_.credit.at[(0, 1, 2, 4, 3)[s]], inc=1, device_id=(who, zz), device_id_type=MESH)
                send() if ok is None else pl.when(ok)(send)
    FINAL = 3 + zn
    done = {}
    def advance(i, upto):
        while done[i] < upto:
            done[i] += 1
            s = done[i]
            rows_ = size(i)[0]
            if s == 1:
                for k in (3, 1, 2, 0):
                    ccopy(i, k).wait_recv()
                    add_rows(acc(i, k), [acc(i, k), gslab(i, fam[k])], rows_)
                    if k == 1:
                        dcopy(i, 0).start(); dcopy(i, 1).start()
                    if k == 2:
                        xcopy(i, 0, 0).start()
                    if k == 0:
                        xcopy(i, 1, 1).start()
                for k in range(4):
                    ccopy(i, k).wait_send()
            elif s == 2:
                for d, h in ((1, 0), (0, 1)):
                    dcopy(i, h).wait_recv()
                    a = half(acc(i, 1 + d), i, h)
                    add_rows(a, [a, buf(i, r_.rh, r_.vrh, h)], rows_ // 2)
                xcopy(i, 1, 0).start(); xcopy(i, 0, 1).start()
            elif s == 3:
                for d in range(2):
                    for h in range(2):
                        xcopy(i, d, h).wait_recv()
                add_rows(acc(i, 0), [acc(i, 0), buf(i, r_.rxy, r_.vrxy, 0), buf(i, r_.rxy, r_.vrxy, 1)], rows_)
                zstage(i, 0)
            elif s < FINAL:
                zstage(i, s - 3)
            else:
                final(i)
    waiting, line, spent = [], [], [0.0]
    def tick():
        line.append(waiting.pop(0) if waiting else None)
        for s, lag in enumerate(LAGS_B):
            i = line[-1 - lag] if lag < len(line) else None
            if i is not None:
                advance(i, s + 1)
    def work(cost):
        spent[0] += cost
        while spent[0] >= PACE_B:
            spent[0] -= PACE_B
            tick()
    def reach(i, stage):
        while done[i] < stage:
            tick()
    def grab(i):
        a = place_of[i]
        if i != VEC and a >= SLOTS_G:
            reach(order[a - SLOTS_G], 1)
        return g(i)
    def submit(i):
        a = place_of[i]
        done[i] = 0
        if i != VEC and a >= SLOTS_A:
            reach(order[a - SLOTS_A], FINAL)
            for s, (_, _, ok) in enumerate(peers):
                def take(s=s):
                    pl.semaphore_wait(r_.credit.at[s], 1)
                take() if ok is None else pl.when(ok)(take)
        for k in (3, 1, 2, 0):
            ccopy(i, k).start()
        waiting.append(i)

    loads = [0]
    def fetch(src, dst):
        c = pltpu.make_async_copy(src, dst, r_.ld.at[loads[0]])
        loads[0] += 1
        c.start()
        return c
    wslot = [0]
    def weight(i):
        s = wslot[0] % 2
        wslot[0] += 1
        c = pltpu.make_async_copy(r_.weights.at[i], r_.w.at[s], r_.ws.at[i])
        c.start()
        return s, c
    p = r_.p
    def rows_of(at, count):
        return p.at[pl.ds(at, count), :]
    def outer(lhs, rhs, dst, tile=512):
        def body(m, c):
            dst[c, :] = dot(lhs(c), rhs(), 0, 0).astype(BF)
        tiles(W, tile, body)
    def back(grad, slot, emit):
        def body(m, c):
            emit(c, dot(grad(), r_.w[slot, c, :], 1, 1))
        tiles(W, 512, body)
    def gain(k):
        return r_.gains[k:k + 1, :]
    def add_sum(k, v):
        r_.sums[pl.ds(k * 8, 8), :] += fold(v)
    def norm_back(k, value, grad, resid, out, low, count=T, step=frames, sums=True):
        def body(s):
            xhat, scale = standard(value(s))
            gr = grad(s)
            if sums:
                add_sum(k, gr * xhat)
                add_sum(k + 1, gr)
            e = gr * gain(k)
            inner = jnp.mean(e * xhat, axis=-1, keepdims=True)
            v = resid(s) + scale * (e - jnp.mean(e, axis=-1, keepdims=True) - xhat * inner)
            out[s, :] = v
            if low is not None:
                low[s, :] = v.astype(BF)
        blocks(count, step, body)

    K, V, FI, Q, DO = 0, rows * E, 2 * rows * E, 3 * rows * E, 3 * rows * E + T
    r_.sums[...] = jnp.zeros_like(r_.sums)
    fo_loads = [fetch(r_.fo_grad.at[i], grab(12 + i)) for i in range(SLOTS_G)]
    third_c = fetch(r_.third, rows_of(FI, T))
    pg = [fetch(r_.pre_grad.at[i], rows_of(K + i * T, T)) for i in range(3)]
    cot_c = fetch(r_.cot, rows_of(V, T))
    ac_c = fetch(r_.after_cross, r_.fc)
    for i in range(SLOTS_G):
        fo_loads[i].wait()
        submit(12 + i)
        work(0.5)
    third_c.wait()
    nxt = weight(8)
    pg.append(fetch(r_.pre_grad.at[3], rows_of(V + T, T)))
    at_pg = [K, K + T, K + 2 * T, V + T]
    for i in range(4):
        slot, wc = nxt
        pg[i].wait(); wc.wait()
        if i < 3:
            nxt = weight(9 + i)
        def emit(c, v, i=i):
            r_.fa[:, c] = v if i == 0 else r_.fa[:, c] + v
        back(lambda i=i: p[pl.ds(at_pg[i], T), :], slot, emit)
        work(2.4)
        if i == 0:
            for q in range(SLOTS_G, 4):
                c = fetch(r_.fo_grad.at[q], grab(12 + q)); c.wait()
                submit(12 + q)
                work(0.5)
        outer(lambda c: p[pl.ds(FI, T), c], lambda i=i: p[pl.ds(at_pg[i], T), :], grab(8 + i))
        submit(8 + i)
        work(2.8)
    cmix_c = fetch(r_.cmix, rows_of(V + T, T))
    co_slot, co_c = weight(7)
    cq_c = fetch(r_.cq, rows_of(FI, T))
    second_c = fetch(r_.second, rows_of(FI + T, T))
    mixed_c = fetch(r_.mixed, rows_of(FI + 2 * T, T))
    k_c = fetch(r_.k, rows_of(K, rows * E))
    t_c = [fetch(r_.tk, r_.t.at[0]), fetch(r_.tv, r_.t.at[1])]
    cot_c.wait(); ac_c.wait()
    norm_back(4, lambda s: r_.fc[s, :], lambda s: r_.fa[s, :], lambda s: p[pl.ds(pl.multiple_of(V + s.start, 16), s.size), :].astype(F32), r_.fa, rows_of(DO, T))
    as_c = fetch(r_.after_self, r_.fc)
    work(4)
    cmix_c.wait(); co_c.wait()
    outer(lambda c: p[pl.ds(V + T, T), c], lambda: p[pl.ds(DO, T), :], grab(7))
    submit(7)
    work(2)
    def emit(c, v):
        p[pl.ds(V + 2 * T, T), c] = v.astype(BF)
    back(lambda: p[pl.ds(DO, T), :], co_slot, emit)
    work(2)
    cqw_slot, cqw_c = weight(4)
    ckw_slot, ckw_c = weight(5)
    cq_c.wait(); t_c[0].wait(); t_c[1].wait()
    tokens = r_.text.shape[0] // rows
    for r in range(rows):
        def pair(h, r=r):
            c = pl.ds(pl.multiple_of(h * 128, 128), 128)
            rk = pl.ds(r * tokens, tokens)
            qrows = pl.ds(FI + r * frames, frames)
            q2, d2 = p[qrows, c], p[pl.ds(V + 2 * T + r * frames, frames), c]
            kk, vv = pair_keys(r_.t[0, rk, c]), pair_keys(r_.t[1, rk, c])
            sh = cross_shares(q2, kk, ids, r_.t_ids[r], tokens)
            dsh = dot(d2, vv, 1, 1)
            ds = (sh * (dsh - halves(sh * dsh, tokens, jnp.sum, 0.0))).astype(BF)
            p[qrows, c] = (dot(ds, kk, 1, 0) * SCALE).astype(BF)
            gk = dot(ds, q2, 0, 0) * SCALE
            gv = dot(sh.astype(BF), d2, 0, 0)
            first = lane_is((tokens, 128), 0)
            r_.t[0, rk, c] = jnp.where(first, gk[:tokens], gk[tokens:]).astype(BF)
            r_.t[1, rk, c] = jnp.where(first, gv[:tokens], gv[tokens:]).astype(BF)
        ids = column(r_.q_ids[r][:, :frames])
        pl.loop(0, heads2)(pair)
        work(4.8)
    v_c = fetch(r_.v, rows_of(V, rows * E))
    second_c.wait()
    outer(lambda c: p[pl.ds(FI + T, T), c], lambda: p[pl.ds(FI, T), :], grab(4))
    submit(4)
    work(2)
    cqw_c.wait()
    def emit(c, v):
        r_.fb[:, c] = v
    back(lambda: p[pl.ds(FI, T), :], cqw_slot, emit)
    work(2)
    cvw_slot, cvw_c = weight(6)
    as_c.wait()
    norm_back(2, lambda s: r_.fc[s, :], lambda s: r_.fb[s, :], lambda s: r_.fa[s, :], r_.fa, rows_of(Q, T))
    lse_c = fetch(r_.lse, r_.lse_s)
    work(4)
    outer(lambda c: r_.text[:, c], lambda: r_.t[0], grab(5))
    submit(5)
    work(1)
    ckw_c.wait()
    def body(m, c):
        v = dot(r_.t[0], r_.w[ckw_slot, c, :], 1, 1)
        r_.fb[pl.ds(0, rows * tokens), c] = v
    tiles(W, 256, body)
    ow_slot, ow_c = weight(3)
    outer(lambda c: r_.text[:, c], lambda: r_.t[1], grab(6))
    submit(6)
    work(1)
    cvw_c.wait()
    part = tokens // zn
    def body(m, c):
        v = r_.fb[pl.ds(0, rows * tokens), c] + dot(r_.t[1], r_.w[cvw_slot, c, :], 1, 1)
        for r in range(rows):
            for j in range(zn):
                r_.tsrc[j, r * part:(r + 1) * part, c] = v[r * tokens + j * part:r * tokens + (j + 1) * part].astype(BF)
    tiles(W, 256, body)
    kw_slot, kw_c = weight(1)
    def tcopy(up, zz, j):
        to = zz + 1 if up else zz - 1
        return remote(r_.tsrc.at[j], r_.trz.at[landing(up, to, j)], r_.ts.at[0 if up else 1, j], r_.tr.at[0 if up else 1, j], (dp, to))
    def trecv(up, zz, j):
        b = r_.trz.at[landing(up, zz, j)]
        return remote(b, b, r_.ts.at[0 if up else 1, j], r_.tr.at[0 if up else 1, j], (dp, zz - 1 if up else zz + 1))
    def tstage(t):
        def body(up, zz):
            for j in (range(zz + 1, zn) if up else range(zz - 1, -1, -1)):
                if t > 0:
                    trecv(up, zz, j).wait_recv()
                    add_rows(r_.tsrc.at[j], [r_.tsrc.at[j], r_.trz.at[landing(up, zz, j)]], rows * part, rows * part)
                tcopy(up, zz, j).start()
            if t > 0:
                trecv(up, zz, zz).wait_recv()
        zroles(t, body)
    def tfinal():
        for zz in range(zn):
            @pl.when(z == zz)
            def _(zz=zz):
                terms = [r_.tsrc.at[zz]]
                if zz > 0:
                    terms.append(r_.trz.at[landing(True, zz, zz)])
                if zz < zn - 1:
                    terms.append(r_.trz.at[landing(False, zz, zz)])
                add_rows(r_.g_text, terms, rows * part, rows * part)
                for j in range(zn):
                    if j > zz:
                        tcopy(True, zz, j).wait_send()
                    if j < zz:
                        tcopy(False, zz, j).wait_send()
    tstage(0)
    mixed_c.wait()
    outer(lambda c: p[pl.ds(FI + 2 * T, T), c], lambda: p[pl.ds(Q, T), :], grab(3))
    submit(3)
    work(2)
    ow_c.wait()
    def emit(c, v):
        p[pl.ds(DO, T), c] = v.astype(BF)
    back(lambda: p[pl.ds(Q, T), :], ow_slot, emit)
    work(2)
    vw_slot, vw_c = weight(2)
    q_c = fetch(r_.q, rows_of(Q, T))
    first_c = fetch(r_.first, rows_of(FI, rows * E))
    tstage(1)
    lse_c.wait(); k_c.wait(); v_c.wait(); q_c.wait()
    kw_c.wait(); vw_c.wait()

    def h2copy(r):
        return remote(r_.h2s.at[r], r_.h2l.at[r], r_.hs.at[0, r], r_.hr.at[0, r], (dp, z - 1))
    def h1copy(r):
        return remote(r_.h1.at[r], r_.hb.at[r], r_.hs.at[1, r], r_.hr.at[1, r], (dp, z - 1))
    def pass_on(r):
        @pl.when(dn_ok)
        def _():
            @pl.when(up_ok)
            def _():
                h2copy(r).wait_recv()
                add_rows(r_.h1.at[r], [r_.h1.at[r], r_.h2l.at[r]], frames, frames)
            h1copy(r).start()
    for r in range(rows):
        r_.bias[...] = mask_keys(r_.q_ids[r], r_.k_ids[r], E - frames)
        def pair(h, r=r):
            c = pl.ds(pl.multiple_of(h * 128, 128), 128)
            rq, rk, rv = pl.ds(Q + r * frames, frames), pl.ds(K + r * E, E), pl.ds(V + r * E, E)
            k2, v2 = p[rk, c], p[rv, c]
            qs, dd = stack_heads(p[rq, c] * jnp.asarray(SCALE, BF)), stack_heads(p[pl.ds(DO + r * frames, frames), c])
            sh = jnp.exp(dot(k2, qs, 1, 1) + r_.bias[...] - r_.lse_s[r, pl.ds(h, 1), :])
            dsh = dot(v2, dd, 1, 1)
            ds = (sh * (dsh - jnp.sum(sh * dsh, axis=0, keepdims=True))).astype(BF)
            p[rk, c] = dot(ds, qs, 1, 0).astype(BF)
            p[rv, c] = dot(sh.astype(BF), dd, 1, 0).astype(BF)
            p[rq, c] = (pick_heads(dot(ds, k2, 0, 0)) * SCALE).astype(BF)
        for part_ in range(4):
            pl.loop(part_ * heads2 // 4, (part_ + 1) * heads2 // 4)(pair)
            work(3.4)
        if r == 0:
            tstage(2)
        if r == 1:
            tstage(3)
            tfinal()
    hid_c = fetch(r_.hidden, rows_of(DO, T))
    first_c.wait()
    for i, at in ((1, K), (2, V)):
        outer(lambda c: p[pl.ds(FI, rows * E), c], lambda at=at: p[pl.ds(at, rows * E), :], grab(i), 256)
        submit(i)
        work(7)
    gq_ = grab(0)
    def body(m, c):
        total = None
        for r in range(rows):
            v = dot(p[pl.ds(FI + r * E + 2 * frames, frames), c], p[pl.ds(Q + r * frames, frames), :], 0, 0)
            total = v if total is None else total + v
        gq_[c, :] = total.astype(BF)
    tiles(W, 512, body)
    submit(0)
    work(2.5)
    for r in range(rows):
        hal_c = fetch(r_.halo.at[r], r_.hal)
        def body(m, c, r=r):
            v = dot(p[pl.ds(K + r * E, E), :], r_.w[kw_slot, c, :], 1, 1) + dot(p[pl.ds(V + r * E, E), :], r_.w[vw_slot, c, :], 1, 1)
            r_.h2s[r, :, c] = v[:frames].astype(BF)
            r_.h1[r, :, c] = v[frames:2 * frames].astype(BF)
            r_.fb[pl.ds(r * frames, frames), c] = v[2 * frames:]
        tiles(W, 512, body)
        hal_c.wait()
        for q in range(2):
            gr = (r_.h2s, r_.h1)[q][r].astype(F32)
            add_sum(0, gr * standard(r_.hal[q].astype(F32))[0])
            add_sum(1, gr)
        @pl.when(z >= 2)
        def _():
            h2copy(r).start()
        work(5)
        if r > 0:
            pass_on(r - 1)
    qw_slot, qw_c = weight(0)
    qw_c.wait(); hid_c.wait()
    def emit(c, v):
        r_.fb[:, c] = r_.fb[:, c] + v
    back(lambda: p[pl.ds(Q, T), :], qw_slot, emit)
    work(2.2)
    pass_on(rows - 1)
    def body(s):
        gr = r_.fb[s, :]
        add_sum(0, gr * standard(p[pl.ds(pl.multiple_of(DO + s.start, 16), s.size), :].astype(F32))[0])
        add_sum(1, gr)
    blocks(T, frames, body)
    sums = jnp.sum(r_.sums[...].reshape(6, 8, W), axis=1)
    sums = jnp.concatenate([sums, jnp.zeros((10, W), F32)], axis=0)
    share = W // (8 * zn)
    keep = lax.broadcasted_iota(jnp.int32, (16, 128), 1) < share
    for d in range(8):
        v = sums[:, d * 128:(d + 1) * 128]
        for j in range(zn):
            moved = pltpu.roll(v, (128 - j * share) % 128, 1)
            r_.vg[d * 16:(d + 1) * 16, j * 128:(j + 1) * 128] = jnp.where(keep, moved, 0.0).astype(BF)
    submit(VEC)
    work(3)
    for r in range(rows):
        @pl.when(up_ok)
        def _():
            h1copy(r).wait_recv()
            add_rows(r_.fb.at[pl.ds(r * frames, frames), :], [r_.fb.at[pl.ds(r * frames, frames), :], r_.hb.at[r]], frames, frames)
    norm_back(0, lambda s: p[pl.ds(pl.multiple_of(DO + s.start, 16), s.size), :].astype(F32), lambda s: r_.fb[s, :], lambda s: r_.fa[s, :], r_.fa, None, sums=False)
    oc = pltpu.make_async_copy(r_.fa, r_.g_hidden, r_.outsem.at[0])
    oc.start()
    for i in order:
        reach(i, FINAL)
    oc.wait()
    for r in range(rows):
        @pl.when(z >= 2)
        def _():
            h2copy(r).wait_send()
        @pl.when(dn_ok)
        def _():
            h1copy(r).wait_send()

def backward(f, hidden, text, cot, q_ids, k_ids, t_ids, zn, rows, frames, cid=3):
    T, E = rows * frames, 3 * frames
    S = jax.ShapeDtypeStruct
    D, V = pltpu.SemaphoreType.DMA, pltpu.VMEM
    VM = pl.BlockSpec(memory_space=pltpu.VMEM)
    tok = text.shape[0]
    part = tok // zn
    vals = dict(f, hidden=hidden, text=text, cot=cot, q_ids=q_ids, k_ids=k_ids, t_ids=t_ids)
    outs = [S((128, 256), F32)] * 8 + [S((128, 1024), F32), S((512, 256), F32), S((16, 128), F32), S((part, W), F32), S((T, W), F32)]
    A = SLOTS_A
    scratch = [V((3 * rows * E + 2 * T, W), BF), V((T, W), F32), V((T, W), F32), V((T, W), F32), V((2, W, W), BF), V((SLOTS_G, W, W), BF),
               V((A, 4, 128, W), BF), V((A, 2, 64, W), BF), V((A, 2, 128, W), BF), V((A, zn + 1, 128, 256), BF),
               V((128, 512), BF), V((4, 16, 512), BF), V((2, 8, 512), BF), V((2, 16, 512), BF), V((zn + 1, 16, 128), BF),
               V((2, tok, W), BF), V((zn, part, W), BF), V((zn + 1, part, W), BF),
               V((rows, frames, W), BF), V((rows, frames, W), BF), V((rows, frames, W), BF), V((rows, frames, W), BF), V((2, frames, W), BF), V((E, 2 * frames), F32), V((rows, W // 128, 2 * frames), F32), V((48, W), F32)]
    n = 17
    scratch += [D((n, 4)), D((n, 4)), D((n, 2)), D((n, 2)), D((n, 2, 2)), D((n, 2, 2)), D((n, 2, zn)), D((n, 2, zn)), D((2, zn)), D((2, zn)), D((2, rows)), D((2, rows)),
                pltpu.SemaphoreType.REGULAR((5,)), D((40,)), D((16,)), D((1,))]
    return pl.pallas_call(
        functools.partial(backward_kernel, zn, rows, frames),
        out_shape=outs,
        in_specs=[VM] * B_IN_VMEM + [ANY] * (len(B_IN) - B_IN_VMEM), out_specs=[VM] * (len(B_OUT) - 1) + [ANY],
        scratch_shapes=scratch,
        compiler_params=pltpu.CompilerParams(collective_id=cid, has_side_effects=True, vmem_limit_bytes=63 << 20),
        name="backward",
    )(*[vals[k] for k in B_IN])

EPSILON = 1e-05

def project(left_side, right_side, kind=F32):
    return jnp.einsum("rfk,kn->rfn", left_side, right_side, preferred_element_type=F32).astype(kind)

def project_back(gradient, right_side, kind=F32):
    return jnp.einsum("rfn,kn->rfk", gradient, right_side, preferred_element_type=F32).astype(kind)

def weight_grad(left_side, gradient):
    return jnp.einsum("rfk,rfn->kn", left_side, gradient, preferred_element_type=F32).astype(BF)

def normalized(values):
    values = values.astype(F32)
    centred = values - jnp.mean(values, axis=-1, keepdims=True)
    scale = lax.rsqrt(jnp.mean(centred * centred, axis=-1, keepdims=True) + EPSILON)
    return centred * scale, scale

def norm_back(values, gain, grad):
    xhat, scale = normalized(values)
    e = gain * grad
    inner = jnp.mean(e * xhat, axis=-1, keepdims=True)
    inputs = scale * (e - jnp.mean(e, axis=-1, keepdims=True) - xhat * inner)
    return jnp.sum(grad * xhat, axis=(0, 1)), jnp.sum(grad, axis=(0, 1)), inputs

def gelu_parts(u):
    half_erf = 0.5 * (1.0 + lax.erf(u * 0.7071067811865476))
    return u * half_erf, half_erf + u * (0.3989422804014327 * jnp.exp(-0.5 * u * u))

def gather_all(weights, vectors, hidden, dpn, zn):
    rows, frames, width = hidden.shape
    share = vectors.shape[1]
    if (dpn, zn) == (8, 4):
        packed = jnp.pad(vectors, ((0, 16 - vectors.shape[0]), (0, 128 - share)))
        *whole, packed, ext = gather(list(weights) + [packed], hidden, dpn, zn)
        packed = packed.reshape(dpn, 16, zn, 128)[:, :vectors.shape[0], :, :share]
        return whole, packed.transpose(1, 0, 2, 3).reshape(vectors.shape[0], width), ext
    whole = [lax.all_gather(lax.all_gather(w, "ctx", axis=1, tiled=True), "dp", axis=0, tiled=True) for w in weights]
    near = lax.ppermute(hidden, "ctx", [(i, i + 1) for i in range(zn - 1)])
    far = lax.ppermute(hidden, "ctx", [(i, i + 2) for i in range(zn - 2)])
    return whole, lax.all_gather(vectors, ("dp", "ctx"), axis=1, tiled=True), jnp.stack([far, near, hidden], axis=1)

def scatter_all(grads, vectors, text, halo, dpn, zn):
    count, width = vectors.shape
    rows, tokens = text.shape[:2]
    if (dpn, zn) == (8, 4):
        share = width // (dpn * zn)
        packed = jnp.pad(vectors.reshape(count, dpn, zn, share).transpose(1, 0, 2, 3), ((0, 0), (0, 16 - count), (0, 0), (0, 128 - share)))
        packed = packed.reshape(dpn * 16, zn * 128).astype(BF)
        folded = text.reshape(rows, zn, tokens // zn, width).transpose(0, 2, 1, 3).reshape(rows * tokens // zn, zn * width)
        *own, packed, folded, back = scatter(list(grads) + [packed], folded, halo, dpn, zn)
        return own, packed[:count, :share], folded.reshape(rows, tokens // zn, width), back
    own = [lax.psum_scatter(lax.psum_scatter(g, "dp", scatter_dimension=0, tiled=True), "ctx", scatter_dimension=1, tiled=True).astype(F32) for g in grads]
    back = lax.ppermute(halo[:, 1], "ctx", [(i + 1, i) for i in range(zn - 1)]).astype(F32)
    back = back + lax.ppermute(halo[:, 0], "ctx", [(i + 2, i) for i in range(zn - 2)]).astype(F32)
    return (own, lax.psum_scatter(vectors, ("dp", "ctx"), scatter_dimension=1, tiled=True),
            lax.psum_scatter(text.astype(F32), "ctx", scatter_dimension=1, tiled=True), back)

def general(hidden, text_states, frame_segments, text_segments, text_lengths, cotangent, *params):
    dpn, zn = lax.axis_size("dp"), lax.axis_size("ctx")
    place = lax.axis_index("ctx")
    rows, frames, width = hidden.shape
    weights, vectors = params[:10], jnp.stack(params[10:])
    reach = 2 * frames
    ids = jnp.pad(frame_segments, ((0, 0), (reach, 0)), constant_values=-1)
    key_ids = lax.dynamic_slice_in_dim(ids, place * frames, reach + frames, 1)
    own_ids = key_ids[:, reach:]
    text_ids = jnp.where(jnp.arange(text_segments.shape[1])[None] < text_lengths[:, None], text_segments, -1)

    whole, vec, ext = gather_all(weights, vectors, hidden, dpn, zn)
    wq, wk, wv, wo, cq, ck, cv, co, fi, fo = whole
    g1, s1, g2, s2, g3, s3 = vec.astype(F32)

    first_ext = (normalized(ext)[0] * g1 + s1).astype(BF)
    first_own = first_ext[:, 2]
    first_ext = first_ext.reshape(rows, 3 * frames, width)
    queries = project(first_own, wq, BF)
    keys = project(first_ext, wk, BF)
    values = project(first_ext, wv, BF)
    self_mixed, self_total = self_forward(queries, keys, values, own_ids, key_ids)
    states = hidden.astype(F32)
    after_self = states + project(self_mixed, wo)
    second_norm = (normalized(after_self)[0] * g2 + s2).astype(BF)
    cross_queries = project(second_norm, cq, BF)
    text_keys = project(text_states, ck, BF)
    text_values = project(text_states, cv, BF)
    cross_mixed = cross_forward(cross_queries, text_keys, text_values, own_ids, text_ids)
    after_cross = after_self + project(cross_mixed, co)
    third_norm = (normalized(after_cross)[0] * g3 + s3).astype(BF)
    pre_act = project(third_norm, fi)
    activated, slope = gelu_parts(pre_act)
    activated = activated.astype(BF)
    block_output = (after_cross + project(activated, fo)).astype(BF)

    fo_grad = weight_grad(activated, cotangent)
    pre_grad = (project_back(cotangent, fo) * slope).astype(BF)
    fi_grad = weight_grad(third_norm, pre_grad)
    g3_grad, s3_grad, part = norm_back(after_cross, g3, project_back(pre_grad, fi))
    cross_grad = cotangent.astype(F32) + part
    cross_low = cross_grad.astype(BF)
    co_grad = weight_grad(cross_mixed, cross_low)
    cross_mixed_grad = project_back(cross_low, co, BF)
    cq_low, tk_low, tv_low = cross_backward(cross_queries, text_keys, text_values, cross_mixed_grad, own_ids, text_ids)
    ck_grad = weight_grad(text_states, tk_low)
    cv_grad = weight_grad(text_states, tv_low)
    text_part = (project_back(tk_low, ck) + project_back(tv_low, cv)).astype(BF)
    cq_grad = weight_grad(second_norm, cq_low)
    g2_grad, s2_grad, part = norm_back(after_self, g2, project_back(cq_low, cq))
    self_grad = cross_grad + part
    self_low = self_grad.astype(BF)
    wo_grad = weight_grad(self_mixed, self_low)
    self_mixed_grad = project_back(self_low, wo, BF)
    q_low, k_low, v_low = self_backward(queries, keys, values, self_total, self_mixed_grad, own_ids, key_ids)
    wq_grad = weight_grad(first_own, q_low)
    wk_grad = weight_grad(first_ext, k_low)
    wv_grad = weight_grad(first_ext, v_low)
    first_grad = (project_back(k_low, wk) + project_back(v_low, wv)).reshape(rows, 3, frames, width)
    own_grad = first_grad[:, 2] + project_back(q_low, wq)
    halo_grad = first_grad[:, :2].astype(BF)
    xhat_ext = normalized(ext)[0]
    g1_grad = jnp.sum(first_grad[:, :2] * xhat_ext[:, :2], axis=(0, 1, 2)) + jnp.sum(own_grad * xhat_ext[:, 2], axis=(0, 1))
    s1_grad = jnp.sum(first_grad[:, :2], axis=(0, 1, 2)) + jnp.sum(own_grad, axis=(0, 1))

    grads = (wq_grad, wk_grad, wv_grad, wo_grad, cq_grad, ck_grad, cv_grad, co_grad, fi_grad, fo_grad)
    vec_grads = jnp.stack([g1_grad, s1_grad, g2_grad, s2_grad, g3_grad, s3_grad])
    own, vec_own, text_grad, back = scatter_all(grads, vec_grads, text_part, halo_grad, dpn, zn)
    part = norm_back(states, g1, own_grad + back.astype(F32))[2]
    return (block_output, self_grad + part, text_grad, *own, *vec_own)

def fused(hidden, text_states, frame_segments, text_segments, text_lengths, cotangent, *params):
    dpn, zn = lax.axis_size("dp"), lax.axis_size("ctx")
    place = lax.axis_index("ctx")
    rows, frames, width = hidden.shape
    weights, vectors = params[:10], jnp.stack(params[10:])
    reach = 2 * frames
    ids = jnp.pad(frame_segments, ((0, 0), (reach, 0)), constant_values=-1)
    key_ids = lax.dynamic_slice_in_dim(ids, place * frames, reach + frames, 1)
    own_ids = key_ids[:, reach:]
    text_ids = jnp.where(jnp.arange(text_segments.shape[1])[None] < text_lengths[:, None], text_segments, -1)

    packed = jnp.pad(vectors, ((0, 16 - vectors.shape[0]), (0, 128 - vectors.shape[1])))
    flat = lambda v: v.reshape(-1, v.shape[-1])
    f = forward(weights, packed, flat(hidden), flat(text_states), flat(cotangent), jnp.concatenate([own_ids, own_ids], axis=1)[:, None, :], key_ids[:, None, :],
                jnp.concatenate([text_ids, text_ids], axis=1)[:, None, :], zn, rows, frames)
    grads = backward(f, flat(hidden), flat(text_states), flat(cotangent), jnp.concatenate([own_ids, own_ids], axis=1)[:, None, :], key_ids[:, None, :],
                     jnp.concatenate([text_ids, text_ids], axis=1)[:, None, :], zn, rows, frames)
    *own, vec_own, text_grad, hidden_grad = grads
    return (f["block"].reshape(hidden.shape), hidden_grad.reshape(hidden.shape), text_grad.reshape(rows, -1, width), *own, *vec_own[:6, :vectors.shape[1]])

def per_device(hidden, text_states, frame_segments, text_segments, text_lengths, cotangent, *params):
    dpn, zn = lax.axis_size("dp"), lax.axis_size("ctx")
    if (dpn, zn) == (8, 4) and params[0].shape == (128, 256):
        return fused(hidden, text_states, frame_segments, text_segments, text_lengths, cotangent, *params)
    return general(hidden, text_states, frame_segments, text_segments, text_lengths, cotangent, *params)

def solution(mesh):
    rows, both = P("dp", "ctx", None), P("dp", "ctx")
    flat = P(("dp", "ctx"))
    placed = (rows, P("dp", None, None), P("dp", None), P("dp", None), P("dp"), rows) + (both,) * 10 + (flat,) * 6
    return jax.shard_map(per_device, mesh=mesh, in_specs=placed, out_specs=(rows,) * 3 + (both,) * 10 + (flat,) * 6, check_vma=False)
```

```python
import functools

import jax
import jax.numpy as jnp
from jax import lax
from jax.experimental import pallas as pl
from jax.experimental.pallas import tpu as pltpu
from jax.sharding import PartitionSpec as P

BF = jnp.bfloat16
F32 = jnp.float32


MESH = pl.DeviceIdType.MESH
ANY = pl.BlockSpec(memory_space=pl.ANY)

def place():
    dp = lax.axis_index("dp"); z = lax.axis_index("ctx")
    core = lax.rem(dp, 2); x = lax.rem(dp // 2, 2); y = dp // 4
    return dp, z, core, x, y

def pieces_of(shapes):
    out = []
    for w, (rows, cols) in enumerate(shapes):
        n = max(1, (rows * cols) // (128 * 256))
        step = rows // n
        for i in range(n):
            out.append((w, i * step, step, rows, cols))
    return out

def gather_kernel(shapes, zn, lags, *refs):
    nw = len(shapes)
    src, hidden, dst, ext = refs[:nw], refs[nw], refs[nw + 1:2 * nw + 1], refs[2 * nw + 1]
    blank, lsem, zs, zr, xs, xr, fs, fr, cs, cr, hl, hs, hr, bs = refs[2 * nw + 2:]
    nrow = hidden.shape[0]
    dp, z, core, x, y = place()
    xn = dp + 2 - 4 * x
    yn = dp + 4 - 8 * y
    dn = yn + 2 - 4 * x
    cn = dp + 1 - 2 * core
    chunks = pieces_of(shapes)
    n = len(chunks)
    up_ok, dn_ok = z < zn - 1, z > 0

    barrier = pltpu.get_barrier_semaphore()
    for who in (xn, yn, cn):
        pl.semaphore_signal(barrier, inc=1, device_id=(who, z), device_id_type=MESH)
    @pl.when(up_ok)
    def _():
        pl.semaphore_signal(barrier, inc=1, device_id=(dp, z + 1), device_id_type=MESH)
    @pl.when(dn_ok)
    def _():
        pl.semaphore_signal(barrier, inc=1, device_id=(dp, z - 1), device_id_type=MESH)
    pl.semaphore_wait(barrier, 3 + up_ok.astype(jnp.int32) + dn_ok.astype(jnp.int32))

    def own(i):
        w, r0, r, rows, cols = chunks[i]
        return src[w].at[pl.ds(r0, r), :]
    def block(i, who, j):
        w, r0, r, rows, cols = chunks[i]
        return dst[w].at[pl.ds(pl.multiple_of(who * rows + r0, r), r), pl.ds(pl.multiple_of(j * cols, cols), cols)]
    def slab(i, who, half=None):
        w, r0, r, rows, cols = chunks[i]
        if half is None:
            return dst[w].at[pl.ds(pl.multiple_of(who * rows + r0, r), r), :]
        h = r // 2
        return dst[w].at[pl.ds(pl.multiple_of(who * rows + r0 + half * h, h), h), :]

    def remote(a, b, s, r, dev):
        return pltpu.make_async_remote_copy(a, b, s, r, device_id=dev, device_id_type=MESH)
    def zcopy(i, j, up, first=False):
        a = own(i) if first else block(i, dp, j)
        return remote(a, block(i, dp, j), zs.at[i, 0 if up else 1, j], zr.at[i, j], (dp, z + 1 if up else z - 1))
    def xcopy(i):
        return remote(slab(i, dp), slab(i, dp), xs.at[i, 0], xr.at[i, 0], (xn, z))
    def ycopy(i):
        return remote(slab(i, dp), slab(i, dp), xs.at[i, 1], xr.at[i, 1], (yn, z))
    def fcopy(i, half):
        who, to = (xn, yn) if half == 0 else (yn, xn)
        return remote(slab(i, who, half), slab(i, who, half), fs.at[i, half], fr.at[i, half], (to, z))
    def frecv(i, half):
        return remote(slab(i, dn, half), slab(i, dn, half), fs.at[i, half], fr.at[i, half], (yn, z))
    def ccopy(i, k):
        who = (dp, xn, yn, dn)[k]
        return remote(slab(i, who), slab(i, who), cs.at[i, k], cr.at[i, k], (cn, z))
    def crecv(i, k):
        who = (dp, xn, yn, dn)[k] + 1 - 2 * core
        return remote(slab(i, who), slab(i, who), cs.at[i, k], cr.at[i, k], (cn, z))
    def hlocal(r):
        return pltpu.make_async_copy(hidden.at[r], ext.at[r, 2], hl.at[r])
    def hcopy(r, hop):
        return remote(ext.at[r, 1] if hop else hidden.at[r], ext.at[r, 1 - hop], hs.at[hop, r], hr.at[hop, r], (dp, z + 1))
    def hblank(r, c):
        return pltpu.make_async_copy(blank, ext.at[r, c], bs.at[r, c])
    def lcopy(i):
        return pltpu.make_async_copy(own(i), block(i, dp, z), lsem.at[i])
    def xrecv(i):
        return remote(slab(i, xn), slab(i, xn), xs.at[i, 0], xr.at[i, 0], (xn, z))
    def yrecv(i):
        return remote(slab(i, yn), slab(i, yn), xs.at[i, 1], xr.at[i, 1], (yn, z))

    for i in range(n):
        @pl.when(up_ok)
        def _():
            zcopy(i, z, True, True).start()
        @pl.when(dn_ok)
        def _():
            zcopy(i, z, False, True).start()
        lcopy(i).start()
    for r in range(nrow):
        hlocal(r).start()
    blank[...] = jnp.zeros_like(blank)

    def halo_step(k):
        if k % 3 == 1 and k // 3 < nrow:
            @pl.when(up_ok)
            def _():
                hcopy(k // 3, 0).start()
        if k % 3 == 0 and 0 <= k // 3 - 1 < nrow:
            r = k // 3 - 1
            @pl.when(dn_ok)
            def _():
                hcopy(r, 0).wait_recv()
                @pl.when(up_ok)
                def _():
                    hcopy(r, 1).start()
        if k % 3 == 2 and 0 <= k // 3 - 1 < nrow:
            r = k // 3 - 1
            @pl.when(z == 0)
            def _():
                hblank(r, 1).start()
            @pl.when(z <= 1)
            def _():
                hblank(r, 0).start()

    def zstage(i, t):
        @pl.when(z - t >= 0)
        def _():
            zcopy(i, z - t, True).wait_recv()
            @pl.when(up_ok)
            def _():
                zcopy(i, z - t, True).start()
        @pl.when(z + t < zn)
        def _():
            zcopy(i, z + t, False).wait_recv()
            @pl.when(dn_ok)
            def _():
                zcopy(i, z + t, False).start()
    def stage(s, i):
        if s == 0 or s == 1:
            zstage(i, s + 1)
        elif s == 2:
            zstage(i, 3)
            lcopy(i).wait()
            xcopy(i).start(); ycopy(i).start(); ccopy(i, 0).start()
        elif s == 3:
            xrecv(i).wait_recv()
            fcopy(i, 0).start(); ccopy(i, 1).start()
            yrecv(i).wait_recv()
            fcopy(i, 1).start(); ccopy(i, 2).start()
        elif s == 4:
            frecv(i, 0).wait_recv(); frecv(i, 1).wait_recv()
            ccopy(i, 3).start()
        else:
            for k in range(4):
                crecv(i, k).wait_recv()
    for k in range(n + lags[-1]):
        halo_step(k)
        for s, lag in enumerate(lags):
            if 0 <= k - lag < n:
                stage(s, k - lag)
    for r in range(nrow):
        hlocal(r).wait()
        @pl.when(up_ok)
        def _():
            hcopy(r, 0).wait_send()
        @pl.when(up_ok & dn_ok)
        def _():
            hcopy(r, 1).wait_send()
        @pl.when(z >= 2)
        def _():
            hcopy(r, 1).wait_recv()
        @pl.when(z == 0)
        def _():
            hblank(r, 1).wait()
        @pl.when(z <= 1)
        def _():
            hblank(r, 0).wait()
    for i in range(n):
        for j in range(zn):
            @pl.when(up_ok & (j <= z))
            def _():
                zcopy(i, j, True).wait_send()
            @pl.when(dn_ok & (j >= z))
            def _():
                zcopy(i, j, False).wait_send()
        xcopy(i).wait_send(); ycopy(i).wait_send()
        fcopy(i, 0).wait_send(); fcopy(i, 1).wait_send()
        for k in range(4):
            ccopy(i, k).wait_send()

def gather(weights, hidden, dpn, zn, cid=0, lags=(0, 1, 2, 4, 6, 8)):
    shapes = tuple(tuple(w.shape) for w in weights)
    n = len(pieces_of(shapes))
    D = pltpu.SemaphoreType.DMA
    rows, frames, width = hidden.shape
    return pl.pallas_call(
        functools.partial(gather_kernel, shapes, zn, lags),
        out_shape=[jax.ShapeDtypeStruct((dpn * r, zn * c), jnp.bfloat16) for r, c in shapes] + [jax.ShapeDtypeStruct((rows, 3, frames, width), jnp.bfloat16)],
        in_specs=[pl.BlockSpec(memory_space=pltpu.VMEM)] * (len(shapes) + 1),
        out_specs=[ANY] * (len(shapes) + 1),
        scratch_shapes=[pltpu.VMEM((frames, width), jnp.bfloat16), D((n,)), D((n, 2, zn)), D((n, zn)), D((n, 2)), D((n, 2)), D((n, 2)), D((n, 2)), D((n, 4)), D((n, 4)),
                        D((rows,)), D((2, rows)), D((2, rows)), D((rows, 2))],
        compiler_params=pltpu.CompilerParams(collective_id=cid, has_side_effects=True),
        name="gather",
    )(*weights, hidden)

def add_rows(dst, terms, rows, step=16):
    @pl.loop(0, rows // step)
    def _(q):
        s = pl.ds(pl.multiple_of(q * step, step), step)
        total = terms[0][s, :].astype(F32)
        for t in terms[1:]:
            total = total + t[s, :].astype(F32)
        dst[s, :] = total.astype(dst.dtype)

def scatter_kernel(shapes, nhalo, zn, lags, *refs):
    nw = len(shapes)
    it = iter(refs)
    take = lambda k: [next(it) for _ in range(k)]
    grads = take(nw)
    text, halo = take(2)
    outs = take(nw)
    text_out, halo_out = take(2)
    acc, rh, rxy, rz = take(nw), take(nw), take(nw), take(nw)
    kinds = sorted({(s[0] // (1 if s[0]*s[1] <= 128*256 else (s[0]*s[1]) // (128*256)), s[1]) for s in shapes})
    stage = dict(zip(kinds, take(len(kinds))))
    tz, h2, h1, hs = take(4)
    ls, cs, cr, hsd, hrc, xs, xr, zs, zr, tzs, tzr, hls, hss, hrs = take(14)
    dp, z, core, x, y = place()
    xn = dp + 2 - 4 * x
    yn = dp + 4 - 8 * y
    dn = yn + 2 - 4 * x
    flip = 1 - 2 * core
    cn = dp + flip
    chunks = pieces_of(shapes)
    first = {}
    for i, c in enumerate(chunks):
        first.setdefault(c[0], i)
    n = len(chunks)
    up_ok, dn_ok = z < zn - 1, z > 0
    barrier = pltpu.get_barrier_semaphore()
    for who in (xn, yn, cn):
        pl.semaphore_signal(barrier, inc=1, device_id=(who, z), device_id_type=MESH)
    @pl.when(up_ok)
    def _():
        pl.semaphore_signal(barrier, inc=1, device_id=(dp, z + 1), device_id_type=MESH)
    @pl.when(dn_ok)
    def _():
        pl.semaphore_signal(barrier, inc=1, device_id=(dp, z - 1), device_id_type=MESH)
    pl.semaphore_wait(barrier, 3 + up_ok.astype(jnp.int32) + dn_ok.astype(jnp.int32))

    def remote(a, b, s, r, dev):
        return pltpu.make_async_remote_copy(a, b, s, r, device_id=dev, device_id_type=MESH)
    def slab(i, who):
        w, r0, r, rows, cols = chunks[i]
        return grads[w].at[pl.ds(pl.multiple_of(who * rows + r0, r), r), :]
    fam = (dp, xn, yn, dn)
    def at(buf, i, *rest):
        w = chunks[i][0]
        return buf[w].at[(i - first[w],) + rest]
    def ccopy(i, k):
        return remote(slab(i, fam[k] + flip), at(acc, i, k), cs.at[i, k], cr.at[i, k], (cn, z))
    def staged(i):
        w, r0, r, rows, cols = chunks[i]
        return stage[(r, cols)]
    slots = {}
    cnt = {}
    for i, c in enumerate(chunks):
        key = (c[2], c[4]); slots[i] = cnt.get(key, 0) % 2; cnt[key] = cnt.get(key, 0) + 1
    kidx = {k: q for q, k in enumerate(kinds)}
    def lcopy(i, k):
        key = (chunks[i][2], chunks[i][4])
        return pltpu.make_async_copy(slab(i, fam[k]), staged(i).at[slots[i], k], ls.at[kidx[key], slots[i], k])
    prev = {}
    nxt = {}
    last = {}
    for i, c in enumerate(chunks):
        key = (c[2], c[4])
        last.setdefault(key, []).append(i)
    for key, l in last.items():
        for a, b in zip(l, l[2:]):
            nxt[a] = b
    def half(ref, i, h):
        r = chunks[i][2]
        return ref.at[pl.ds(h * (r // 2), r // 2), :]
    def dcopy(i, h):
        return remote(half(at(acc, i, 3), i, h), at(rh, i, h), hsd.at[i, h], hrc.at[i, h], ((xn, yn)[h], z))
    def xcopy(i, d, h):
        return remote(half(at(acc, i, 1 + d), i, h), half(at(rxy, i, d), i, h), xs.at[i, d, h], xr.at[i, d, h], ((xn, yn)[d], z))
    def col(ref, i, j):
        cols = chunks[i][4]
        return ref.at[:, pl.ds(j * cols, cols)]
    def zcopy(i, up, j):
        return remote(col(at(acc, i, 0), i, j), at(rz, i, 0 if up else 1, j), zs.at[i, 0 if up else 1, j], zr.at[i, 0 if up else 1, j], (dp, z + 1 if up else z - 1))
    tc = text.shape[1] // zn
    tr = text.shape[0]
    def tcopy(up, j):
        return remote(text.at[:, pl.ds(j * tc, tc)], tz.at[0 if up else 1, j], tzs.at[0 if up else 1, j], tzr.at[0 if up else 1, j], (dp, z + 1 if up else z - 1))
    def h2copy(r):
        return remote(halo.at[r, 0], h2.at[r], hss.at[0, r], hrs.at[0, r], (dp, z - 1))
    def h1local(r):
        return pltpu.make_async_copy(halo.at[r, 1], h1.at[r], hls.at[r])
    def h1copy(r):
        return remote(h1.at[r], halo_out.at[r], hss.at[1, r], hrs.at[1, r], (dp, z - 1))

    @pl.when(z >= 2)
    def _():
        for r in range(nhalo):
            h2copy(r).start()
    @pl.when(dn_ok)
    def _():
        for r in range(nhalo):
            h1local(r).start()
    for i in range(n):
        for k in (3, 1, 2, 0):
            ccopy(i, k).start()
    for key, l in last.items():
        for i in l[:2]:
            for k in (3, 1, 2, 0):
                lcopy(i, k).start()

    def zadd(i, j, z_static, up):
        w, r0, r, rows, cols = chunks[i]
        a = col(at(acc, i, 0), i, j)
        add_rows(a, [a, at(rz, i, 0 if up else 1, j)], r)
    def zstage(i, t):
        w, r0, r, rows, cols = chunks[i]
        for up in (True, False):
            @pl.when(z == (t if up else zn - 1 - t))
            def _(up=up):
                zz = t if up else zn - 1 - t
                js = range(zz + 1, zn) if up else range(zz - 1, -1, -1)
                for j in js:
                    if t > 0:
                        zcopy(i, up, j).wait_recv()
                        zadd(i, j, zz, up)
                    zcopy(i, up, j).start()
                if t > 0:
                    zcopy(i, up, zz).wait_recv()
    def final(i):
        w, r0, r, rows, cols = chunks[i]
        o = outs[w].at[pl.ds(r0, r), :]
        for zz in range(zn):
            @pl.when(z == zz)
            def _(zz=zz):
                terms = [col(at(acc, i, 0), i, zz)]
                if zz > 0: terms.append(at(rz, i, 0, zz))
                if zz < zn - 1: terms.append(at(rz, i, 1, zz))
                add_rows(o, terms, r)
    def text_stage(t):
        for up in (True, False):
            @pl.when(z == (t if up else zn - 1 - t))
            def _(up=up):
                zz = t if up else zn - 1 - t
                js = range(zz + 1, zn) if up else range(zz - 1, -1, -1)
                for j in js:
                    if t > 0:
                        tcopy(up, j).wait_recv()
                        a = text.at[:, pl.ds(j * tc, tc)]
                        add_rows(a, [a, tz.at[0 if up else 1, j]], tr)
                    tcopy(up, j).start()
                if t > 0:
                    tcopy(up, zz).wait_recv()
    def text_final():
        for zz in range(zn):
            @pl.when(z == zz)
            def _(zz=zz):
                terms = [text.at[:, pl.ds(zz * tc, tc)]]
                if zz > 0: terms.append(tz.at[0, zz])
                if zz < zn - 1: terms.append(tz.at[1, zz])
                add_rows(text_out, terms, tr)
    def halo_stage(r):
        @pl.when(dn_ok)
        def _():
            h1local(r).wait()
            @pl.when(up_ok)
            def _():
                h2copy(r).wait_recv()
                add_rows(h1.at[r], [h1.at[r], h2.at[r]], h1.shape[1])
            h1copy(r).start()
        @pl.when(z == zn - 1)
        def _():
            pltpu.make_async_copy(hs, halo_out.at[r], hls.at[r]).start()

    def stage_of(s, i):
        w, r0, r, rows, cols = chunks[i]
        if s == 0:
            A = lambda k: at(acc, i, k)
            S = lambda k: staged(i).at[slots[i], k]
            for k in (3, 1, 2, 0):
                ccopy(i, k).wait_recv()
                lcopy(i, k).wait()
                add_rows(A(k), [A(k), S(k)], r)
                if k == 1:
                    dcopy(i, 0).start(); dcopy(i, 1).start()
                if k == 2:
                    xcopy(i, 0, 0).start()
                if k == 0:
                    xcopy(i, 1, 1).start()
            if i in nxt:
                for k in (3, 1, 2, 0):
                    lcopy(nxt[i], k).start()
        elif s == 1:
            dcopy(i, 0).wait_recv()
            a = half(at(acc, i, 2), i, 0)
            add_rows(a, [a, at(rh, i, 0)], r // 2, min(16, r // 2))
            dcopy(i, 1).wait_recv()
            b = half(at(acc, i, 1), i, 1)
            add_rows(b, [b, at(rh, i, 1)], r // 2, min(16, r // 2))
            xcopy(i, 1, 0).start()
            xcopy(i, 0, 1).start()
        elif s == 2:
            for d in range(2):
                for h in range(2):
                    xcopy(i, d, h).wait_recv()
            a = at(acc, i, 0)
            add_rows(a, [a, at(rxy, i, 0), at(rxy, i, 1)], r)
            zstage(i, 0)
        elif s < 2 + zn:
            zstage(i, s - 2)
            if s == 1 + zn:
                final(i)
    for k in range(n + lags[-1]):
        for s, lag in enumerate(lags):
            if 0 <= k - lag < n:
                stage_of(s, k - lag)
        if k == 0:
            hs[...] = jnp.zeros_like(hs)
        if 1 <= k <= zn:
            text_stage(k - 1)
        if k == zn + 1:
            text_final()
        if 2 <= k < 2 + nhalo:
            halo_stage(k - 2)
    for i in range(n):
        for k in range(4):
            ccopy(i, k).wait_send()
        for h in range(2):
            dcopy(i, h).wait_send()
            for d in range(2):
                xcopy(i, d, h).wait_send()
        for j in range(zn):
            @pl.when(up_ok & (j > z))
            def _():
                zcopy(i, True, j).wait_send()
            @pl.when(dn_ok & (j < z))
            def _():
                zcopy(i, False, j).wait_send()
    for j in range(zn):
        @pl.when(up_ok & (j > z))
        def _():
            tcopy(True, j).wait_send()
        @pl.when(dn_ok & (j < z))
        def _():
            tcopy(False, j).wait_send()
    for r in range(nhalo):
        @pl.when(z >= 2)
        def _():
            h2copy(r).wait_send()
        @pl.when(dn_ok)
        def _():
            h1copy(r).wait_send()
        @pl.when(up_ok)
        def _():
            h1copy(r).wait_recv()
        @pl.when(z == zn - 1)
        def _():
            pltpu.make_async_copy(hs, halo_out.at[r], hls.at[r]).wait()

def scatter(grads, text, halo, dpn, zn, cid=1, lags=(0, 1, 2, 3, 4, 5)):
    shapes = tuple((g.shape[0] // dpn, g.shape[1] // zn) for g in grads)
    chunks = pieces_of(shapes)
    n = len(chunks)
    cnt = [sum(c[0] == w for c in chunks) for w in range(len(shapes))]
    rr = [next(c[2] for c in chunks if c[0] == w) for w in range(len(shapes))]
    kinds = sorted({(r, s[1]) for r, s in zip(rr, shapes)})
    D = pltpu.SemaphoreType.DMA
    V = pltpu.VMEM
    T = halo.shape
    tr, tc = text.shape[0], text.shape[1] // zn
    scratch = [V((cnt[w], 4, rr[w], zn * shapes[w][1]), BF) for w in range(len(shapes))]
    scratch += [V((cnt[w], 2, rr[w] // 2, zn * shapes[w][1]), BF) for w in range(len(shapes))]
    scratch += [V((cnt[w], 2, rr[w], zn * shapes[w][1]), BF) for w in range(len(shapes))]
    scratch += [V((cnt[w], 2, zn, rr[w], shapes[w][1]), BF) for w in range(len(shapes))]
    scratch += [V((2, 4, r, zn * c), BF) for r, c in kinds]
    scratch += [V((2, zn, tr, tc), BF), V((T[0],) + T[2:], BF), V((T[0],) + T[2:], BF), V(T[2:], BF)]
    scratch += [D((len(kinds), 2, 4)), D((n, 4)), D((n, 4)), D((n, 2)), D((n, 2)), D((n, 2, 2)), D((n, 2, 2)), D((n, 2, zn)), D((n, 2, zn)),
                D((2, zn)), D((2, zn)), D((T[0],)), D((2, T[0])), D((2, T[0]))]
    VM = pl.BlockSpec(memory_space=pltpu.VMEM)
    return pl.pallas_call(
        functools.partial(scatter_kernel, shapes, T[0], zn, lags),
        out_shape=[jax.ShapeDtypeStruct(s, F32) for s in shapes] + [jax.ShapeDtypeStruct((tr, tc), F32), jax.ShapeDtypeStruct((T[0],) + T[2:], BF)],
        in_specs=[ANY] * len(shapes) + [VM, ANY],
        out_specs=[VM] * (len(shapes) + 1) + [ANY],
        scratch_shapes=scratch,
        compiler_params=pltpu.CompilerParams(collective_id=cid, has_side_effects=True, vmem_limit_bytes=60 << 20),
        name="scatter",
    )(*grads, text, halo)

HEAD = 64
SCALE = 0.125
MASKED = -1e9

def dot(a, b, ca, cb):
    return lax.dot_general(a, b, (((ca,), (cb,)), ((), ())), preferred_element_type=F32)

def lane_is(shape, h):
    lanes = lax.broadcasted_iota(jnp.int32, shape, 1)
    return (lanes < HEAD) if h == 0 else (lanes >= HEAD)

def self_allowed(q_ids, k_ids, back):
    nq, nk = q_ids.shape[0], k_ids.shape[1]
    qi = lax.broadcasted_iota(jnp.int32, (nq, nk), 0)
    ki = lax.broadcasted_iota(jnp.int32, (nq, nk), 1)
    return (q_ids == k_ids) & (ki <= qi + back)

def self_forward_kernel(qs, ks, q, k, v, o, lse, bias):
    nq, nk = q.shape[1], k.shape[1]
    @pl.when(pl.program_id(1) == 0)
    def _():
        bias[...] = jnp.where(self_allowed(qs[0], ks[0], nk - nq), 0.0, MASKED)
    q2, k2, v2 = q[0], k[0], v[0]
    outs, totals = [], []
    for h in range(2):
        mine = lane_is(q2.shape, h)
        qh = jnp.where(mine, q2 * jnp.asarray(SCALE, BF), jnp.zeros_like(q2))
        s = dot(qh, k2, 1, 1) + bias[...]
        top = jnp.max(s, axis=1, keepdims=True)
        p = jnp.exp(s - top)
        total = jnp.sum(p, axis=1, keepdims=True)
        outs.append(dot(p.astype(BF), v2, 1, 0) / total)
        totals.append(jnp.broadcast_to(top + jnp.log(total), q2.shape))
    first = lane_is(q2.shape, 0)
    o[0] = jnp.where(first, outs[0], outs[1]).astype(BF)
    lse[0] = jnp.where(first, totals[0], totals[1])

def self_backward_kernel(qs, ks, q, k, v, lse, do, dq, dk, dv, bias):
    nq, nk = q.shape[1], k.shape[1]
    @pl.when(pl.program_id(1) == 0)
    def _():
        bias[...] = jnp.where(self_allowed(qs[0], ks[0], nk - nq), 0.0, MASKED)
    q2, k2, v2, d2 = q[0], k[0], v[0], do[0]
    gq, gk, gv = [], [], []
    for h in range(2):
        mine = lane_is(q2.shape, h)
        zero = jnp.zeros_like(q2)
        qh = jnp.where(mine, q2 * jnp.asarray(SCALE, BF), zero)
        dh = jnp.where(mine, d2, zero)
        s = dot(qh, k2, 1, 1) + bias[...]
        p = jnp.exp(s - lse[0][:, h * HEAD:h * HEAD + 1])
        dp = dot(dh, v2, 1, 1)
        inner = jnp.sum(p * dp, axis=1, keepdims=True)
        ds = (p * (dp - inner)).astype(BF)
        gq.append(dot(ds, k2, 1, 0) * SCALE)
        gk.append(dot(ds, qh, 0, 0))
        gv.append(dot(p.astype(BF), dh, 0, 0))
    dq[0] = jnp.where(lane_is(q2.shape, 0), gq[0], gq[1]).astype(BF)
    dk[0] = (gk[0] + gk[1]).astype(BF)
    dv[0] = (gv[0] + gv[1]).astype(BF)

def specs(nq, nk):
    qb = pl.BlockSpec((1, nq, 128), lambda r, p: (r, 0, p))
    kb = pl.BlockSpec((1, nk, 128), lambda r, p: (r, 0, p))
    qid = pl.BlockSpec((1, nq, 1), lambda r, p: (r, 0, 0))
    kid = pl.BlockSpec((1, 1, nk), lambda r, p: (r, 0, 0))
    return qb, kb, qid, kid

def self_forward(q, k, v, q_ids, k_ids):
    rows, nq, width = q.shape
    nk = k.shape[1]
    qb, kb, qid, kid = specs(nq, nk)
    return pl.pallas_call(
        self_forward_kernel, grid=(rows, width // 128),
        in_specs=[qid, kid, qb, kb, kb], out_specs=[qb, qb],
        out_shape=[jax.ShapeDtypeStruct(q.shape, BF), jax.ShapeDtypeStruct(q.shape, F32)],
        scratch_shapes=[pltpu.VMEM((nq, nk), F32)], name="self_attention",
    )(q_ids[:, :, None], k_ids[:, None, :], q, k, v)

def self_backward(q, k, v, lse, do, q_ids, k_ids):
    rows, nq, width = q.shape
    nk = k.shape[1]
    qb, kb, qid, kid = specs(nq, nk)
    return pl.pallas_call(
        self_backward_kernel, grid=(rows, width // 128),
        in_specs=[qid, kid, qb, kb, kb, qb, qb], out_specs=[qb, kb, kb],
        out_shape=[jax.ShapeDtypeStruct(q.shape, BF), jax.ShapeDtypeStruct(k.shape, BF), jax.ShapeDtypeStruct(k.shape, BF)],
        scratch_shapes=[pltpu.VMEM((nq, nk), F32)], name="self_attention_back",
    )(q_ids[:, :, None], k_ids[:, None, :], q, k, v, lse, do)

def pair_keys(k2):
    first = lane_is(k2.shape, 0)
    zero = jnp.zeros_like(k2)
    return jnp.concatenate([jnp.where(first, k2, zero), jnp.where(first, zero, k2)], axis=0)

def halves(values, tokens, reduce, fill):
    left = lax.broadcasted_iota(jnp.int32, values.shape, 1) < tokens
    a = reduce(jnp.where(left, values, fill), axis=1, keepdims=True)
    b = reduce(jnp.where(left, fill, values), axis=1, keepdims=True)
    return jnp.where(left, a, b)

def cross_shares(q2, kk, ids_q, ids_k, tokens):
    s = dot(q2 * jnp.asarray(SCALE, BF), kk, 1, 1)
    s = jnp.where(ids_q == ids_k, s, MASKED)
    p = jnp.exp(s - halves(s, tokens, jnp.max, MASKED))
    return p / halves(p, tokens, jnp.sum, 0.0)

def cross_forward_kernel(qs, ks, q, k, v, o):
    tokens = k.shape[1]
    p = cross_shares(q[0], pair_keys(k[0]), qs[0], ks[0], tokens)
    o[0] = dot(p.astype(BF), pair_keys(v[0]), 1, 0).astype(BF)

def cross_backward_kernel(qs, ks, q, k, v, do, dq, dk, dv):
    tokens = k.shape[1]
    q2, d2 = q[0], do[0]
    kk, vv = pair_keys(k[0]), pair_keys(v[0])
    p = cross_shares(q2, kk, qs[0], ks[0], tokens)
    dp = dot(d2, vv, 1, 1)
    ds = (p * (dp - halves(p * dp, tokens, jnp.sum, 0.0))).astype(BF)
    dq[0] = (dot(ds, kk, 1, 0) * SCALE).astype(BF)
    gk = dot(ds, q2, 0, 0) * SCALE
    gv = dot(p.astype(BF), d2, 0, 0)
    first = lane_is((tokens, 128), 0)
    dk[0] = jnp.where(first, gk[:tokens], gk[tokens:]).astype(BF)
    dv[0] = jnp.where(first, gv[:tokens], gv[tokens:]).astype(BF)

def cross_specs(nq, nk):
    qb, kb, qid, _ = specs(nq, nk)
    return qb, kb, qid, pl.BlockSpec((1, 1, 2 * nk), lambda r, p: (r, 0, 0))

def cross_forward(q, k, v, q_ids, k_ids):
    rows, nq, width = q.shape
    qb, kb, qid, kid = cross_specs(nq, k.shape[1])
    return pl.pallas_call(
        cross_forward_kernel, grid=(rows, width // 128),
        in_specs=[qid, kid, qb, kb, kb], out_specs=qb,
        out_shape=jax.ShapeDtypeStruct(q.shape, BF), name="cross_attention",
    )(q_ids[:, :, None], jnp.concatenate([k_ids, k_ids], axis=1)[:, None, :], q, k, v)

def cross_backward(q, k, v, do, q_ids, k_ids):
    rows, nq, width = q.shape
    qb, kb, qid, kid = cross_specs(nq, k.shape[1])
    return pl.pallas_call(
        cross_backward_kernel, grid=(rows, width // 128),
        in_specs=[qid, kid, qb, kb, kb, qb], out_specs=[qb, kb, kb],
        out_shape=[jax.ShapeDtypeStruct(q.shape, BF), jax.ShapeDtypeStruct(k.shape, BF), jax.ShapeDtypeStruct(k.shape, BF)],
        name="cross_attention_back",
    )(q_ids[:, :, None], jnp.concatenate([k_ids, k_ids], axis=1)[:, None, :], q, k, v, do)

EPS = 1e-05
W = 1024
SLAB = 128
PACE_F = 10.0
VEC = 16

class Names:
    def __init__(self, names, refs):
        for n, r in zip(names, refs, strict=True):
            setattr(self, n, r)

def barrier_with(peers):
    sem = pltpu.get_barrier_semaphore()
    total = 0
    for who, zz, ok in peers:
        def send(who=who, zz=zz):
            pl.semaphore_signal(sem, inc=1, device_id=(who, zz), device_id_type=MESH)
        if ok is None:
            send()
            total = total + 1
        else:
            pl.when(ok)(send)
            total = total + ok.astype(jnp.int32)
    pl.semaphore_wait(sem, total)

def blocks(rows, step, body):
    @pl.loop(0, rows // step)
    def _(q):
        body(pl.ds(pl.multiple_of(q * step, step), step))

def tiles(width, tile, body):
    @pl.loop(0, width // tile)
    def _(n):
        body(n, pl.ds(pl.multiple_of(n * tile, tile), tile))

def lanes_at(n, size, offset=0):
    return pl.ds(pl.multiple_of(n, 128) + offset if offset else pl.multiple_of(n, 128), size)

def standard(v):
    centred = v - jnp.mean(v, axis=-1, keepdims=True)
    scale = lax.rsqrt(jnp.mean(centred * centred, axis=-1, keepdims=True) + EPS)
    return centred * scale, scale

def gelu_pair(u):
    half_erf = 0.5 * (1.0 + lax.erf(u * 0.7071067811865476))
    return u * half_erf, half_erf + u * (0.3989422804014327 * jnp.exp(-0.5 * u * u))

def column(row):
    return jnp.broadcast_to(row, (8, row.shape[1])).T[:, :1]

def stack_heads(v):
    zero, first = jnp.zeros_like(v), lane_is(v.shape, 0)
    return jnp.concatenate([jnp.where(first, v, zero), jnp.where(first, zero, v)], axis=0)

def pick_heads(v):
    n = v.shape[0] // 2
    return jnp.where(lane_is((n, v.shape[1]), 0), v[:n], v[n:])

def mask_keys(q_row, k_row, back):
    k, q = column(k_row), q_row
    shape = (k.shape[0], q.shape[1])
    ki, qi = lax.broadcasted_iota(jnp.int32, shape, 0), lax.broadcasted_iota(jnp.int32, shape, 1)
    n = shape[1] // 2
    qi = jnp.where(qi >= n, qi - n, qi)
    return jnp.where((k == q) & (ki <= qi + back), 0.0, MASKED)

class Pump:
    def __init__(self, step, count, pace):
        self.step, self.count, self.pace, self.next, self.spent = step, count, pace, 0, 0.0
    def upto(self, k):
        while self.next <= min(k, self.count - 1):
            self.step(self.next)
            self.next += 1
    def work(self, cost):
        self.spent += cost
        while self.spent >= self.pace:
            self.spent -= self.pace
            self.upto(self.next)

F_IN = ["q_w", "k_w", "v_w", "o_w", "cq_w", "ck_w", "cv_w", "co_w", "fi_w", "fo_w", "vecs", "hidden", "text", "cot", "q_ids", "k_ids", "t_ids"]
F_OUT = ["weights", "gains", "halo", "first", "q", "k", "v", "lse", "mixed", "after_self", "second", "cq", "tk", "tv", "cmix", "after_cross", "third", "pre_grad", "fo_grad", "block"]
F_SCR = ["s_halo", "s_pool", "s_q", "s_mixed", "s_lse", "s_as", "s_second", "s_cq", "s_tk", "s_tv", "s_cmix", "s_ac", "s_third", "s_act", "s_w", "s_fog", "s_bias", "s_vec", "s_gain", "s_out",
         "lsem", "zs", "zr", "xs", "xr", "fs", "fr", "cs", "cr", "hs", "hr", "ws", "save", "fogs"]

def forward_kernel(zn, rows, frames, *refs):
    r_ = Names(F_IN + F_OUT + F_SCR, refs)
    T, E = rows * frames, 3 * frames
    heads2 = W // 128
    dp, z, core, x, y = place()
    xn = dp + 2 - 4 * x
    yn = dp + 4 - 8 * y
    dn = yn + 2 - 4 * x
    cn = dp + 1 - 2 * core
    up_ok, dn_ok = z < zn - 1, z > 0
    order = [VEC] + list(range(16))
    n = len(order)
    barrier_with([(xn, z, None), (yn, z, None), (cn, z, None), (dp, z + 1, up_ok), (dp, z - 1, dn_ok)])

    def own(i):
        if i == VEC:
            return r_.vecs
        if i < 8:
            return refs[i]
        if i < 12:
            return r_.fi_w.at[:, pl.ds((i - 8) * 256, 256)]
        return r_.fo_w.at[pl.ds((i - 12) * SLAB, SLAB), :]
    def slab(i, who, half=None):
        base = r_.s_vec if i == VEC else r_.weights.at[i]
        size = 16 if i == VEC else SLAB
        if half is None:
            return base.at[pl.ds(pl.multiple_of(who * size, size), size), :]
        h = size // 2
        return base.at[pl.ds(pl.multiple_of(who * size + half * h, h), h), :]
    def block(i, who, j):
        base = r_.s_vec if i == VEC else r_.weights.at[i]
        size, cols = (16, 128) if i == VEC else (SLAB, 256)
        return base.at[pl.ds(pl.multiple_of(who * size, size), size), pl.ds(pl.multiple_of(j * cols, cols), cols)]
    def remote(a, b, s, r, dev):
        return pltpu.make_async_remote_copy(a, b, s, r, device_id=dev, device_id_type=MESH)
    def zcopy(i, j, up, first=False):
        a = own(i) if first else block(i, dp, j)
        return remote(a, block(i, dp, j), r_.zs.at[i, 0 if up else 1, j], r_.zr.at[i, j], (dp, z + 1 if up else z - 1))
    def xcopy(i, d):
        return remote(slab(i, dp), slab(i, dp), r_.xs.at[i, d], r_.xr.at[i, d], ((xn, yn)[d], z))
    def xrecv(i, d):
        who = (xn, yn)[d]
        return remote(slab(i, who), slab(i, who), r_.xs.at[i, d], r_.xr.at[i, d], (who, z))
    def fcopy(i, half):
        who, to = (xn, yn) if half == 0 else (yn, xn)
        return remote(slab(i, who, half), slab(i, who, half), r_.fs.at[i, half], r_.fr.at[i, half], (to, z))
    def frecv(i, half):
        return remote(slab(i, dn, half), slab(i, dn, half), r_.fs.at[i, half], r_.fr.at[i, half], (yn, z))
    def ccopy(i, k):
        who = (dp, xn, yn, dn)[k]
        return remote(slab(i, who), slab(i, who), r_.cs.at[i, k], r_.cr.at[i, k], (cn, z))
    def crecv(i, k):
        who = (dp, xn, yn, dn)[k] + 1 - 2 * core
        return remote(slab(i, who), slab(i, who), r_.cs.at[i, k], r_.cr.at[i, k], (cn, z))
    def lcopy(i):
        return pltpu.make_async_copy(own(i), block(i, dp, z), r_.lsem.at[i])
    def hcopy(r, hop):
        a = r_.s_halo.at[r, 1] if hop else r_.hidden.at[pl.ds(r * frames, frames), :]
        return remote(a, r_.s_halo.at[r, 1 - hop], r_.hs.at[hop, r], r_.hr.at[hop, r], (dp, z + 1))
    def begin(i):
        @pl.when(up_ok)
        def _():
            zcopy(i, z, True, True).start()
        @pl.when(dn_ok)
        def _():
            zcopy(i, z, False, True).start()
        lcopy(i).start()
    def zstage(i, t):
        @pl.when(z - t >= 0)
        def _():
            zcopy(i, z - t, True).wait_recv()
            @pl.when(up_ok)
            def _():
                zcopy(i, z - t, True).start()
        @pl.when(z + t < zn)
        def _():
            zcopy(i, z + t, False).wait_recv()
            @pl.when(dn_ok)
            def _():
                zcopy(i, z + t, False).start()
    done = {i: 0 for i in order}
    def advance(i, s):
        while done[i] < s:
            done[i] += 1
            t = done[i]
            if t < zn - 1:
                zstage(i, t)
            elif t == zn - 1:
                zstage(i, t)
                lcopy(i).wait()
                xcopy(i, 0).start(); xcopy(i, 1).start(); ccopy(i, 0).start()
            elif t == zn:
                for d in range(2):
                    xrecv(i, d).wait_recv()
                    fcopy(i, d).start(); ccopy(i, 1 + d).start()
            elif t == zn + 1:
                frecv(i, 0).wait_recv(); frecv(i, 1).wait_recv()
                ccopy(i, 3).start()
            else:
                for k in range(4):
                    crecv(i, k).wait_recv()
    LAST = zn + 2
    lags = (0, 1, 2, 4, 6, 7)
    AHEAD = 6
    def halo_step(k):
        for r in range(rows):
            if k == 2 * r:
                @pl.when(up_ok)
                def _():
                    hcopy(r, 0).start()
            if k == 2 * r + 4:
                @pl.when(dn_ok)
                def _():
                    hcopy(r, 0).wait_recv()
                    @pl.when(up_ok)
                    def _():
                        hcopy(r, 1).start()
    def step(k):
        if k + AHEAD < n:
            begin(order[k + AHEAD])
        for s, lag in enumerate(lags):
            if 0 <= k - lag < n:
                advance(order[k - lag], s + 1)
        halo_step(k)
    pump = Pump(step, n + lags[-1], PACE_F)
    def need(i):
        a = order.index(i)
        pump.upto(a + 7)
        advance(i, LAST)
    SLOTS = 3
    def load(i, slot):
        need(i)
        c = pltpu.make_async_copy(r_.weights.at[i], r_.s_w.at[slot], r_.ws.at[slot])
        c.start()
        return c
    for a in range(AHEAD):
        begin(order[a])

    saves = []
    def save(src, dst):
        c = pltpu.make_async_copy(src, dst, r_.save.at[len(saves)])
        c.start()
        saves.append(c)
        return c
    waited = set()
    def settle(c):
        if id(c) not in waited:
            c.wait()
            waited.add(id(c))

    def dense(lhs, slot, emit, tile=512):
        tiles(W, tile, lambda m, c: emit(m, c, dot(lhs(), r_.s_w[slot, :, c], 1, 0)))
    def gain(k):
        return r_.s_gain[k:k + 1, :]
    def norm(src, dst, at_src, at_dst, g):
        v = src[pl.ds(at_src, frames), :].astype(F32)
        dst[pl.ds(at_dst, frames), :] = (standard(v)[0] * gain(g) + gain(g + 1)).astype(BF)
    def norm_all(src, dst, g):
        pl.loop(0, rows)(lambda r: norm(src, dst, pl.multiple_of(r * frames, frames), pl.multiple_of(r * frames, frames), g))

    FIRST, KEY, VAL = 0, rows * E, 2 * rows * E
    pool = r_.s_pool
    @pl.when(z == 0)
    def _():
        r_.s_halo[:, 1] = jnp.zeros((rows, frames, W), BF)
    @pl.when(z <= 1)
    def _():
        r_.s_halo[:, 0] = jnp.zeros((rows, frames, W), BF)

    need(VEC)
    share = W // (8 * zn)
    for d in range(8):
        g = r_.s_vec[pl.ds(d * 16, 16), :].astype(F32)
        total = g[:, :128]
        for j in range(1, zn):
            total = total + pltpu.roll(g[:, j * 128:(j + 1) * 128], j * share, 1)
        r_.s_gain[:, d * 128:(d + 1) * 128] = total
    r_.gains[...] = r_.s_gain[...]
    for r in range(rows):
        norm(r_.hidden, pool, r * frames, FIRST + r * E + 2 * frames, 0)
    pump.work(6)
    load(0, 0).wait()
    for r in range(rows):
        def emit(m, c, v, r=r):
            r_.s_q[pl.ds(r * frames, frames), c] = v.astype(BF)
        dense(lambda r=r: pool[pl.ds(FIRST + r * E + 2 * frames, frames), :], 0, emit)
    save(r_.s_q, r_.q)
    pump.work(2.5)
    kc = load(1, 1)
    vc = load(2, 2)
    kc.wait(); vc.wait()

    def attend(r):
        r_.s_bias[...] = mask_keys(r_.q_ids[r], r_.k_ids[r], E - frames)
        def pair(p):
            c = pl.ds(pl.multiple_of(p * 128, 128), 128)
            rq = pl.ds(r * frames, frames)
            qs = stack_heads(r_.s_q[rq, c] * jnp.asarray(SCALE, BF))
            s = dot(pool[pl.ds(KEY + r * E, E), c], qs, 1, 1) + r_.s_bias[...]
            top = jnp.max(s, axis=0, keepdims=True)
            sh = jnp.exp(s - top)
            total = jnp.sum(sh, axis=0, keepdims=True)
            out = dot((sh / total).astype(BF), pool[pl.ds(VAL + r * E, E), c], 0, 0)
            r_.s_mixed[rq, c] = pick_heads(out).astype(BF)
            r_.s_lse[r, pl.ds(p, 1), :] = top + jnp.log(total)
        for part in range(4):
            pl.loop(part * heads2 // 4, (part + 1) * heads2 // 4)(pair)
            pump.work(2.6)

    for r in range(rows):
        pump.upto(2 * r + 4)
        @pl.when(z >= 2)
        def _():
            hcopy(r, 1).wait_recv()
        for c in range(2):
            norm(r_.s_halo.at[r, c], pool, 0, FIRST + r * E + c * frames, 0)
        save(r_.s_halo.at[r], r_.halo.at[r])
        save(pool.at[pl.ds(FIRST + r * E, E), :], r_.first.at[pl.ds(r * E, E), :])
        for base, slot in ((KEY, 1), (VAL, 2)):
            def emit(m, c, v, base=base, r=r):
                pool[pl.ds(base + r * E, E), c] = v.astype(BF)
            dense(lambda r=r: pool[pl.ds(FIRST + r * E, E), :], slot, emit)
            save(pool.at[pl.ds(base + r * E, E), :], (r_.k if base == KEY else r_.v).at[pl.ds(r * E, E), :])
        pump.work(5.5)
        if r == rows - 1:
            c3, c4, c5 = load(3, 0), load(4, 1), load(5, 2)
        attend(r)
    save(r_.s_mixed, r_.mixed); save(r_.s_lse, r_.lse)

    c3.wait()
    def emit(m, c, v):
        r_.s_as[:, c] = r_.hidden[:, c].astype(F32) + v
    dense(lambda: r_.s_mixed[...], 0, emit)
    pump.work(2.2)
    c6 = load(6, 0)
    norm_all(r_.s_as, r_.s_second, 2)
    save(r_.s_as, r_.after_self); save(r_.s_second, r_.second)
    pump.work(1.5)
    c4.wait()
    def emit(m, c, v):
        r_.s_cq[:, c] = v.astype(BF)
    dense(lambda: r_.s_second[...], 1, emit)
    save(r_.s_cq, r_.cq)
    pump.work(2.2)
    c7 = load(7, 1)
    for ready, slot, dst, out in ((c5, 2, r_.s_tk, r_.tk), (c6, 0, r_.s_tv, r_.tv)):
        ready.wait()
        def emit(m, c, v, dst=dst):
            dst[:, c] = v.astype(BF)
        dense(lambda: r_.text[...], slot, emit)
        save(dst, out)
        pump.work(1)
    c8 = load(8, 2)
    tokens = r_.text.shape[0] // rows
    for r in range(rows):
        def pair(p, r=r):
            c = pl.ds(pl.multiple_of(p * 128, 128), 128)
            rq, rk = pl.ds(r * frames, frames), pl.ds(r * tokens, tokens)
            sh = cross_shares(r_.s_cq[rq, c], pair_keys(r_.s_tk[rk, c]), ids, r_.t_ids[r], tokens)
            r_.s_cmix[rq, c] = dot(sh.astype(BF), pair_keys(r_.s_tv[rk, c]), 1, 0).astype(BF)
        ids = column(r_.q_ids[r][:, :frames])
        pl.loop(0, heads2)(pair)
        pump.work(3.7)
    save(r_.s_cmix, r_.cmix)
    c9 = load(9, 0)
    c7.wait()
    def emit(m, c, v):
        r_.s_ac[:, c] = r_.s_as[:, c] + v
    dense(lambda: r_.s_cmix[...], 1, emit)
    pump.work(2.2)
    norm_all(r_.s_ac, r_.s_third, 4)
    save(r_.s_ac, r_.after_cross); save(r_.s_third, r_.third)
    pump.work(1.5)

    for c in saves:
        settle(c)
    SLOPE, PRE = 0, 4 * T
    ready = {8: (2, c8), 9: (0, c9)}
    for i in range(4):
        if i == 0:
            ready[10] = (1, load(10, 1))
        slot, c = ready[8 + i]
        c.wait()
        def emit(m, c, v, i=i):
            act, slope = gelu_pair(v)
            for u in range(4):
                to = (i % 2) * 2 + u % 2
                lanes = pl.ds(pl.multiple_of((2 * (2 * m + u // 2) + i // 2) * 128, 128), 128)
                part = slice(u * 128, (u + 1) * 128)
                r_.s_act[to, :, lanes] = act[:, part].astype(BF)
                pool[pl.ds(SLOPE + to * T, T), lanes] = slope[:, part].astype(BF)
        dense(lambda: r_.s_third[...], slot, emit)
        pump.work(3.6)
        if i < 2:
            ready[11 + i] = (slot, load(11 + i, slot))
    fog = []
    def out_grad(i):
        def body(m, c):
            r_.s_fog[i % 2, c, :] = dot(r_.s_act[i, :, c], r_.cot[...], 0, 0).astype(BF)
        if i >= 2:
            fog[i - 2].wait()
        tiles(W, 512, body)
        g = pltpu.make_async_copy(r_.s_fog.at[i % 2], r_.fo_grad.at[i], r_.fogs.at[i])
        g.start()
        fog.append(g)
        pump.work(2.8)
    out_grad(0); out_grad(1)
    ready[13] = (1, load(13, 1))
    out_grad(2); out_grad(3)
    ready[14] = (2, load(14, 2))
    for i in range(4):
        slot, c = ready[12 + i]
        c.wait()
        def emit(m, c, v):
            r_.s_ac[:, c] = r_.s_ac[:, c] + v
        dense(lambda i=i: r_.s_act[i], slot, emit)
        def body(m, c, i=i, slot=slot):
            v = dot(r_.cot[...], r_.s_w[slot, c, :], 1, 1)
            v = v * pool[pl.ds(SLOPE + i * T, T), c].astype(F32)
            for u in range(4):
                to = (u % 2) * 2 + i // 2
                lanes = pl.ds(pl.multiple_of((2 * m + u // 2) * 256, 256) + (i % 2) * 128, 128)
                pool[pl.ds(PRE + to * T, T), lanes] = v[:, u * 128:(u + 1) * 128].astype(BF)
        tiles(W, 512, body)
        pump.work(4.4)
        if i == 0:
            ready[15] = (slot, load(15, slot))
    def body(s):
        r_.s_out[s, :] = r_.s_ac[s, :].astype(BF)
    blocks(T, frames, body)
    save(r_.s_out, r_.block)
    for i in range(4):
        save(pool.at[pl.ds(PRE + i * T, T), :], r_.pre_grad.at[i])

    pump.upto(pump.count)
    for i in order:
        advance(i, LAST)
    for c in fog[2:]:
        c.wait()
    for c in saves:
        settle(c)
    for r in range(rows):
        @pl.when(up_ok)
        def _():
            hcopy(r, 0).wait_send()
        @pl.when(up_ok & dn_ok)
        def _():
            hcopy(r, 1).wait_send()
    for i in order:
        for j in range(zn):
            @pl.when(up_ok & (j <= z))
            def _():
                zcopy(i, j, True).wait_send()
            @pl.when(dn_ok & (j >= z))
            def _():
                zcopy(i, j, False).wait_send()
        for k in range(2):
            xcopy(i, k).wait_send(); fcopy(i, k).wait_send()
        for k in range(4):
            ccopy(i, k).wait_send()

def forward(weights, vecs, hidden, text, cot, q_ids, k_ids, t_ids, zn, rows, frames, cid=2):
    T, E = rows * frames, 3 * frames
    S = jax.ShapeDtypeStruct
    D, V = pltpu.SemaphoreType.DMA, pltpu.VMEM
    VM = pl.BlockSpec(memory_space=pltpu.VMEM)
    tok = text.shape[0]
    outs = dict(weights=S((16, W, W), BF), gains=S((16, W), F32), halo=S((rows, 2, frames, W), BF), first=S((rows * E, W), BF), q=S((T, W), BF), k=S((rows * E, W), BF),
                v=S((rows * E, W), BF), lse=S((rows, W // 128, 2 * frames), F32), mixed=S((T, W), BF), after_self=S((T, W), F32), second=S((T, W), BF), cq=S((T, W), BF), tk=S((tok, W), BF), tv=S((tok, W), BF),
                cmix=S((T, W), BF), after_cross=S((T, W), F32), third=S((T, W), BF), pre_grad=S((4, T, W), BF), fo_grad=S((4, W, W), BF), block=S((T, W), BF))
    scratch = [V((rows, 2, frames, W), BF), V((3 * rows * E, W), BF), V((T, W), BF), V((T, W), BF), V((rows, W // 128, 2 * frames), F32), V((T, W), F32), V((T, W), BF), V((T, W), BF), V((tok, W), BF), V((tok, W), BF),
               V((T, W), BF), V((T, W), F32), V((T, W), BF), V((4, T, W), BF), V((3, W, W), BF), V((2, W, W), BF), V((E, 2 * frames), F32), V((128, 512), BF), V((16, W), F32), V((T, W), BF)]
    n = 17
    scratch += [D((n,)), D((n, 2, zn)), D((n, zn)), D((n, 2)), D((n, 2)), D((n, 2)), D((n, 2)), D((n, 4)), D((n, 4)), D((2, rows)), D((2, rows)), D((3,)), D((48,)), D((4,))]
    result = pl.pallas_call(
        functools.partial(forward_kernel, zn, rows, frames),
        out_shape=[outs[k] for k in F_OUT],
        in_specs=[VM] * len(F_IN), out_specs=[VM if k == "gains" else ANY for k in F_OUT],
        scratch_shapes=scratch,
        compiler_params=pltpu.CompilerParams(collective_id=cid, has_side_effects=True, vmem_limit_bytes=62 << 20),
        name="forward",
    )(*weights, vecs, hidden, text, cot, q_ids, k_ids, t_ids)
    return dict(zip(F_OUT, result))

SLOTS_G, SLOTS_A = 3, 8
PACE_B, PACE_TAIL = 10.0, 20.0
LAGS_B = (0, 1, 3, 4, 5, 6, 7)

def add_rows(dst, terms, rows, step=64):
    step = min(step, rows)
    @pl.loop(0, rows // step)
    def _(q):
        s = pl.ds(pl.multiple_of(q * step, step), step)
        total = terms[0][s, :].astype(F32)
        for t in terms[1:]:
            total = total + t[s, :].astype(F32)
        dst[s, :] = total.astype(dst.dtype)

def fold(v):
    return jnp.sum(v.reshape(v.shape[0] // 8, 8, v.shape[1]), axis=0)

B_IN = ["gains", "q_ids", "k_ids", "t_ids", "text",
        "hidden", "cot", "weights", "halo", "first", "q", "k", "v", "lse", "mixed", "after_self", "second", "cq", "tk", "tv", "cmix", "after_cross", "third", "pre_grad", "fo_grad"]
B_IN_VMEM = 5
B_OUT = ["g_q", "g_k", "g_v", "g_o", "g_cq", "g_ck", "g_cv", "g_co", "g_fi", "g_fo", "g_vec", "g_text", "g_hidden"]
B_SCR = ["p", "fa", "fb", "fc", "w", "g", "acc", "rh", "rxy", "rz", "vg", "vacc", "vrh", "vrxy", "vrz", "t", "tsrc", "trz", "h2s", "h2l", "h1", "hb", "hal", "bias", "lse_s", "sums",
         "cs", "cr", "ds", "dr", "xs", "xr", "zs", "zr", "ts", "tr", "hs", "hr", "credit", "ld", "ws", "outsem"]

def backward_kernel(zn, rows, frames, *refs):
    r_ = Names(B_IN + B_OUT + B_SCR, refs)
    T, E = rows * frames, 3 * frames
    heads2 = W // 128
    dp, z, core, x, y = place()
    xn = dp + 2 - 4 * x
    yn = dp + 4 - 8 * y
    dn = yn + 2 - 4 * x
    flip = 1 - 2 * core
    cn = dp + flip
    up_ok, dn_ok = z < zn - 1, z > 0
    peers = [(xn, z, None), (yn, z, None), (cn, z, None), (dp, z + 1, up_ok), (dp, z - 1, dn_ok)]
    barrier_with(peers)
    order = [12, 13, 14, 15, 8, 9, 10, 11, 7, 4, 5, 6, 3, 1, 2, 0, VEC]
    place_of = {i: a for a, i in enumerate(order)}
    fam = (dp, xn, yn, dn)

    def size(i):
        return (16, 128) if i == VEC else (SLAB, 256)
    def g(i):
        return r_.vg if i == VEC else r_.g.at[place_of[i] % SLOTS_G]
    def buf(i, big, small, *rest):
        base = small if i == VEC else big.at[place_of[i] % SLOTS_A]
        return base.at[rest] if rest else base
    def acc(i, k):
        return buf(i, r_.acc, r_.vacc, k)
    def gslab(i, who):
        s = size(i)[0]
        return g(i).at[pl.ds(pl.multiple_of(who * s, s), s), :]
    def remote(a, b, s, r, dev):
        return pltpu.make_async_remote_copy(a, b, s, r, device_id=dev, device_id_type=MESH)
    def ccopy(i, k):
        return remote(gslab(i, fam[k] + flip), acc(i, k), r_.cs.at[i, k], r_.cr.at[i, k], (cn, z))
    def half(ref, i, h):
        n = size(i)[0] // 2
        return ref.at[pl.ds(h * n, n), :]
    def dcopy(i, h):
        return remote(half(acc(i, 3), i, h), buf(i, r_.rh, r_.vrh, h), r_.ds.at[i, h], r_.dr.at[i, h], ((xn, yn)[h], z))
    def xcopy(i, d, h):
        return remote(half(acc(i, 1 + d), i, h), half(buf(i, r_.rxy, r_.vrxy, d), i, h), r_.xs.at[i, d, h], r_.xr.at[i, d, h], ((xn, yn)[d], z))
    def col(ref, i, j):
        c = size(i)[1]
        return ref.at[:, pl.ds(j * c, c)]
    def landing(up, zz, j):
        return j - zz if up else zn - zz + j
    def zcopy(i, up, zz, j):
        to = zz + 1 if up else zz - 1
        return remote(col(acc(i, 0), i, j), buf(i, r_.rz, r_.vrz, landing(up, to, j)), r_.zs.at[i, 0 if up else 1, j], r_.zr.at[i, 0 if up else 1, j], (dp, to))
    def zrecv(i, up, zz, j):
        b = buf(i, r_.rz, r_.vrz, landing(up, zz, j))
        return remote(b, b, r_.zs.at[i, 0 if up else 1, j], r_.zr.at[i, 0 if up else 1, j], (dp, zz - 1 if up else zz + 1))
    def zroles(t, body):
        for up in (True, False):
            zz = t if up else zn - 1 - t
            pl.when(z == zz)(functools.partial(body, up, zz))
    def zstage(i, t):
        def body(up, zz):
            for j in (range(zz + 1, zn) if up else range(zz - 1, -1, -1)):
                if t > 0:
                    zrecv(i, up, zz, j).wait_recv()
                    a = col(acc(i, 0), i, j)
                    add_rows(a, [a, buf(i, r_.rz, r_.vrz, landing(up, zz, j))], size(i)[0])
                zcopy(i, up, zz, j).start()
            if t > 0:
                zrecv(i, up, zz, zz).wait_recv()
        zroles(t, body)
    def result(i):
        if i == VEC:
            return r_.g_vec
        if i < 8:
            return refs[len(B_IN) + i]
        if i < 12:
            return r_.g_fi.at[:, pl.ds((i - 8) * 256, 256)]
        return r_.g_fo.at[pl.ds((i - 12) * SLAB, SLAB), :]
    def final(i):
        for zz in range(zn):
            @pl.when(z == zz)
            def _(zz=zz):
                terms = [col(acc(i, 0), i, zz)]
                if zz > 0:
                    terms.append(buf(i, r_.rz, r_.vrz, landing(True, zz, zz)))
                if zz < zn - 1:
                    terms.append(buf(i, r_.rz, r_.vrz, landing(False, zz, zz)))
                add_rows(result(i), terms, size(i)[0])
                for j in range(zn):
                    if j > zz:
                        zcopy(i, True, zz, j).wait_send()
                    if j < zz:
                        zcopy(i, False, zz, j).wait_send()
        for h in range(2):
            dcopy(i, h).wait_send()
            for d in range(2):
                xcopy(i, d, h).wait_send()
        if place_of[i] + SLOTS_A < 16:
            for s, (who, zz, ok) in enumerate(peers):
                def send(s=s, who=who, zz=zz):
                    pl.semaphore_signal(r_.credit.at[(0, 1, 2, 4, 3)[s]], inc=1, device_id=(who, zz), device_id_type=MESH)
                send() if ok is None else pl.when(ok)(send)
    FINAL = 3 + zn
    done = {}
    def advance(i, upto):
        while done[i] < upto:
            done[i] += 1
            s = done[i]
            rows_ = size(i)[0]
            if s == 1:
                for k in (3, 1, 2, 0):
                    ccopy(i, k).wait_recv()
                    add_rows(acc(i, k), [acc(i, k), gslab(i, fam[k])], rows_)
                    if k == 1:
                        dcopy(i, 0).start(); dcopy(i, 1).start()
                    if k == 2:
                        xcopy(i, 0, 0).start()
                    if k == 0:
                        xcopy(i, 1, 1).start()
                for k in range(4):
                    ccopy(i, k).wait_send()
            elif s == 2:
                for d, h in ((1, 0), (0, 1)):
                    dcopy(i, h).wait_recv()
                    a = half(acc(i, 1 + d), i, h)
                    add_rows(a, [a, buf(i, r_.rh, r_.vrh, h)], rows_ // 2)
                xcopy(i, 1, 0).start(); xcopy(i, 0, 1).start()
            elif s == 3:
                for d in range(2):
                    for h in range(2):
                        xcopy(i, d, h).wait_recv()
                add_rows(acc(i, 0), [acc(i, 0), buf(i, r_.rxy, r_.vrxy, 0), buf(i, r_.rxy, r_.vrxy, 1)], rows_)
                zstage(i, 0)
            elif s < FINAL:
                zstage(i, s - 3)
            else:
                final(i)
    waiting, line, spent, pace = [], [], [0.0], [PACE_B]
    def tick():
        line.append(waiting.pop(0) if waiting else None)
        for s, lag in enumerate(LAGS_B):
            i = line[-1 - lag] if lag < len(line) else None
            if i is not None:
                advance(i, s + 1)
    def work(cost):
        spent[0] += cost
        while spent[0] >= pace[0]:
            spent[0] -= pace[0]
            tick()
    def reach(i, stage):
        while done[i] < stage:
            tick()
    def grab(i):
        a = place_of[i]
        if i != VEC and a >= SLOTS_G:
            reach(order[a - SLOTS_G], 1)
        return g(i)
    def submit(i):
        a = place_of[i]
        done[i] = 0
        if i != VEC and a >= SLOTS_A:
            reach(order[a - SLOTS_A], FINAL)
            for s, (_, _, ok) in enumerate(peers):
                def take(s=s):
                    pl.semaphore_wait(r_.credit.at[s], 1)
                take() if ok is None else pl.when(ok)(take)
        for k in (3, 1, 2, 0):
            ccopy(i, k).start()
        waiting.append(i)

    loads = [0]
    def fetch(src, dst):
        c = pltpu.make_async_copy(src, dst, r_.ld.at[loads[0]])
        loads[0] += 1
        c.start()
        return c
    wslot = [0]
    def weight(i):
        s = wslot[0] % 2
        wslot[0] += 1
        c = pltpu.make_async_copy(r_.weights.at[i], r_.w.at[s], r_.ws.at[i])
        c.start()
        return s, c
    p = r_.p
    def rows_of(at, count):
        return p.at[pl.ds(at, count), :]
    def outer(lhs, rhs, dst, tile=512):
        def body(m, c):
            dst[c, :] = dot(lhs(c), rhs(), 0, 0).astype(BF)
        tiles(W, tile, body)
    def back(grad, slot, emit):
        def body(m, c):
            emit(c, dot(grad(), r_.w[slot, c, :], 1, 1))
        tiles(W, 512, body)
    def gain(k):
        return r_.gains[k:k + 1, :]
    def add_sum(k, v):
        r_.sums[pl.ds(k * 8, 8), :] += fold(v)
    def norm_back(k, value, grad, resid, out, low, count=T, step=frames, sums=True):
        def body(s):
            xhat, scale = standard(value(s))
            gr = grad(s)
            if sums:
                add_sum(k, gr * xhat)
                add_sum(k + 1, gr)
            e = gr * gain(k)
            inner = jnp.mean(e * xhat, axis=-1, keepdims=True)
            v = resid(s) + scale * (e - jnp.mean(e, axis=-1, keepdims=True) - xhat * inner)
            out[s, :] = v
            if low is not None:
                low[s, :] = v.astype(BF)
        blocks(count, step, body)

    K, V, FI, Q, DO = 0, rows * E, 2 * rows * E, 3 * rows * E, 3 * rows * E + T
    r_.sums[...] = jnp.zeros_like(r_.sums)
    fo_loads = [fetch(r_.fo_grad.at[i], grab(12 + i)) for i in range(SLOTS_G)]
    third_c = fetch(r_.third, rows_of(FI, T))
    pg = [fetch(r_.pre_grad.at[i], rows_of(K + i * T, T)) for i in range(3)]
    cot_c = fetch(r_.cot, rows_of(V, T))
    ac_c = fetch(r_.after_cross, r_.fc)
    for i in range(SLOTS_G):
        fo_loads[i].wait()
        submit(12 + i)
        work(0.5)
    third_c.wait()
    nxt = weight(8)
    pg.append(fetch(r_.pre_grad.at[3], rows_of(V + T, T)))
    at_pg = [K, K + T, K + 2 * T, V + T]
    for i in range(4):
        slot, wc = nxt
        pg[i].wait(); wc.wait()
        if i < 3:
            nxt = weight(9 + i)
        def emit(c, v, i=i):
            r_.fa[:, c] = v if i == 0 else r_.fa[:, c] + v
        back(lambda i=i: p[pl.ds(at_pg[i], T), :], slot, emit)
        work(2.4)
        if i == 0:
            for q in range(SLOTS_G, 4):
                c = fetch(r_.fo_grad.at[q], grab(12 + q)); c.wait()
                submit(12 + q)
                work(0.5)
        outer(lambda c: p[pl.ds(FI, T), c], lambda i=i: p[pl.ds(at_pg[i], T), :], grab(8 + i))
        submit(8 + i)
        work(2.8)
    cmix_c = fetch(r_.cmix, rows_of(V + T, T))
    co_slot, co_c = weight(7)
    cq_c = fetch(r_.cq, rows_of(FI, T))
    second_c = fetch(r_.second, rows_of(FI + T, T))
    mixed_c = fetch(r_.mixed, rows_of(FI + 2 * T, T))
    k_c = fetch(r_.k, rows_of(K, rows * E))
    t_c = [fetch(r_.tk, r_.t.at[0]), fetch(r_.tv, r_.t.at[1])]
    cot_c.wait(); ac_c.wait()
    norm_back(4, lambda s: r_.fc[s, :], lambda s: r_.fa[s, :], lambda s: p[pl.ds(pl.multiple_of(V + s.start, 16), s.size), :].astype(F32), r_.fa, rows_of(DO, T))
    as_c = fetch(r_.after_self, r_.fc)
    work(4)
    cmix_c.wait(); co_c.wait()
    outer(lambda c: p[pl.ds(V + T, T), c], lambda: p[pl.ds(DO, T), :], grab(7))
    submit(7)
    work(2)
    def emit(c, v):
        p[pl.ds(V + 2 * T, T), c] = v.astype(BF)
    back(lambda: p[pl.ds(DO, T), :], co_slot, emit)
    work(2)
    cqw_slot, cqw_c = weight(4)
    ckw_slot, ckw_c = weight(5)
    cq_c.wait(); t_c[0].wait(); t_c[1].wait()
    tokens = r_.text.shape[0] // rows
    for r in range(rows):
        def pair(h, r=r):
            c = pl.ds(pl.multiple_of(h * 128, 128), 128)
            rk = pl.ds(r * tokens, tokens)
            qrows = pl.ds(FI + r * frames, frames)
            q2, d2 = p[qrows, c], p[pl.ds(V + 2 * T + r * frames, frames), c]
            kk, vv = pair_keys(r_.t[0, rk, c]), pair_keys(r_.t[1, rk, c])
            sh = cross_shares(q2, kk, ids, r_.t_ids[r], tokens)
            dsh = dot(d2, vv, 1, 1)
            ds = (sh * (dsh - halves(sh * dsh, tokens, jnp.sum, 0.0))).astype(BF)
            p[qrows, c] = (dot(ds, kk, 1, 0) * SCALE).astype(BF)
            gk = dot(ds, q2, 0, 0) * SCALE
            gv = dot(sh.astype(BF), d2, 0, 0)
            first = lane_is((tokens, 128), 0)
            r_.t[0, rk, c] = jnp.where(first, gk[:tokens], gk[tokens:]).astype(BF)
            r_.t[1, rk, c] = jnp.where(first, gv[:tokens], gv[tokens:]).astype(BF)
        ids = column(r_.q_ids[r][:, :frames])
        pl.loop(0, heads2)(pair)
        work(4.8)
    v_c = fetch(r_.v, rows_of(V, rows * E))
    second_c.wait()
    outer(lambda c: p[pl.ds(FI + T, T), c], lambda: p[pl.ds(FI, T), :], grab(4))
    submit(4)
    work(2)
    cqw_c.wait()
    def emit(c, v):
        r_.fb[:, c] = v
    back(lambda: p[pl.ds(FI, T), :], cqw_slot, emit)
    work(2)
    cvw_slot, cvw_c = weight(6)
    as_c.wait()
    norm_back(2, lambda s: r_.fc[s, :], lambda s: r_.fb[s, :], lambda s: r_.fa[s, :], r_.fa, rows_of(Q, T))
    lse_c = fetch(r_.lse, r_.lse_s)
    work(4)
    outer(lambda c: r_.text[:, c], lambda: r_.t[0], grab(5))
    submit(5)
    work(1)
    ckw_c.wait()
    def body(m, c):
        v = dot(r_.t[0], r_.w[ckw_slot, c, :], 1, 1)
        r_.fb[pl.ds(0, rows * tokens), c] = v
    tiles(W, 256, body)
    ow_slot, ow_c = weight(3)
    outer(lambda c: r_.text[:, c], lambda: r_.t[1], grab(6))
    submit(6)
    work(1)
    cvw_c.wait()
    part = tokens // zn
    def body(m, c):
        v = r_.fb[pl.ds(0, rows * tokens), c] + dot(r_.t[1], r_.w[cvw_slot, c, :], 1, 1)
        for r in range(rows):
            for j in range(zn):
                r_.tsrc[j, r * part:(r + 1) * part, c] = v[r * tokens + j * part:r * tokens + (j + 1) * part].astype(BF)
    tiles(W, 256, body)
    kw_slot, kw_c = weight(1)
    def tcopy(up, zz, j):
        to = zz + 1 if up else zz - 1
        return remote(r_.tsrc.at[j], r_.trz.at[landing(up, to, j)], r_.ts.at[0 if up else 1, j], r_.tr.at[0 if up else 1, j], (dp, to))
    def trecv(up, zz, j):
        b = r_.trz.at[landing(up, zz, j)]
        return remote(b, b, r_.ts.at[0 if up else 1, j], r_.tr.at[0 if up else 1, j], (dp, zz - 1 if up else zz + 1))
    def tstage(t):
        def body(up, zz):
            for j in (range(zz + 1, zn) if up else range(zz - 1, -1, -1)):
                if t > 0:
                    trecv(up, zz, j).wait_recv()
                    add_rows(r_.tsrc.at[j], [r_.tsrc.at[j], r_.trz.at[landing(up, zz, j)]], rows * part, rows * part)
                tcopy(up, zz, j).start()
            if t > 0:
                trecv(up, zz, zz).wait_recv()
        zroles(t, body)
    def tfinal():
        for zz in range(zn):
            @pl.when(z == zz)
            def _(zz=zz):
                terms = [r_.tsrc.at[zz]]
                if zz > 0:
                    terms.append(r_.trz.at[landing(True, zz, zz)])
                if zz < zn - 1:
                    terms.append(r_.trz.at[landing(False, zz, zz)])
                add_rows(r_.g_text, terms, rows * part, rows * part)
                for j in range(zn):
                    if j > zz:
                        tcopy(True, zz, j).wait_send()
                    if j < zz:
                        tcopy(False, zz, j).wait_send()
    tstage(0)
    mixed_c.wait()
    outer(lambda c: p[pl.ds(FI + 2 * T, T), c], lambda: p[pl.ds(Q, T), :], grab(3))
    submit(3)
    work(2)
    ow_c.wait()
    def emit(c, v):
        p[pl.ds(DO, T), c] = v.astype(BF)
    back(lambda: p[pl.ds(Q, T), :], ow_slot, emit)
    work(2)
    vw_slot, vw_c = weight(2)
    q_c = fetch(r_.q, rows_of(Q, T))
    first_c = fetch(r_.first, rows_of(FI, rows * E))
    tstage(1)
    lse_c.wait(); k_c.wait(); v_c.wait(); q_c.wait()
    kw_c.wait(); vw_c.wait()

    def h2copy(r):
        return remote(r_.h2s.at[r], r_.h2l.at[r], r_.hs.at[0, r], r_.hr.at[0, r], (dp, z - 1))
    def h1copy(r):
        return remote(r_.h1.at[r], r_.hb.at[r], r_.hs.at[1, r], r_.hr.at[1, r], (dp, z - 1))
    def pass_on(r):
        @pl.when(dn_ok)
        def _():
            @pl.when(up_ok)
            def _():
                h2copy(r).wait_recv()
                add_rows(r_.h1.at[r], [r_.h1.at[r], r_.h2l.at[r]], frames, frames)
            h1copy(r).start()
    for r in range(rows):
        r_.bias[...] = mask_keys(r_.q_ids[r], r_.k_ids[r], E - frames)
        def pair(h, r=r):
            c = pl.ds(pl.multiple_of(h * 128, 128), 128)
            rq, rk, rv = pl.ds(Q + r * frames, frames), pl.ds(K + r * E, E), pl.ds(V + r * E, E)
            k2, v2 = p[rk, c], p[rv, c]
            qs, dd = stack_heads(p[rq, c] * jnp.asarray(SCALE, BF)), stack_heads(p[pl.ds(DO + r * frames, frames), c])
            sh = jnp.exp(dot(k2, qs, 1, 1) + r_.bias[...] - r_.lse_s[r, pl.ds(h, 1), :])
            dsh = dot(v2, dd, 1, 1)
            ds = (sh * (dsh - jnp.sum(sh * dsh, axis=0, keepdims=True))).astype(BF)
            p[rk, c] = dot(ds, qs, 1, 0).astype(BF)
            p[rv, c] = dot(sh.astype(BF), dd, 1, 0).astype(BF)
            p[rq, c] = (pick_heads(dot(ds, k2, 0, 0)) * SCALE).astype(BF)
        for part_ in range(4):
            pl.loop(part_ * heads2 // 4, (part_ + 1) * heads2 // 4)(pair)
            work(3.4)
        if r == 0:
            tstage(2)
        if r == 1:
            tstage(3)
            tfinal()
    pace[0] = PACE_TAIL
    hid_c = fetch(r_.hidden, rows_of(DO, T))
    first_c.wait()
    for i, at in ((1, K), (2, V)):
        outer(lambda c: p[pl.ds(FI, rows * E), c], lambda at=at: p[pl.ds(at, rows * E), :], grab(i), 256)
        submit(i)
        work(7)
    gq_ = grab(0)
    def body(m, c):
        total = None
        for r in range(rows):
            v = dot(p[pl.ds(FI + r * E + 2 * frames, frames), c], p[pl.ds(Q + r * frames, frames), :], 0, 0)
            total = v if total is None else total + v
        gq_[c, :] = total.astype(BF)
    tiles(W, 512, body)
    submit(0)
    work(2.5)
    for r in range(rows):
        hal_c = fetch(r_.halo.at[r], r_.hal)
        def body(m, c, r=r):
            v = dot(p[pl.ds(K + r * E, E), :], r_.w[kw_slot, c, :], 1, 1) + dot(p[pl.ds(V + r * E, E), :], r_.w[vw_slot, c, :], 1, 1)
            r_.h2s[r, :, c] = v[:frames].astype(BF)
            r_.h1[r, :, c] = v[frames:2 * frames].astype(BF)
            r_.fb[pl.ds(r * frames, frames), c] = v[2 * frames:]
        tiles(W, 512, body)
        hal_c.wait()
        for q in range(2):
            gr = (r_.h2s, r_.h1)[q][r].astype(F32)
            add_sum(0, gr * standard(r_.hal[q].astype(F32))[0])
            add_sum(1, gr)
        @pl.when(z >= 2)
        def _():
            h2copy(r).start()
        work(5)
        if r > 0:
            pass_on(r - 1)
    qw_slot, qw_c = weight(0)
    qw_c.wait(); hid_c.wait()
    def emit(c, v):
        r_.fb[:, c] = r_.fb[:, c] + v
    back(lambda: p[pl.ds(Q, T), :], qw_slot, emit)
    work(2.2)
    pass_on(rows - 1)
    def body(s):
        gr = r_.fb[s, :]
        add_sum(0, gr * standard(p[pl.ds(pl.multiple_of(DO + s.start, 16), s.size), :].astype(F32))[0])
        add_sum(1, gr)
    blocks(T, frames, body)
    sums = jnp.sum(r_.sums[...].reshape(6, 8, W), axis=1)
    sums = jnp.concatenate([sums, jnp.zeros((10, W), F32)], axis=0)
    share = W // (8 * zn)
    keep = lax.broadcasted_iota(jnp.int32, (16, 128), 1) < share
    for d in range(8):
        v = sums[:, d * 128:(d + 1) * 128]
        for j in range(zn):
            moved = pltpu.roll(v, (128 - j * share) % 128, 1)
            r_.vg[d * 16:(d + 1) * 16, j * 128:(j + 1) * 128] = jnp.where(keep, moved, 0.0).astype(BF)
    submit(VEC)
    work(3)
    for r in range(rows):
        @pl.when(up_ok)
        def _():
            h1copy(r).wait_recv()
            add_rows(r_.fb.at[pl.ds(r * frames, frames), :], [r_.fb.at[pl.ds(r * frames, frames), :], r_.hb.at[r]], frames, frames)
    norm_back(0, lambda s: p[pl.ds(pl.multiple_of(DO + s.start, 16), s.size), :].astype(F32), lambda s: r_.fb[s, :], lambda s: r_.fa[s, :], r_.fa, None, sums=False)
    oc = pltpu.make_async_copy(r_.fa, r_.g_hidden, r_.outsem.at[0])
    oc.start()
    for i in order:
        reach(i, FINAL)
    oc.wait()
    for r in range(rows):
        @pl.when(z >= 2)
        def _():
            h2copy(r).wait_send()
        @pl.when(dn_ok)
        def _():
            h1copy(r).wait_send()

def backward(f, hidden, text, cot, q_ids, k_ids, t_ids, zn, rows, frames, cid=3):
    T, E = rows * frames, 3 * frames
    S = jax.ShapeDtypeStruct
    D, V = pltpu.SemaphoreType.DMA, pltpu.VMEM
    VM = pl.BlockSpec(memory_space=pltpu.VMEM)
    tok = text.shape[0]
    part = tok // zn
    vals = dict(f, hidden=hidden, text=text, cot=cot, q_ids=q_ids, k_ids=k_ids, t_ids=t_ids)
    outs = [S((128, 256), F32)] * 8 + [S((128, 1024), F32), S((512, 256), F32), S((16, 128), F32), S((part, W), F32), S((T, W), F32)]
    A = SLOTS_A
    scratch = [V((3 * rows * E + 2 * T, W), BF), V((T, W), F32), V((T, W), F32), V((T, W), F32), V((2, W, W), BF), V((SLOTS_G, W, W), BF),
               V((A, 4, 128, W), BF), V((A, 2, 64, W), BF), V((A, 2, 128, W), BF), V((A, zn + 1, 128, 256), BF),
               V((128, 512), BF), V((4, 16, 512), BF), V((2, 8, 512), BF), V((2, 16, 512), BF), V((zn + 1, 16, 128), BF),
               V((2, tok, W), BF), V((zn, part, W), BF), V((zn + 1, part, W), BF),
               V((rows, frames, W), BF), V((rows, frames, W), BF), V((rows, frames, W), BF), V((rows, frames, W), BF), V((2, frames, W), BF), V((E, 2 * frames), F32), V((rows, W // 128, 2 * frames), F32), V((48, W), F32)]
    n = 17
    scratch += [D((n, 4)), D((n, 4)), D((n, 2)), D((n, 2)), D((n, 2, 2)), D((n, 2, 2)), D((n, 2, zn)), D((n, 2, zn)), D((2, zn)), D((2, zn)), D((2, rows)), D((2, rows)),
                pltpu.SemaphoreType.REGULAR((5,)), D((40,)), D((16,)), D((1,))]
    return pl.pallas_call(
        functools.partial(backward_kernel, zn, rows, frames),
        out_shape=outs,
        in_specs=[VM] * B_IN_VMEM + [ANY] * (len(B_IN) - B_IN_VMEM), out_specs=[VM] * (len(B_OUT) - 1) + [ANY],
        scratch_shapes=scratch,
        compiler_params=pltpu.CompilerParams(collective_id=cid, has_side_effects=True, vmem_limit_bytes=63 << 20),
        name="backward",
    )(*[vals[k] for k in B_IN])

EPSILON = 1e-05

def project(left_side, right_side, kind=F32):
    return jnp.einsum("rfk,kn->rfn", left_side, right_side, preferred_element_type=F32).astype(kind)

def project_back(gradient, right_side, kind=F32):
    return jnp.einsum("rfn,kn->rfk", gradient, right_side, preferred_element_type=F32).astype(kind)

def weight_grad(left_side, gradient):
    return jnp.einsum("rfk,rfn->kn", left_side, gradient, preferred_element_type=F32).astype(BF)

def normalized(values):
    values = values.astype(F32)
    centred = values - jnp.mean(values, axis=-1, keepdims=True)
    scale = lax.rsqrt(jnp.mean(centred * centred, axis=-1, keepdims=True) + EPSILON)
    return centred * scale, scale

def norm_back(values, gain, grad):
    xhat, scale = normalized(values)
    e = gain * grad
    inner = jnp.mean(e * xhat, axis=-1, keepdims=True)
    inputs = scale * (e - jnp.mean(e, axis=-1, keepdims=True) - xhat * inner)
    return jnp.sum(grad * xhat, axis=(0, 1)), jnp.sum(grad, axis=(0, 1)), inputs

def gelu_parts(u):
    half_erf = 0.5 * (1.0 + lax.erf(u * 0.7071067811865476))
    return u * half_erf, half_erf + u * (0.3989422804014327 * jnp.exp(-0.5 * u * u))

def gather_all(weights, vectors, hidden, dpn, zn):
    rows, frames, width = hidden.shape
    share = vectors.shape[1]
    if (dpn, zn) == (8, 4):
        packed = jnp.pad(vectors, ((0, 16 - vectors.shape[0]), (0, 128 - share)))
        *whole, packed, ext = gather(list(weights) + [packed], hidden, dpn, zn)
        packed = packed.reshape(dpn, 16, zn, 128)[:, :vectors.shape[0], :, :share]
        return whole, packed.transpose(1, 0, 2, 3).reshape(vectors.shape[0], width), ext
    whole = [lax.all_gather(lax.all_gather(w, "ctx", axis=1, tiled=True), "dp", axis=0, tiled=True) for w in weights]
    near = lax.ppermute(hidden, "ctx", [(i, i + 1) for i in range(zn - 1)])
    far = lax.ppermute(hidden, "ctx", [(i, i + 2) for i in range(zn - 2)])
    return whole, lax.all_gather(vectors, ("dp", "ctx"), axis=1, tiled=True), jnp.stack([far, near, hidden], axis=1)

def scatter_all(grads, vectors, text, halo, dpn, zn):
    count, width = vectors.shape
    rows, tokens = text.shape[:2]
    if (dpn, zn) == (8, 4):
        share = width // (dpn * zn)
        packed = jnp.pad(vectors.reshape(count, dpn, zn, share).transpose(1, 0, 2, 3), ((0, 0), (0, 16 - count), (0, 0), (0, 128 - share)))
        packed = packed.reshape(dpn * 16, zn * 128).astype(BF)
        folded = text.reshape(rows, zn, tokens // zn, width).transpose(0, 2, 1, 3).reshape(rows * tokens // zn, zn * width)
        *own, packed, folded, back = scatter(list(grads) + [packed], folded, halo, dpn, zn)
        return own, packed[:count, :share], folded.reshape(rows, tokens // zn, width), back
    own = [lax.psum_scatter(lax.psum_scatter(g, "dp", scatter_dimension=0, tiled=True), "ctx", scatter_dimension=1, tiled=True).astype(F32) for g in grads]
    back = lax.ppermute(halo[:, 1], "ctx", [(i + 1, i) for i in range(zn - 1)]).astype(F32)
    back = back + lax.ppermute(halo[:, 0], "ctx", [(i + 2, i) for i in range(zn - 2)]).astype(F32)
    return (own, lax.psum_scatter(vectors, ("dp", "ctx"), scatter_dimension=1, tiled=True),
            lax.psum_scatter(text.astype(F32), "ctx", scatter_dimension=1, tiled=True), back)

def general(hidden, text_states, frame_segments, text_segments, text_lengths, cotangent, *params):
    dpn, zn = lax.axis_size("dp"), lax.axis_size("ctx")
    place = lax.axis_index("ctx")
    rows, frames, width = hidden.shape
    weights, vectors = params[:10], jnp.stack(params[10:])
    reach = 2 * frames
    ids = jnp.pad(frame_segments, ((0, 0), (reach, 0)), constant_values=-1)
    key_ids = lax.dynamic_slice_in_dim(ids, place * frames, reach + frames, 1)
    own_ids = key_ids[:, reach:]
    text_ids = jnp.where(jnp.arange(text_segments.shape[1])[None] < text_lengths[:, None], text_segments, -1)

    whole, vec, ext = gather_all(weights, vectors, hidden, dpn, zn)
    wq, wk, wv, wo, cq, ck, cv, co, fi, fo = whole
    g1, s1, g2, s2, g3, s3 = vec.astype(F32)

    first_ext = (normalized(ext)[0] * g1 + s1).astype(BF)
    first_own = first_ext[:, 2]
    first_ext = first_ext.reshape(rows, 3 * frames, width)
    queries = project(first_own, wq, BF)
    keys = project(first_ext, wk, BF)
    values = project(first_ext, wv, BF)
    self_mixed, self_total = self_forward(queries, keys, values, own_ids, key_ids)
    states = hidden.astype(F32)
    after_self = states + project(self_mixed, wo)
    second_norm = (normalized(after_self)[0] * g2 + s2).astype(BF)
    cross_queries = project(second_norm, cq, BF)
    text_keys = project(text_states, ck, BF)
    text_values = project(text_states, cv, BF)
    cross_mixed = cross_forward(cross_queries, text_keys, text_values, own_ids, text_ids)
    after_cross = after_self + project(cross_mixed, co)
    third_norm = (normalized(after_cross)[0] * g3 + s3).astype(BF)
    pre_act = project(third_norm, fi)
    activated, slope = gelu_parts(pre_act)
    activated = activated.astype(BF)
    block_output = (after_cross + project(activated, fo)).astype(BF)

    fo_grad = weight_grad(activated, cotangent)
    pre_grad = (project_back(cotangent, fo) * slope).astype(BF)
    fi_grad = weight_grad(third_norm, pre_grad)
    g3_grad, s3_grad, part = norm_back(after_cross, g3, project_back(pre_grad, fi))
    cross_grad = cotangent.astype(F32) + part
    cross_low = cross_grad.astype(BF)
    co_grad = weight_grad(cross_mixed, cross_low)
    cross_mixed_grad = project_back(cross_low, co, BF)
    cq_low, tk_low, tv_low = cross_backward(cross_queries, text_keys, text_values, cross_mixed_grad, own_ids, text_ids)
    ck_grad = weight_grad(text_states, tk_low)
    cv_grad = weight_grad(text_states, tv_low)
    text_part = (project_back(tk_low, ck) + project_back(tv_low, cv)).astype(BF)
    cq_grad = weight_grad(second_norm, cq_low)
    g2_grad, s2_grad, part = norm_back(after_self, g2, project_back(cq_low, cq))
    self_grad = cross_grad + part
    self_low = self_grad.astype(BF)
    wo_grad = weight_grad(self_mixed, self_low)
    self_mixed_grad = project_back(self_low, wo, BF)
    q_low, k_low, v_low = self_backward(queries, keys, values, self_total, self_mixed_grad, own_ids, key_ids)
    wq_grad = weight_grad(first_own, q_low)
    wk_grad = weight_grad(first_ext, k_low)
    wv_grad = weight_grad(first_ext, v_low)
    first_grad = (project_back(k_low, wk) + project_back(v_low, wv)).reshape(rows, 3, frames, width)
    own_grad = first_grad[:, 2] + project_back(q_low, wq)
    halo_grad = first_grad[:, :2].astype(BF)
    xhat_ext = normalized(ext)[0]
    g1_grad = jnp.sum(first_grad[:, :2] * xhat_ext[:, :2], axis=(0, 1, 2)) + jnp.sum(own_grad * xhat_ext[:, 2], axis=(0, 1))
    s1_grad = jnp.sum(first_grad[:, :2], axis=(0, 1, 2)) + jnp.sum(own_grad, axis=(0, 1))

    grads = (wq_grad, wk_grad, wv_grad, wo_grad, cq_grad, ck_grad, cv_grad, co_grad, fi_grad, fo_grad)
    vec_grads = jnp.stack([g1_grad, s1_grad, g2_grad, s2_grad, g3_grad, s3_grad])
    own, vec_own, text_grad, back = scatter_all(grads, vec_grads, text_part, halo_grad, dpn, zn)
    part = norm_back(states, g1, own_grad + back.astype(F32))[2]
    return (block_output, self_grad + part, text_grad, *own, *vec_own)

def fused(hidden, text_states, frame_segments, text_segments, text_lengths, cotangent, *params):
    dpn, zn = lax.axis_size("dp"), lax.axis_size("ctx")
    place = lax.axis_index("ctx")
    rows, frames, width = hidden.shape
    weights, vectors = params[:10], jnp.stack(params[10:])
    reach = 2 * frames
    ids = jnp.pad(frame_segments, ((0, 0), (reach, 0)), constant_values=-1)
    key_ids = lax.dynamic_slice_in_dim(ids, place * frames, reach + frames, 1)
    own_ids = key_ids[:, reach:]
    text_ids = jnp.where(jnp.arange(text_segments.shape[1])[None] < text_lengths[:, None], text_segments, -1)

    packed = jnp.pad(vectors, ((0, 16 - vectors.shape[0]), (0, 128 - vectors.shape[1])))
    flat = lambda v: v.reshape(-1, v.shape[-1])
    f = forward(weights, packed, flat(hidden), flat(text_states), flat(cotangent), jnp.concatenate([own_ids, own_ids], axis=1)[:, None, :], key_ids[:, None, :],
                jnp.concatenate([text_ids, text_ids], axis=1)[:, None, :], zn, rows, frames)
    grads = backward(f, flat(hidden), flat(text_states), flat(cotangent), jnp.concatenate([own_ids, own_ids], axis=1)[:, None, :], key_ids[:, None, :],
                     jnp.concatenate([text_ids, text_ids], axis=1)[:, None, :], zn, rows, frames)
    *own, vec_own, text_grad, hidden_grad = grads
    return (f["block"].reshape(hidden.shape), hidden_grad.reshape(hidden.shape), text_grad.reshape(rows, -1, width), *own, *vec_own[:6, :vectors.shape[1]])

def per_device(hidden, text_states, frame_segments, text_segments, text_lengths, cotangent, *params):
    dpn, zn = lax.axis_size("dp"), lax.axis_size("ctx")
    if (dpn, zn) == (8, 4) and params[0].shape == (128, 256):
        return fused(hidden, text_states, frame_segments, text_segments, text_lengths, cotangent, *params)
    return general(hidden, text_states, frame_segments, text_segments, text_lengths, cotangent, *params)

def solution(mesh):
    rows, both = P("dp", "ctx", None), P("dp", "ctx")
    flat = P(("dp", "ctx"))
    placed = (rows, P("dp", None, None), P("dp", None), P("dp", None), P("dp"), rows) + (both,) * 10 + (flat,) * 6
    return jax.shard_map(per_device, mesh=mesh, in_specs=placed, out_specs=(rows,) * 3 + (both,) * 10 + (flat,) * 6, check_vma=False)
```
